32 devices in a mesh: dp: 16 (over z, y, core), fsdp: 2 (over x).
Axes of the slice: x: 2, y: 2, z: 4, core: 2. Of those that a mesh axis runs over, the one named last changes fastest.
Arguments:
- text_tokens: bfloat16 [18432, 768], P(('dp', 'fsdp')), may hold values from -6 to 6
- image_tokens: bfloat16 [57600, 768], P(('dp', 'fsdp')), may hold values from -6 to 6
- pair_counts: int32 [32], replicated, may hold values from 9 to 36, as said below
- log_scale: float32 [1], replicated, may hold values from 3.7 to 4.1
- text_gain: bfloat16 [768], P('fsdp'), may hold values from 0.25 to 1.75
- text_offset: bfloat16 [768], P('fsdp'), may hold values from -1.1953125 to 1.1953125
- text_joint: bfloat16 [768, 2304], P('fsdp'), may hold values from -0.21875 to 0.21875
- text_mixer: bfloat16 [768, 768], P('fsdp'), may hold values from -0.4375 to 0.4375
- text_mixbias: bfloat16 [768], P('fsdp'), may hold values from -1.1953125 to 1.1953125
- text_feedgain: bfloat16 [768], P('fsdp'), may hold values from 0.25 to 1.75
- text_feedoffset: bfloat16 [768], P('fsdp'), may hold values from -1.1953125 to 1.1953125
- text_upward: bfloat16 [768, 3072], P('fsdp'), may hold values from -0.21875 to 0.21875
- text_upbias: bfloat16 [3072], P('fsdp'), may hold values from -1.1953125 to 1.1953125
- text_downward: bfloat16 [3072, 768], P('fsdp'), may hold values from -0.109375 to 0.109375
- text_downbias: bfloat16 [768], P('fsdp'), may hold values from -1.1953125 to 1.1953125
- text_endgain: bfloat16 [768], P('fsdp'), may hold values from 0.25 to 1.75
- text_endoffset: bfloat16 [768], P('fsdp'), may hold values from -1.1953125 to 1.1953125
- text_project: bfloat16 [768, 768], P('fsdp'), may hold values from -0.21875 to 0.21875
- image_gain: bfloat16 [768], replicated, may hold values from 0.25 to 1.75
- image_offset: bfloat16 [768], replicated, may hold values from -1.1953125 to 1.1953125
- image_joint: bfloat16 [768, 2304], replicated, may hold values from -0.21875 to 0.21875
- image_mixer: bfloat16 [768, 768], replicated, may hold values from -0.5 to 0.5
- image_mixbias: bfloat16 [768], replicated, may hold values from -1.1953125 to 1.1953125
- image_feedgain: bfloat16 [768], replicated, may hold values from 0.25 to 1.75
- image_feedoffset: bfloat16 [768], replicated, may hold values from -1.1953125 to 1.1953125
- image_upward: bfloat16 [768, 3072], replicated, may hold values from -0.21875 to 0.21875
- image_upbias: bfloat16 [3072], replicated, may hold values from -1.1953125 to 1.1953125
- image_downward: bfloat16 [3072, 768], replicated, may hold values from -0.109375 to 0.109375
- image_downbias: bfloat16 [768], replicated, may hold values from -1.1953125 to 1.1953125
- image_endgain: bfloat16 [768], replicated, may hold values from 0.25 to 1.75
- image_endoffset: bfloat16 [768], replicated, may hold values from -1.1953125 to 1.1953125
- image_project: bfloat16 [768, 768], replicated, may hold values from -0.21875 to 0.21875
Outputs:
- grad_gain: float32 [768], P('fsdp')
- grad_offset: float32 [768], P('fsdp')
- grad_joint: float32 [768, 2304], P('fsdp')
- grad_mixer: float32 [768, 768], P('fsdp')
- grad_mixbias: float32 [768], P('fsdp')
- grad_feedgain: float32 [768], P('fsdp')
- grad_feedoffset: float32 [768], P('fsdp')
- grad_upward: float32 [768, 3072], P('fsdp')
- grad_upbias: float32 [3072], P('fsdp')
- grad_downward: float32 [3072, 768], P('fsdp')
- grad_downbias: float32 [768], P('fsdp')
- grad_endgain: float32 [768], P('fsdp')
- grad_endoffset: float32 [768], P('fsdp')
- grad_project: float32 [768, 768], P('fsdp')
- grad_scale: float32 [1], replicated
- grad_tokens: float32 [18432, 768], P(('dp', 'fsdp'))
- loss_value: float32 [1], replicated
The draws below stay inside these ranges and needn't reach their ends.
Inputs may be any that keep to these rules, and one draw needn't show every extreme that they name: `pair_counts`: each count is 36 divided by 1, 2, 3 or 4, rounded down; some device holds 36 live pairs; live pairs take a device's first slots.
All inputs are finite; a program needn't handle non-finite values.
Results may differ from the reference program's by a relative error of at most 0.018.
Values may be sent and summed in bfloat16 or wider, within the bound.
A program may use at most 136 MiB of HBM per device.

```python
from functools import partial
import jax
import jax.numpy as jnp
from jax import lax

D = 768
HEADS = 12
HEAD_DIM = 64
FF = 3072
EMBED = 768
TEXT_LEN = 16
IMAGE_LEN = 50
SLOTS = 36
GROUPS = 32
PAIRS = 1152


def draw_pair_counts(key, part):
    first_key = jax.random.fold_in(key, 11)
    second_key = jax.random.fold_in(key, 23)
    divisor = jax.random.randint(first_key, (GROUPS,), 1, 5)
    counts = SLOTS // divisor
    chosen = jax.random.randint(second_key, (), 0, GROUPS)
    counts = jnp.where(jnp.arange(GROUPS) == chosen, SLOTS, counts)
    return counts.astype(jnp.int32)


def steps_of(stream_key, dims, split, smallest, largest):
    def one(dim, parts):
        heights = jax.random.uniform(jax.random.fold_in(jax.random.fold_in(stream_key, 6), dim), (parts,), jnp.float32, smallest / len(split), largest / len(split))
        return jnp.repeat(jnp.exp(heights), dims[dim] // parts).reshape((-1,) + (1,) * (len(dims) - dim - 1))

    factor_of = one(*split[0])
    for cut in split[1:]:
        factor_of = factor_of * one(*cut)
    return factor_of


def noise(rng, dims, spread, bound, cuts=(), held_as=jnp.bfloat16):
    loudness = steps_of(rng, dims, cuts, -0.22, 0.18) if cuts else 1.0
    result = jax.random.normal(rng, dims, jnp.float32) * spread * loudness
    return jnp.minimum(jnp.maximum(result, -bound), bound).astype(held_as)


def setup_inputs(seed: int = 0) -> dict:
    streams_of = jax.random.split(jax.random.key(seed), 33)
    return {
        "text_tokens": noise(streams_of[0], (PAIRS * TEXT_LEN, D), 1.0, 6.0, ((0, 32),)),
        "image_tokens": noise(streams_of[1], (PAIRS * IMAGE_LEN, D), 1.0, 6.0, ((0, 32),)),
        "pair_counts": draw_pair_counts(jax.random.fold_in(streams_of[32], 71), 0),
        "log_scale": jnp.clip(jax.random.uniform(streams_of[3], (1,), jnp.float32, 3.7, 4.1), 3.7, 4.1),
        "text_gain": jnp.clip(1.0 + 0.15 * jax.random.normal(streams_of[4], (D,), jnp.float32), 0.25, 1.75).astype(jnp.bfloat16),
        "text_offset": noise(streams_of[5], (D,), 0.2, 1.1953125, ((0, 2),)),
        "text_joint": noise(streams_of[6], (D, 3 * D), D ** -0.5, 0.21875, ((0, 2),)),
        "text_mixer": noise(streams_of[7], (D, D), (D // 4) ** -0.5, 0.4375, ((0, 2),)),
        "text_mixbias": noise(streams_of[8], (D,), 0.2, 1.1953125, ((0, 2),)),
        "text_feedgain": jnp.clip(1.0 + 0.15 * jax.random.normal(streams_of[9], (D,), jnp.float32), 0.25, 1.75).astype(jnp.bfloat16),
        "text_feedoffset": noise(streams_of[10], (D,), 0.2, 1.1953125, ((0, 2),)),
        "text_upward": noise(streams_of[11], (D, FF), D ** -0.5, 0.21875, ((0, 2),)),
        "text_upbias": noise(streams_of[12], (FF,), 0.2, 1.1953125, ((0, 2),)),
        "text_downward": noise(streams_of[13], (FF, D), FF ** -0.5, 0.109375, ((0, 2),)),
        "text_downbias": noise(streams_of[14], (D,), 0.2, 1.1953125, ((0, 2),)),
        "text_endgain": jnp.clip(1.0 + 0.15 * jax.random.normal(streams_of[15], (D,), jnp.float32), 0.25, 1.75).astype(jnp.bfloat16),
        "text_endoffset": noise(streams_of[16], (D,), 0.2, 1.1953125, ((0, 2),)),
        "text_project": noise(streams_of[17], (D, EMBED), D ** -0.5, 0.21875, ((0, 2),)),
        "image_gain": jnp.clip(1.0 + 0.15 * jax.random.normal(streams_of[18], (D,), jnp.float32), 0.25, 1.75).astype(jnp.bfloat16),
        "image_offset": noise(streams_of[19], (D,), 0.2, 1.1953125),
        "image_joint": noise(streams_of[20], (D, 3 * D), D ** -0.5, 0.21875),
        "image_mixer": noise(streams_of[21], (D, D), (D // 7) ** -0.5, 0.5),
        "image_mixbias": noise(streams_of[22], (D,), 0.2, 1.1953125),
        "image_feedgain": jnp.clip(1.0 + 0.15 * jax.random.normal(streams_of[23], (D,), jnp.float32), 0.25, 1.75).astype(jnp.bfloat16),
        "image_feedoffset": noise(streams_of[24], (D,), 0.2, 1.1953125),
        "image_upward": noise(streams_of[25], (D, FF), D ** -0.5, 0.21875),
        "image_upbias": noise(streams_of[26], (FF,), 0.2, 1.1953125),
        "image_downward": noise(streams_of[27], (FF, D), FF ** -0.5, 0.109375),
        "image_downbias": noise(streams_of[28], (D,), 0.2, 1.1953125),
        "image_endgain": jnp.clip(1.0 + 0.15 * jax.random.normal(streams_of[29], (D,), jnp.float32), 0.25, 1.75).astype(jnp.bfloat16),
        "image_endoffset": noise(streams_of[30], (D,), 0.2, 1.1953125),
        "image_project": noise(streams_of[31], (D, EMBED), D ** -0.5, 0.21875),
    }


@jax.custom_vjp
def low(v):
    return lax.optimization_barrier(v.astype(jnp.bfloat16)).astype(jnp.float32)

@jax.custom_vjp
def low_back(v):
    return v

def low_keep(v):
    return (low(v), None)

def low_pass(kept, grad):
    return (grad,)

def back_keep(v):
    return (v, None)

def back_low(kept, grad):
    return (low(grad),)
low.defvjp(low_keep, low_pass)
low_back.defvjp(back_keep, back_low)
HIGHEST = lax.Precision.HIGHEST
EPSILON = 1e-06

def matmul(left_side, right_side):
    return jnp.dot(left_side, right_side, precision=HIGHEST, preferred_element_type=jnp.float32)

def layer_norm(values, gain_vector, offset):
    centred = values - lax.optimization_barrier(jnp.mean(values, axis=-1, keepdims=True))
    variance = lax.optimization_barrier(jnp.mean(centred * centred, axis=-1, keepdims=True))
    return centred * lax.rsqrt(variance + EPSILON) * gain_vector + offset

def normalize(embedding):
    return embedding * lax.rsqrt(lax.optimization_barrier(jnp.sum(embedding * embedding, axis=-1, keepdims=True)) + EPSILON)

def block_embed(tokens, weights, length):
    norm_gain, norm_offset, joint_weight, mixer_weight, mixer_bias, feed_gain, feed_offset, up_weight, up_bias, down_weight, down_bias, end_gain, end_offset, projection = weights
    total_rows, model_width = tokens.shape
    seq_count = total_rows // length
    factor = HEAD_DIM ** (-0.5)
    normed = low(layer_norm(tokens, norm_gain, norm_offset))
    triple = low(low_back(matmul(normed, joint_weight))).reshape(seq_count, length, 3, HEADS, HEAD_DIM)
    queries = triple[:, :, 0]
    keyset = triple[:, :, 1]
    valueset = triple[:, :, 2]
    scores = low_back(jnp.einsum('sqhd,skhd->shqk', queries, keyset, precision=HIGHEST) * factor)
    soft_low = low(jax.nn.softmax(scores, axis=-1))
    attended = jnp.einsum('shqk,skhd->sqhd', soft_low, valueset, precision=HIGHEST)
    attended = low(low_back(attended.reshape(total_rows, model_width)))
    residual = tokens + low_back(matmul(attended, mixer_weight)) + mixer_bias
    normed_two = low(layer_norm(residual, feed_gain, feed_offset))
    pre_active = low_back(matmul(normed_two, up_weight)) + up_bias
    active = low(jax.nn.gelu(pre_active))
    output = residual + low_back(matmul(active, down_weight)) + down_bias
    final_norm = layer_norm(output, end_gain, end_offset)
    pooled = lax.optimization_barrier(jnp.mean(final_norm.reshape(seq_count, length, model_width), axis=1))
    embedding = low_back(matmul(low(pooled), projection))
    return normalize(embedding)

def contrast(text_unit, image_unit, live_mask, scale_value, live_total):
    temper = jnp.exp(scale_value[0])
    text_low = low(text_unit)
    image_low = low(image_unit)
    text_blocks = text_low.reshape(GROUPS, SLOTS, EMBED)
    live_blocks = live_mask.reshape(GROUPS, SLOTS)

    def row_block(column_sum, inputs):
        block_rows, block_live = inputs
        cosine = low_back(lax.dot_general(block_rows, image_low, (((1,), (1,)), ((), ())), precision=HIGHEST, preferred_element_type=jnp.float32))
        scaled = jnp.exp(temper * cosine - temper)
        row_sum = lax.optimization_barrier(jnp.sum(scaled * live_mask[None, :], axis=1))
        column_sum = column_sum + lax.optimization_barrier(jnp.sum(scaled * block_live[:, None], axis=0))
        return (column_sum, temper + jnp.log(row_sum))
    column_sum, row_log = lax.scan(jax.checkpoint(row_block), jnp.zeros((PAIRS,), jnp.float32), (text_blocks, live_blocks))
    row_log = row_log.reshape(PAIRS)
    column_log = temper + jnp.log(column_sum)
    diagonal = temper * lax.optimization_barrier(jnp.sum(text_low * image_low, axis=1))
    loss_terms = live_mask * (row_log - diagonal) + live_mask * (column_log - diagonal)
    return jnp.sum(loss_terms) / (2.0 * live_total)

def reference(text_tokens, image_tokens, pair_counts, log_scale, text_gain, text_offset, text_joint, text_mixer, text_mixbias, text_feedgain, text_feedoffset, text_upward, text_upbias, text_downward, text_downbias, text_endgain, text_endoffset, text_project, image_gain, image_offset, image_joint, image_mixer, image_mixbias, image_feedgain, image_feedoffset, image_upward, image_upbias, image_downward, image_downbias, image_endgain, image_endoffset, image_project):
    text_weights = tuple((weight_array.astype(jnp.float32) for weight_array in (text_gain, text_offset, text_joint, text_mixer, text_mixbias, text_feedgain, text_feedoffset, text_upward, text_upbias, text_downward, text_downbias, text_endgain, text_endoffset, text_project)))
    image_weights = tuple((weight_array.astype(jnp.float32) for weight_array in (image_gain, image_offset, image_joint, image_mixer, image_mixbias, image_feedgain, image_feedoffset, image_upward, image_upbias, image_downward, image_downbias, image_endgain, image_endoffset, image_project)))
    live_mask = (jnp.arange(SLOTS)[None, :] < pair_counts[:, None]).astype(jnp.float32).reshape(PAIRS)
    live_total = jnp.sum(live_mask)
    image_rows = image_tokens.astype(jnp.float32).reshape(GROUPS, SLOTS * IMAGE_LEN, D)
    image_unit = lax.map(partial(block_embed, weights=image_weights, length=IMAGE_LEN), image_rows).reshape(PAIRS, EMBED)

    def objective(weights, scale_value, tokens):
        token_rows = tokens.reshape(GROUPS, SLOTS * TEXT_LEN, D)
        embed_block = jax.checkpoint(partial(block_embed, weights=weights, length=TEXT_LEN))
        text_unit = lax.map(embed_block, token_rows).reshape(PAIRS, EMBED)
        return contrast(text_unit, image_unit, live_mask, scale_value, live_total)
    loss_value, pullback = jax.vjp(objective, text_weights, log_scale, text_tokens.astype(jnp.float32))
    weight_grads, scale_grad, token_grad = pullback(jnp.ones_like(loss_value))
    return (weight_grads[0], weight_grads[1], weight_grads[2], weight_grads[3], weight_grads[4], weight_grads[5], weight_grads[6], weight_grads[7], weight_grads[8], weight_grads[9], weight_grads[10], weight_grads[11], weight_grads[12], weight_grads[13], scale_grad, token_grad, loss_value.reshape(1))
```

```python
import functools

import jax
import jax.numpy as jnp
from jax import lax
from jax.experimental import pallas as pl
from jax.experimental.pallas import tpu as pltpu
from jax.sharding import PartitionSpec as P

HEADS = 12
HEAD_DIM = 64
TEXT_LEN = 16
IMAGE_LEN = 50
SLOTS = 36


EPSILON = 1e-06


def product(left_side, right_side):
    return jnp.dot(left_side, right_side, preferred_element_type=jnp.float32)


def contract_last(left_side, right_side):
    return lax.dot_general(
        left_side, right_side, (((1,), (1,)), ((), ())), preferred_element_type=jnp.float32
    )


def contract_first(left_side, right_side):
    return lax.dot_general(
        left_side, right_side, (((0,), (0,)), ((), ())), preferred_element_type=jnp.float32
    )


def layer_norm(values, gain_vector, offset):
    centred = values - jnp.mean(values, axis=-1, keepdims=True)
    variance = jnp.mean(centred * centred, axis=-1, keepdims=True)
    return centred * lax.rsqrt(variance + EPSILON) * gain_vector.astype(
        jnp.float32
    ) + offset.astype(jnp.float32)


def normalize(embedding):
    return embedding * lax.rsqrt(jnp.sum(embedding * embedding, axis=-1, keepdims=True) + EPSILON)


def forward_block(tokens, weights, length):
    (
        norm_gain,
        norm_offset,
        joint_weight,
        mixer_weight,
        mixer_bias,
        feed_gain,
        feed_offset,
        up_weight,
        up_bias,
        down_weight,
        down_bias,
        end_gain,
        end_offset,
        projection,
    ) = weights
    inputs = tokens.astype(jnp.float32)
    total_rows, model_width = inputs.shape
    seq_count = total_rows // length
    factor = HEAD_DIM ** (-0.5)
    normed = layer_norm(inputs, norm_gain, norm_offset).astype(jnp.bfloat16)
    triple = (
        product(normed, joint_weight)
        .astype(jnp.bfloat16)
        .reshape(seq_count, length, 3, HEADS, HEAD_DIM)
    )
    queries = triple[:, :, 0]
    keyset = triple[:, :, 1]
    valueset = triple[:, :, 2]
    scores = (
        jnp.einsum("sqhd,skhd->shqk", queries, keyset, preferred_element_type=jnp.float32) * factor
    )
    soft_weights = jax.nn.softmax(scores, axis=-1)
    soft_low = soft_weights.astype(jnp.bfloat16)
    attended = jnp.einsum("shqk,skhd->sqhd", soft_low, valueset, preferred_element_type=jnp.float32)
    attended = attended.reshape(total_rows, model_width).astype(jnp.bfloat16)
    residual = inputs + product(attended, mixer_weight) + mixer_bias.astype(jnp.float32)
    normed_two = layer_norm(residual, feed_gain, feed_offset).astype(jnp.bfloat16)
    pre_active = product(normed_two, up_weight) + up_bias.astype(jnp.float32)
    active = jax.nn.gelu(pre_active).astype(jnp.bfloat16)
    output = residual + product(active, down_weight) + down_bias.astype(jnp.float32)
    final_norm = layer_norm(output, end_gain, end_offset)
    pooled = jnp.mean(final_norm.reshape(seq_count, length, model_width), axis=1)
    embedding = product(pooled.astype(jnp.bfloat16), projection)
    unit_vector = normalize(embedding)
    kept_values = (
        inputs,
        normed,
        triple,
        soft_weights,
        soft_low,
        attended,
        residual,
        normed_two,
        pre_active,
        active,
        output,
        pooled,
        embedding,
    )
    return (unit_vector, kept_values)


def backward_block(kept_values, weights, unit_grad, length):
    (
        norm_gain,
        norm_offset,
        joint_weight,
        mixer_weight,
        mixer_bias,
        feed_gain,
        feed_offset,
        up_weight,
        up_bias,
        down_weight,
        down_bias,
        end_gain,
        end_offset,
        projection,
    ) = weights
    (
        inputs,
        normed,
        triple,
        soft_weights,
        soft_low,
        attended,
        residual,
        normed_two,
        pre_active,
        active,
        output,
        pooled,
        embedding,
    ) = kept_values
    total_rows, model_width = inputs.shape
    seq_count = total_rows // length
    factor = HEAD_DIM ** (-0.5)
    unused_unit, norm_back = jax.vjp(normalize, embedding)
    embed_grad = norm_back(unit_grad)[0].astype(jnp.bfloat16)
    pooled_grad = contract_last(embed_grad, projection)
    final_grad = jnp.broadcast_to(
        pooled_grad[:, None, :] / length, (seq_count, length, model_width)
    ).reshape(total_rows, model_width)
    unused_final, end_back = jax.vjp(
        layer_norm, output, end_gain.astype(jnp.float32), end_offset.astype(jnp.float32)
    )
    output_grad, endgain_grad, endoffset_grad = end_back(final_grad)
    down_low = output_grad.astype(jnp.bfloat16)
    downbias_grad = jnp.sum(output_grad, axis=0)
    active_grad = contract_last(down_low, down_weight)
    unused_active, gelu_back = jax.vjp(jax.nn.gelu, pre_active)
    pre_grad = gelu_back(active_grad)[0]
    upbias_grad = jnp.sum(pre_grad, axis=0)
    pre_low = pre_grad.astype(jnp.bfloat16)
    normed_grad = contract_last(pre_low, up_weight)
    unused_feed, feed_back = jax.vjp(
        layer_norm, residual, feed_gain.astype(jnp.float32), feed_offset.astype(jnp.float32)
    )
    residual_part, feedgain_grad, feedoffset_grad = feed_back(normed_grad)
    residual_grad = output_grad + residual_part
    mixbias_grad = jnp.sum(residual_grad, axis=0)
    mix_low = residual_grad.astype(jnp.bfloat16)
    attended_grad = contract_last(mix_low, mixer_weight).astype(jnp.bfloat16)
    attended_grad = attended_grad.reshape(seq_count, length, HEADS, HEAD_DIM)
    queries = triple[:, :, 0]
    keyset = triple[:, :, 1]
    valueset = triple[:, :, 2]
    soft_grad = jnp.einsum(
        "sqhd,skhd->shqk", attended_grad, valueset, preferred_element_type=jnp.float32
    )
    value_grad = jnp.einsum(
        "shqk,sqhd->skhd", soft_low, attended_grad, preferred_element_type=jnp.float32
    )
    score_grad = soft_weights * (
        soft_grad - jnp.sum(soft_weights * soft_grad, axis=-1, keepdims=True)
    )
    score_grad = score_grad.astype(jnp.bfloat16)
    query_grad = (
        jnp.einsum("shqk,skhd->sqhd", score_grad, keyset, preferred_element_type=jnp.float32)
        * factor
    )
    key_grad = (
        jnp.einsum("shqk,sqhd->skhd", score_grad, queries, preferred_element_type=jnp.float32)
        * factor
    )
    triple_grad = jnp.stack([query_grad, key_grad, value_grad], axis=2)
    triple_grad = triple_grad.reshape(total_rows, 3 * model_width).astype(jnp.bfloat16)
    first_grad = contract_last(triple_grad, joint_weight)
    unused_first, first_back = jax.vjp(
        layer_norm, inputs, norm_gain.astype(jnp.float32), norm_offset.astype(jnp.float32)
    )
    input_part, gain_grad, offset_grad = first_back(first_grad)
    input_grad = residual_grad + input_part
    factors = (
        (normed, triple_grad),
        (attended, mix_low),
        (normed_two, pre_low),
        (active, down_low),
        (pooled.astype(jnp.bfloat16), embed_grad),
    )
    vectors = (
        gain_grad,
        offset_grad,
        mixbias_grad,
        feedgain_grad,
        feedoffset_grad,
        upbias_grad,
        downbias_grad,
        endgain_grad,
        endoffset_grad,
    )
    return (factors, vectors, input_grad)


WIDTH = 768
HALF = 384
QUARTER = 192
SUB = 2
ROWS = QUARTER // SUB
PART = ROWS // 2
UNITS = 13
STEPS = UNITS * SUB
FACTOR_A = 8
FACTOR_B = 10
VECTOR_ROWS = 16
MESH = pl.DeviceIdType.MESH


def factor_a(unit):
    return jnp.minimum(unit, 4) + jnp.clip(unit - 7, 0, 2) + jnp.maximum(unit - 11, 0)


def factor_b(unit):
    return jnp.maximum(unit - 3, 0)


def reduce_body(
    a_hbm,
    b_hbm,
    vector_ref,
    grad_hbm,
    vector_out,
    a_vmem,
    b_vmem,
    core_out,
    part,
    core_in,
    x_in,
    y_in,
    end_in,
    mid_in,
    total,
    vector_core,
    vector_x,
    vector_y,
    vector_z,
    vector_sum,
    a_sem,
    b_sem,
    core_sems,
    x_sems,
    y_sems,
    end_sems,
    mid_sems,
    back_sems,
    wide_sems,
    twin_sems,
    out_sem,
    vector_sems,
):
    dp = lax.axis_index("dp")
    x = lax.axis_index("fsdp")
    z = dp // 4
    y = (dp // 2) % 2
    core = dp % 2
    at_end = (z == 0) | (z == 3)
    at_mid = (z == 1) | (z == 2)
    z_pair = z + 1 - 2 * (z % 2)
    core_peer = (dp + 1 - 2 * core, x)
    x_peer = (dp, 1 - x)
    y_peer = (dp + 2 - 4 * y, x)
    pair_peer = (z_pair * 4 + y * 2 + core, x)
    mid_peer = ((3 - z) * 4 + y * 2 + core, x)

    a_copies = [pltpu.make_async_copy(a_hbm.at[k], a_vmem.at[k], a_sem.at[k]) for k in range(FACTOR_A)]
    b_copies = [pltpu.make_async_copy(b_hbm.at[k], b_vmem.at[k], b_sem.at[k]) for k in range(FACTOR_B)]
    for unit in range(UNITS):
        if unit < 5 or unit in (8, 9, 12):
            a_copies[min(unit, 4) + min(max(unit - 7, 0), 2) + max(unit - 11, 0)].start()
        if unit == 0 or unit >= 4:
            b_copies[max(unit - 3, 0)].start()

    barrier = pltpu.get_barrier_semaphore()
    for peer in (core_peer, x_peer, y_peer):
        pl.semaphore_signal(barrier, inc=1, device_id=peer, device_id_type=MESH)
    for step in range(1, 4):
        other = ((z + step) % 4) * 4 + y * 2 + core
        pl.semaphore_signal(barrier, inc=1, device_id=(other, x), device_id_type=MESH)
    pl.semaphore_wait(barrier, 6)

    def remote(source, target, sems, index, peer):
        return pltpu.make_async_remote_copy(
            src_ref=source,
            dst_ref=target,
            send_sem=sems.at[0, index],
            recv_sem=sems.at[1, index],
            device_id=peer,
            device_id_type=MESH,
        )

    def core_copy(step):
        return remote(core_out.at[step % 2], core_in.at[step], core_sems, step, core_peer)

    def x_copy(step):
        return remote(part.at[step, 1 - x], x_in.at[step], x_sems, step, x_peer)

    def y_copy(step):
        rows = pl.ds(pl.multiple_of((1 - y) * PART, PART), PART)
        return remote(part.at[step, x, rows], y_in.at[step], y_sems, step, y_peer)

    def own_rows():
        return pl.ds(pl.multiple_of(y * PART, PART), PART)

    def end_copy(step):
        return remote(part.at[step, x, own_rows()], end_in.at[step], end_sems, step, pair_peer)

    def mid_copy(step):
        return remote(part.at[step, x, own_rows()], mid_in.at[step], mid_sems, step, mid_peer)

    def total_rows(step):
        return pl.ds(pl.multiple_of(y * PART, PART), PART)

    def back_copy(step):
        piece = total.at[step, core, total_rows(step)]
        return remote(piece, piece, back_sems, step, pair_peer)

    def wide_copy(step):
        piece = total.at[step, core, total_rows(step)]
        return remote(piece, piece, wide_sems, step, y_peer)

    def twin_copy(step):
        piece = total.at[step, core]
        return remote(piece, piece, twin_sems, step, core_peer)

    def out_copy(step, which):
        unit = step // SUB
        offset = pl.multiple_of(which * QUARTER + (step % SUB) * ROWS, ROWS)
        return pltpu.make_async_copy(
            total.at[step, which], grad_hbm.at[unit, pl.ds(offset, ROWS)], out_sem.at[step, which]
        )

    vector_first = remote(vector_ref, vector_core, vector_sems, 0, core_peer)
    vector_second = remote(vector_sum.at[0], vector_x, vector_sems, 1, x_peer)
    vector_third = remote(vector_sum.at[1], vector_y, vector_sems, 2, y_peer)
    vector_last = []
    for step in range(1, 4):
        other = ((z + step) % 4) * 4 + y * 2 + core
        vector_last.append(
            remote(vector_sum.at[2], vector_z.at[step - 1], vector_sems, 2 + step, (other, x))
        )

    def wide(values):
        return values.astype(jnp.float32)

    def low(values):
        return values.astype(jnp.bfloat16)

    @pl.loop(0, STEPS + 8)
    def _(time):
        @pl.when((time >= 1) & (time - 1 < STEPS))
        def _():
            step = time - 1
            core_copy(step).wait()
            part[step, 1 - x] = low(wide(part[step, 1 - x]) + wide(core_in[step, 1 - x]))
            x_copy(step).start()
            part[step, x] = low(wide(part[step, x]) + wide(core_in[step, x]))

        @pl.when(time < STEPS)
        def _():
            step = time
            unit = step // SUB
            half = step % SUB
            slot_a = factor_a(unit)
            slot_b = factor_b(unit)

            @pl.when((half == 0) & ((unit < 5) | (unit == 8) | (unit == 9) | (unit == 12)))
            def _():
                pltpu.make_async_copy(a_hbm.at[slot_a], a_vmem.at[slot_a], a_sem.at[slot_a]).wait()

            @pl.when((half == 0) & ((unit == 0) | (unit >= 4)))
            def _():
                pltpu.make_async_copy(b_hbm.at[slot_b], b_vmem.at[slot_b], b_sem.at[slot_b]).wait()

            right = b_vmem[slot_b]
            for which in range(2):
                rows = pl.ds(
                    pl.multiple_of(which * HALF + (1 - core) * QUARTER + half * ROWS, ROWS), ROWS
                )
                core_out[step % 2, which] = low(product(a_vmem[slot_a, rows], right))
            core_copy(step).start()
            for which in range(2):
                rows = pl.ds(
                    pl.multiple_of(which * HALF + core * QUARTER + half * ROWS, ROWS), ROWS
                )
                part[step, which] = low(product(a_vmem[slot_a, rows], right))

        @pl.when((time >= 2) & (time - 2 < STEPS))
        def _():
            step = time - 2
            x_copy(step).wait()
            rows = pl.ds(pl.multiple_of((1 - y) * PART, PART), PART)
            part[step, x, rows] = low(wide(part[step, x, rows]) + wide(x_in[step, rows]))
            y_copy(step).start()
            part[step, x, own_rows()] = low(
                wide(part[step, x, own_rows()]) + wide(x_in[step, own_rows()])
            )

        @pl.when((time >= 3) & (time - 3 < STEPS))
        def _():
            step = time - 3
            y_copy(step).wait()
            part[step, x, own_rows()] = low(
                wide(part[step, x, own_rows()]) + wide(y_in[step])
            )

            @pl.when(at_end)
            def _():
                end_copy(step).start()

        @pl.when((time >= 4) & (time - 4 < STEPS))
        def _():
            step = time - 4

            @pl.when(at_end)
            def _():
                end_copy(step).wait_send()

            @pl.when(at_mid)
            def _():
                end_copy(step).wait_recv()
                part[step, x, own_rows()] = low(
                    wide(part[step, x, own_rows()]) + wide(end_in[step])
                )
                mid_copy(step).start()

        @pl.when((time >= 5) & (time - 5 < STEPS) & at_mid)
        def _():
            step = time - 5
            mid_copy(step).wait()
            total[step, core, total_rows(step)] = low(
                wide(part[step, x, own_rows()]) + wide(mid_in[step])
            )
            back_copy(step).start()
            wide_copy(step).start()

        @pl.when((time >= 6) & (time - 6 < STEPS))
        def _():
            step = time - 6

            @pl.when(at_end)
            def _():
                back_copy(step).wait_recv()
                wide_copy(step).start()

            @pl.when(at_mid)
            def _():
                back_copy(step).wait_send()

        @pl.when((time >= 7) & (time - 7 < STEPS))
        def _():
            step = time - 7
            wide_copy(step).wait()
            twin_copy(step).start()
            out_copy(step, core).start()

        @pl.when((time >= 8) & (time - 8 < STEPS))
        def _():
            step = time - 8
            twin_copy(step).wait()
            out_copy(step, 1 - core).start()

        @pl.when(time == 0)
        def _():
            vector_first.start()

        @pl.when(time == 1)
        def _():
            vector_first.wait()
            vector_sum[0] = vector_ref[...] + vector_core[...]
            vector_second.start()

        @pl.when(time == 3)
        def _():
            vector_second.wait()
            vector_sum[1] = vector_sum[0] + vector_x[...]
            vector_third.start()

        @pl.when(time == 5)
        def _():
            vector_third.wait()
            vector_sum[2] = vector_sum[1] + vector_y[...]
            for copy in vector_last:
                copy.start()

        @pl.when(time == 7)
        def _():
            for copy in vector_last:
                copy.wait()
            order = lax.broadcasted_iota(jnp.int32, (VECTOR_ROWS, WIDTH), 0) * 0 + z
            own = vector_sum[2]
            before_one = vector_z[0]
            before_two = vector_z[1]
            before_three = vector_z[2]

            def pick(where):
                shift = (order - where + 4) % 4
                return jnp.where(
                    shift == 0,
                    own,
                    jnp.where(
                        shift == 1,
                        before_one,
                        jnp.where(shift == 2, before_two, before_three),
                    ),
                )

            vector_out[...] = (pick(0) + pick(1)) + (pick(2) + pick(3))

    @pl.loop(0, STEPS)
    def _(step):
        out_copy(step, core).wait()
        out_copy(step, 1 - core).wait()


def reduce_kernel(factors, vectors):
    (normed, triple_grad), (attended, mix_low), (normed_two, pre_low), (active, down_low), last = (
        factors
    )
    pooled, embed_grad = last
    rows = normed.shape[0]
    active_t = active.T.reshape(2, 4, HALF, rows).transpose(1, 0, 2, 3).reshape(4, WIDTH, rows)
    pooled_t = jnp.pad(pooled.T, ((0, 0), (0, rows - pooled.shape[0])))
    left = jnp.concatenate(
        [active_t, normed_two.T[None], attended.T[None], normed.T[None], pooled_t[None]], axis=0
    )
    right = jnp.concatenate(
        [
            down_low[None],
            pre_low.reshape(rows, 4, WIDTH).transpose(1, 0, 2),
            mix_low[None],
            triple_grad.reshape(rows, 3, WIDTH).transpose(1, 0, 2),
            jnp.pad(embed_grad, ((0, rows - embed_grad.shape[0]), (0, 0)))[None],
        ],
        axis=0,
    )
    packed = jnp.concatenate([vector.reshape(-1, WIDTH) for vector in vectors], axis=0)
    packed = jnp.pad(packed, ((0, VECTOR_ROWS - packed.shape[0]), (0, 0)))
    any_spec = pl.BlockSpec(memory_space=pl.ANY)
    vmem_spec = pl.BlockSpec(memory_space=pltpu.VMEM)
    dma = pltpu.SemaphoreType.DMA
    grads, packed = pl.pallas_call(
        reduce_body,
        out_shape=(
            jax.ShapeDtypeStruct((UNITS, HALF, WIDTH), jnp.bfloat16),
            jax.ShapeDtypeStruct((VECTOR_ROWS, WIDTH), jnp.float32),
        ),
        in_specs=[any_spec, any_spec, vmem_spec],
        out_specs=(any_spec, vmem_spec),
        scratch_shapes=[
            pltpu.VMEM((FACTOR_A, WIDTH, rows), jnp.bfloat16),
            pltpu.VMEM((FACTOR_B, rows, WIDTH), jnp.bfloat16),
            pltpu.VMEM((2, 2, ROWS, WIDTH), jnp.bfloat16),
            pltpu.VMEM((STEPS, 2, ROWS, WIDTH), jnp.bfloat16),
            pltpu.VMEM((STEPS, 2, ROWS, WIDTH), jnp.bfloat16),
            pltpu.VMEM((STEPS, ROWS, WIDTH), jnp.bfloat16),
            pltpu.VMEM((STEPS, PART, WIDTH), jnp.bfloat16),
            pltpu.VMEM((STEPS, PART, WIDTH), jnp.bfloat16),
            pltpu.VMEM((STEPS, PART, WIDTH), jnp.bfloat16),
            pltpu.VMEM((STEPS, 2, ROWS, WIDTH), jnp.bfloat16),
            pltpu.VMEM((VECTOR_ROWS, WIDTH), jnp.float32),
            pltpu.VMEM((VECTOR_ROWS, WIDTH), jnp.float32),
            pltpu.VMEM((VECTOR_ROWS, WIDTH), jnp.float32),
            pltpu.VMEM((3, VECTOR_ROWS, WIDTH), jnp.float32),
            pltpu.VMEM((3, VECTOR_ROWS, WIDTH), jnp.float32),
            dma((FACTOR_A,)),
            dma((FACTOR_B,)),
            dma((2, STEPS)),
            dma((2, STEPS)),
            dma((2, STEPS)),
            dma((2, STEPS)),
            dma((2, STEPS)),
            dma((2, STEPS)),
            dma((2, STEPS)),
            dma((2, STEPS)),
            dma((STEPS, 2)),
            dma((2, 6)),
        ],
        compiler_params=pltpu.CompilerParams(
            collective_id=0, has_side_effects=True, vmem_limit_bytes=62 * 1024 * 1024
        ),
    )(left, right, packed)
    shard = lax.axis_index("fsdp")
    wide = grads.astype(jnp.float32)

    def matrix(first, count):
        return wide[first : first + count].transpose(1, 0, 2).reshape(HALF, count * WIDTH)

    def vector(first, count):
        full = packed[first : first + count].reshape(2, count * HALF)
        return lax.dynamic_index_in_dim(full, shard, 0, keepdims=False)

    return (
        vector(0, 1),
        vector(1, 1),
        matrix(9, 3),
        matrix(8, 1),
        vector(2, 1),
        vector(3, 1),
        vector(4, 1),
        matrix(4, 4),
        vector(5, 4),
        wide[0:4].reshape(4 * HALF, WIDTH),
        vector(9, 1),
        vector(10, 1),
        vector(11, 1),
        matrix(12, 1),
    )


def reduce_plain(factors, vectors):
    terms = [contract_first(left, right) for left, right in factors]
    joint, mixer, upward, downward, project = terms
    gain, offset, mixbias, feedgain, feedoffset, upbias, downbias, endgain, endoffset = vectors
    ordered = (
        gain,
        offset,
        joint,
        mixer,
        mixbias,
        feedgain,
        feedoffset,
        upward,
        upbias,
        downward,
        downbias,
        endgain,
        endoffset,
        project,
    )
    shards = tuple(
        lax.psum_scatter(term, "fsdp", scatter_dimension=0, tiled=True) for term in ordered
    )
    return lax.psum(shards, "dp")


def on_device(
    text_tokens,
    image_tokens,
    pair_counts,
    log_scale,
    text_gain,
    text_offset,
    text_joint,
    text_mixer,
    text_mixbias,
    text_feedgain,
    text_feedoffset,
    text_upward,
    text_upbias,
    text_downward,
    text_downbias,
    text_endgain,
    text_endoffset,
    text_project,
    image_gain,
    image_offset,
    image_joint,
    image_mixer,
    image_mixbias,
    image_feedgain,
    image_feedoffset,
    image_upward,
    image_upbias,
    image_downward,
    image_downbias,
    image_endgain,
    image_endoffset,
    image_project,
):
    image_weights = (
        image_gain,
        image_offset,
        image_joint,
        image_mixer,
        image_mixbias,
        image_feedgain,
        image_feedoffset,
        image_upward,
        image_upbias,
        image_downward,
        image_downbias,
        image_endgain,
        image_endoffset,
        image_project,
    )
    group_count = lax.axis_size("dp") * lax.axis_size("fsdp")
    device = lax.axis_index("dp") * lax.axis_size("fsdp") + lax.axis_index("fsdp")
    pair_total = group_count * SLOTS
    live_all = (
        (jnp.arange(SLOTS)[None, :] < pair_counts[:, None]).astype(jnp.float32).reshape(pair_total)
    )
    live_total = jnp.sum(live_all)
    text_live = lax.dynamic_slice_in_dim(live_all, device * SLOTS, SLOTS)
    temper = jnp.exp(log_scale[0])
    half_inverse = 1.0 / (2.0 * live_total)
    image_unit = forward_block(image_tokens, image_weights, IMAGE_LEN)[0]
    image_low = image_unit.astype(jnp.bfloat16)
    shard_piece = lax.all_gather(image_low, ("dp", "fsdp"), axis=0, tiled=True)
    text_weights = tuple(
        lax.all_gather(shard, "fsdp", axis=0, tiled=True)
        for shard in (
            text_gain,
            text_offset,
            text_joint,
            text_mixer,
            text_mixbias,
            text_feedgain,
            text_feedoffset,
            text_upward,
            text_upbias,
            text_downward,
            text_downbias,
            text_endgain,
            text_endoffset,
            text_project,
        )
    )
    text_unit, kept_values = forward_block(text_tokens, text_weights, TEXT_LEN)
    text_low = text_unit.astype(jnp.bfloat16)
    cosine = contract_last(text_low, shard_piece)
    scaled = jnp.exp(temper * cosine - temper)
    image_live = live_all
    forward_row_sum = jnp.sum(scaled * image_live[None, :], axis=1)
    forward_column_sum = jnp.sum(scaled * text_live[:, None], axis=0)
    column_sum = forward_column_sum
    column_sum = lax.psum(column_sum, ("dp", "fsdp"))
    diagonal_cos = jnp.sum(text_low.astype(jnp.float32) * image_low.astype(jnp.float32), axis=1)
    row_log = temper + jnp.log(forward_row_sum)
    column_log = temper + jnp.log(lax.dynamic_slice_in_dim(column_sum, device * SLOTS, SLOTS))
    diagonal = temper * diagonal_cos
    loss_part = jnp.sum(text_live * (row_log - diagonal) + text_live * (column_log - diagonal)) / (
        2.0 * live_total
    )
    coupling = (
        scaled * (text_live / forward_row_sum)[:, None] * image_live[None, :]
        + scaled * text_live[:, None] * (image_live / column_sum)[None, :]
    ) * half_inverse
    temper_grad = jnp.sum(coupling * cosine)
    unit_grad = product((temper * coupling).astype(jnp.bfloat16), shard_piece)
    unit_grad, temper_grad = (unit_grad, temper_grad)
    unit_grad = unit_grad - temper / live_total * text_live[:, None] * image_low.astype(jnp.float32)
    temper_grad = temper_grad - jnp.sum(text_live * diagonal_cos) / live_total
    loss_total, scale_total = lax.psum((loss_part, temper * temper_grad), ("dp", "fsdp"))
    factors, vectors, token_grad = backward_block(
        kept_values, text_weights, unit_grad, TEXT_LEN
    )
    if (lax.axis_size("dp"), lax.axis_size("fsdp")) == (16, 2):
        final_grads = reduce_kernel(factors, vectors)
    else:
        final_grads = reduce_plain(factors, vectors)
    return (
        *final_grads,
        jnp.reshape(scale_total, (1,)),
        token_grad,
        jnp.reshape(loss_total, (1,)),
    )


def solution(mesh):
    return jax.shard_map(
        on_device,
        mesh=mesh,
        in_specs=(
            P(("dp", "fsdp"), None),
            P(("dp", "fsdp"), None),
            P(),
            P(),
            P("fsdp"),
            P("fsdp"),
            P("fsdp", None),
            P("fsdp", None),
            P("fsdp"),
            P("fsdp"),
            P("fsdp"),
            P("fsdp", None),
            P("fsdp"),
            P("fsdp", None),
            P("fsdp"),
            P("fsdp"),
            P("fsdp"),
            P("fsdp", None),
            P(),
            P(),
            P(),
            P(),
            P(),
            P(),
            P(),
            P(),
            P(),
            P(),
            P(),
            P(),
            P(),
            P(),
        ),
        out_specs=(
            P("fsdp"),
            P("fsdp"),
            P("fsdp", None),
            P("fsdp", None),
            P("fsdp"),
            P("fsdp"),
            P("fsdp"),
            P("fsdp", None),
            P("fsdp"),
            P("fsdp", None),
            P("fsdp"),
            P("fsdp"),
            P("fsdp"),
            P("fsdp", None),
            P(),
            P(("dp", "fsdp"), None),
            P(),
        ),
        check_vma=False,
    )
```

```python
import jax
import jax.numpy as jnp
from jax import lax
from jax.experimental import pallas as pl
from jax.experimental.pallas import tpu as pltpu
from jax.sharding import PartitionSpec as P

HEADS = 12
HEAD_DIM = 64
TEXT_LEN = 16
IMAGE_LEN = 50
SLOTS = 36


EPSILON = 1e-06


def product(left_side, right_side):
    return jnp.dot(left_side, right_side, preferred_element_type=jnp.float32)


def contract_last(left_side, right_side):
    return lax.dot_general(
        left_side, right_side, (((1,), (1,)), ((), ())), preferred_element_type=jnp.float32
    )


def contract_first(left_side, right_side):
    return lax.dot_general(
        left_side, right_side, (((0,), (0,)), ((), ())), preferred_element_type=jnp.float32
    )


def layer_norm(values, gain_vector, offset):
    centred = values - jnp.mean(values, axis=-1, keepdims=True)
    variance = jnp.mean(centred * centred, axis=-1, keepdims=True)
    return centred * lax.rsqrt(variance + EPSILON) * gain_vector.astype(
        jnp.float32
    ) + offset.astype(jnp.float32)


def normalize(embedding):
    return embedding * lax.rsqrt(jnp.sum(embedding * embedding, axis=-1, keepdims=True) + EPSILON)


def forward_block(tokens, weights, length):
    (
        norm_gain,
        norm_offset,
        joint_weight,
        mixer_weight,
        mixer_bias,
        feed_gain,
        feed_offset,
        up_weight,
        up_bias,
        down_weight,
        down_bias,
        end_gain,
        end_offset,
        projection,
    ) = weights
    inputs = tokens.astype(jnp.float32)
    total_rows, model_width = inputs.shape
    seq_count = total_rows // length
    factor = HEAD_DIM ** (-0.5)
    normed = layer_norm(inputs, norm_gain, norm_offset).astype(jnp.bfloat16)
    triple = (
        product(normed, joint_weight)
        .astype(jnp.bfloat16)
        .reshape(seq_count, length, 3, HEADS, HEAD_DIM)
    )
    queries = triple[:, :, 0]
    keyset = triple[:, :, 1]
    valueset = triple[:, :, 2]
    scores = (
        jnp.einsum("sqhd,skhd->shqk", queries, keyset, preferred_element_type=jnp.float32) * factor
    )
    soft_weights = jax.nn.softmax(scores, axis=-1)
    soft_low = soft_weights.astype(jnp.bfloat16)
    attended = jnp.einsum("shqk,skhd->sqhd", soft_low, valueset, preferred_element_type=jnp.float32)
    attended = attended.reshape(total_rows, model_width).astype(jnp.bfloat16)
    residual = inputs + product(attended, mixer_weight) + mixer_bias.astype(jnp.float32)
    normed_two = layer_norm(residual, feed_gain, feed_offset).astype(jnp.bfloat16)
    pre_active = product(normed_two, up_weight) + up_bias.astype(jnp.float32)
    active = jax.nn.gelu(pre_active).astype(jnp.bfloat16)
    output = residual + product(active, down_weight) + down_bias.astype(jnp.float32)
    final_norm = layer_norm(output, end_gain, end_offset)
    pooled = jnp.mean(final_norm.reshape(seq_count, length, model_width), axis=1)
    embedding = product(pooled.astype(jnp.bfloat16), projection)
    unit_vector = normalize(embedding)
    kept_values = (
        inputs,
        normed,
        triple,
        soft_weights,
        soft_low,
        attended,
        residual,
        normed_two,
        pre_active,
        active,
        output,
        pooled,
        embedding,
    )
    return (unit_vector, kept_values)


def backward_block(kept_values, weights, unit_grad, length):
    (
        norm_gain,
        norm_offset,
        joint_weight,
        mixer_weight,
        mixer_bias,
        feed_gain,
        feed_offset,
        up_weight,
        up_bias,
        down_weight,
        down_bias,
        end_gain,
        end_offset,
        projection,
    ) = weights
    (
        inputs,
        normed,
        triple,
        soft_weights,
        soft_low,
        attended,
        residual,
        normed_two,
        pre_active,
        active,
        output,
        pooled,
        embedding,
    ) = kept_values
    total_rows, model_width = inputs.shape
    seq_count = total_rows // length
    factor = HEAD_DIM ** (-0.5)
    unused_unit, norm_back = jax.vjp(normalize, embedding)
    embed_grad = norm_back(unit_grad)[0].astype(jnp.bfloat16)
    pooled_grad = contract_last(embed_grad, projection)
    final_grad = jnp.broadcast_to(
        pooled_grad[:, None, :] / length, (seq_count, length, model_width)
    ).reshape(total_rows, model_width)
    unused_final, end_back = jax.vjp(
        layer_norm, output, end_gain.astype(jnp.float32), end_offset.astype(jnp.float32)
    )
    output_grad, endgain_grad, endoffset_grad = end_back(final_grad)
    down_low = output_grad.astype(jnp.bfloat16)
    downbias_grad = jnp.sum(output_grad, axis=0)
    active_grad = contract_last(down_low, down_weight)
    unused_active, gelu_back = jax.vjp(jax.nn.gelu, pre_active)
    pre_grad = gelu_back(active_grad)[0]
    upbias_grad = jnp.sum(pre_grad, axis=0)
    pre_low = pre_grad.astype(jnp.bfloat16)
    normed_grad = contract_last(pre_low, up_weight)
    unused_feed, feed_back = jax.vjp(
        layer_norm, residual, feed_gain.astype(jnp.float32), feed_offset.astype(jnp.float32)
    )
    residual_part, feedgain_grad, feedoffset_grad = feed_back(normed_grad)
    residual_grad = output_grad + residual_part
    mixbias_grad = jnp.sum(residual_grad, axis=0)
    mix_low = residual_grad.astype(jnp.bfloat16)
    attended_grad = contract_last(mix_low, mixer_weight).astype(jnp.bfloat16)
    attended_grad = attended_grad.reshape(seq_count, length, HEADS, HEAD_DIM)
    queries = triple[:, :, 0]
    keyset = triple[:, :, 1]
    valueset = triple[:, :, 2]
    soft_grad = jnp.einsum(
        "sqhd,skhd->shqk", attended_grad, valueset, preferred_element_type=jnp.float32
    )
    value_grad = jnp.einsum(
        "shqk,sqhd->skhd", soft_low, attended_grad, preferred_element_type=jnp.float32
    )
    score_grad = soft_weights * (
        soft_grad - jnp.sum(soft_weights * soft_grad, axis=-1, keepdims=True)
    )
    score_grad = score_grad.astype(jnp.bfloat16)
    query_grad = (
        jnp.einsum("shqk,skhd->sqhd", score_grad, keyset, preferred_element_type=jnp.float32)
        * factor
    )
    key_grad = (
        jnp.einsum("shqk,sqhd->skhd", score_grad, queries, preferred_element_type=jnp.float32)
        * factor
    )
    triple_grad = jnp.stack([query_grad, key_grad, value_grad], axis=2)
    triple_grad = triple_grad.reshape(total_rows, 3 * model_width).astype(jnp.bfloat16)
    first_grad = contract_last(triple_grad, joint_weight)
    unused_first, first_back = jax.vjp(
        layer_norm, inputs, norm_gain.astype(jnp.float32), norm_offset.astype(jnp.float32)
    )
    input_part, gain_grad, offset_grad = first_back(first_grad)
    input_grad = residual_grad + input_part
    factors = (
        (normed, triple_grad),
        (attended, mix_low),
        (normed_two, pre_low),
        (active, down_low),
        (pooled.astype(jnp.bfloat16), embed_grad),
    )
    vectors = (
        gain_grad,
        offset_grad,
        mixbias_grad,
        feedgain_grad,
        feedoffset_grad,
        upbias_grad,
        downbias_grad,
        endgain_grad,
        endoffset_grad,
    )
    return (factors, vectors, input_grad)


WIDTH = 768
HALF = 384
QUARTER = 192
SUB = 2
ROWS = QUARTER // SUB
PART = ROWS // 2
UNITS = 13
STEPS = UNITS * SUB
FACTOR_A = 8
FACTOR_B = 10
VECTOR_ROWS = 16
MESH = pl.DeviceIdType.MESH


ROOT_SCALE = 0.125
PAIR = 128
CUT = -1e30
TEXT_GROUP = 96
CHUNK = 96
SLOT_ROWS = 40
NEAR = 8
GELU_ROOT = 0.7978845608028654
GELU_CUBE = 0.044715


def wide(values):
    return values.astype(jnp.float32)


def low(values):
    return values.astype(jnp.bfloat16)


def centred_scale(values):
    centred = values - jnp.mean(values, axis=-1, keepdims=True)
    variance = jnp.mean(centred * centred, axis=-1, keepdims=True)
    rate = lax.rsqrt(variance + EPSILON)
    return centred * rate, rate


def gelu_value(values):
    inner = GELU_ROOT * (values + GELU_CUBE * (values * values * values))
    half = 0.5 * values
    return half + half * jnp.tanh(inner)


def gelu_slope(values):
    square = values * values
    bend = jnp.tanh(GELU_ROOT * values * (1.0 + GELU_CUBE * square))
    inner_slope = GELU_ROOT * (1.0 + (3.0 * GELU_CUBE) * square)
    return 0.5 * (1.0 + bend) + 0.5 * values * (1.0 - bend * bend) * inner_slope


def norm_back(values, grad, gain):
    unit, rate = centred_scale(values)
    scaled = grad * gain
    mean = jnp.mean(scaled, axis=-1, keepdims=True)
    slope = jnp.mean(scaled * unit, axis=-1, keepdims=True)
    return rate * (scaled - mean - unit * slope), grad * unit


def column_sum(values):
    return jnp.sum(values, axis=0, keepdims=True)


def peers_of(dp, x):
    z, y, core = dp // 4, (dp // 2) % 2, dp % 2
    near = []
    for step in range(1, NEAR):
        flip_x, flip_y, flip_core = step % 2, (step // 2) % 2, step // 4
        other_y = y + flip_y - 2 * flip_y * y
        other_core = core + flip_core - 2 * flip_core * core
        other_x = x + flip_x - 2 * flip_x * x
        near.append((z * 4 + other_y * 2 + other_core, other_x))
    far = [(((z + step) % 4) * 4 + y * 2 + core, x) for step in range(1, 4)]
    return near, far


def text_body(
    token_ref,
    vector_ref,
    image_ref,
    live_ref,
    own_live_ref,
    scale_ref,
    joint_hbm,
    mixer_hbm,
    up_hbm,
    down_hbm,
    project_hbm,
    left_hbm,
    right_hbm,
    vector_out,
    token_out,
    joint,
    mixer,
    up,
    down,
    project,
    left,
    right,
    triple,
    residual,
    active_in,
    output,
    work,
    images,
    near_sums,
    far_sums,
    weight_sem,
    image_sem,
    near_sem,
    far_sem,
    store_sem,
):
    dp = lax.axis_index("dp")
    x = lax.axis_index("fsdp")
    z, y, core = dp // 4, (dp // 2) % 2, dp % 2
    near, far = peers_of(dp, x)
    x_peer, y_peer, core_peer = near[0], near[1], near[3]
    loads = [
        pltpu.make_async_copy(source, target, weight_sem.at[index])
        for index, (source, target) in enumerate(
            (
                (joint_hbm, joint),
                (mixer_hbm, mixer),
                (up_hbm, up),
                (down_hbm, down),
                (project_hbm, project),
            )
        )
    ]
    for load in loads:
        load.start()
    barrier = pltpu.get_barrier_semaphore()
    for peer in near + far:
        pl.semaphore_signal(barrier, inc=1, device_id=peer, device_id_type=MESH)

    def send(source, target, sems, index, peer):
        return pltpu.make_async_remote_copy(
            src_ref=source,
            dst_ref=target,
            send_sem=sems.at[0, index],
            recv_sem=sems.at[1, index],
            device_id=peer,
            device_id_type=MESH,
        )

    own_slot = images.at[core, y, x, z]
    z_sends = [send(own_slot, own_slot, image_sem, k, far[k]) for k in range(3)]
    line = images.at[core, y, x]
    y_send = send(line, line, image_sem, 3, y_peer)
    x_send = send(line, line, image_sem, 4, x_peer)
    other_line = images.at[core, 1 - y, x]
    x_again = send(other_line, other_line, image_sem, 5, x_peer)
    plane = images.at[core]
    core_send = send(plane, plane, image_sem, 6, core_peer)

    rows, width = token_ref.shape
    feed = up.shape[1]
    seqs = rows // TEXT_LEN

    def vector(index):
        return wide(jnp.concatenate([vector_ref[0, index], vector_ref[1, index]], axis=1))

    def span(index, size):
        return pl.ds(pl.multiple_of(index * size, size), size)

    gain, offset, mix_bias, feed_gain, feed_offset, down_bias, end_gain, end_offset = (
        vector(index) for index in range(8)
    )
    images[core, y, x, z] = image_ref[...]

    @pl.loop(0, rows // CHUNK)
    def _(index):
        chunk = span(index, CHUNK)
        unit, rate = centred_scale(wide(token_ref[chunk]))
        left[6, chunk] = low(unit * gain + offset)

    loads[0].wait()
    pl.semaphore_wait(barrier, 10)
    for copy in z_sends:
        copy.start()

    @pl.loop(0, 3)
    def _(index):
        cols = span(index, width)
        triple[:, cols] = low(product(left[6], joint[:, cols]))

    for copy in z_sends:
        copy.wait()
    x_send.start()
    y_send.start()

    lane = lax.broadcasted_iota(jnp.int32, (TEXT_GROUP, PAIR), 1) < HEAD_DIM
    row_seq = lax.broadcasted_iota(jnp.int32, (2 * TEXT_GROUP, TEXT_GROUP), 0)
    row_seq = jnp.where(row_seq >= TEXT_GROUP, row_seq - TEXT_GROUP, row_seq) // TEXT_LEN
    col_seq = lax.broadcasted_iota(jnp.int32, (2 * TEXT_GROUP, TEXT_GROUP), 1) // TEXT_LEN
    same = jnp.where(row_seq == col_seq, 0.0, CUT)
    pairs = width // PAIR

    def split_heads(values):
        return low(
            jnp.concatenate([jnp.where(lane, values, 0.0), jnp.where(lane, 0.0, values)], axis=0)
        )

    def join_heads(values):
        return jnp.where(lane, values[:TEXT_GROUP], values[TEXT_GROUP:])

    def head_scores(group, pair):
        query = split_heads(wide(triple[group, pl.ds(pair * PAIR, PAIR)]) * ROOT_SCALE)
        keys = triple[group, pl.ds(width + pair * PAIR, PAIR)]
        values = triple[group, pl.ds(2 * width + pair * PAIR, PAIR)]
        scores = contract_last(query, keys) + same
        return query, keys, values, jnp.exp(scores - jnp.max(scores, axis=-1, keepdims=True))

    @pl.loop(0, rows // TEXT_GROUP)
    def _(index):
        group = span(index, TEXT_GROUP)
        for pair in range(pairs):
            query, keys, values, soft = head_scores(group, pair)
            mixed = product(low(soft), jnp.concatenate([values, jnp.ones_like(values)], axis=1))
            mixed = mixed[:, :PAIR] / mixed[:, PAIR:]
            left[5, group, pl.ds(pair * PAIR, PAIR)] = low(join_heads(mixed))

    x_send.wait()
    y_send.wait()
    x_again.start()
    loads[1].wait()
    residual[...] = product(left[5], mixer[...])

    @pl.loop(0, rows // CHUNK)
    def _(index):
        chunk = span(index, CHUNK)
        values = wide(token_ref[chunk]) + residual[chunk] + mix_bias
        residual[chunk] = values
        unit, rate = centred_scale(values)
        left[4, chunk] = low(unit * feed_gain + feed_offset)

    loads[2].wait()
    for index in range(feed // width):
        cols = pl.ds(index * width, width)
        bias = jnp.concatenate(
            [vector_ref[index // 2, 8 + (index % 2) * 2 + part] for part in range(2)], axis=1
        )
        values = product(left[4], up[:, cols]) + wide(bias)
        active_in[:, cols] = values
        values = low(gelu_value(values))
        for part in range(2):
            block = index * 2 + part
            left[block % 4, :, pl.ds((block // 4) * HALF, HALF)] = values[
                :, part * HALF : (part + 1) * HALF
            ]
    x_again.wait()
    core_send.start()
    loads[3].wait()
    total = None
    for block in range(4):
        for side in range(2):
            term = product(
                left[block, :, pl.ds(side * HALF, HALF)],
                down[pl.ds(side * 2 * width + block * HALF, HALF)],
            )
            total = term if total is None else total + term
    output[...] = total

    @pl.loop(0, rows // CHUNK)
    def _(index):
        chunk = span(index, CHUNK)
        values = residual[chunk] + output[chunk] + down_bias
        output[chunk] = values
        unit, rate = centred_scale(values)
        work[span(index, 8), :] = jnp.pad(
            jnp.sum(unit.reshape(CHUNK // TEXT_LEN, TEXT_LEN, width), axis=1), ((0, 2), (0, 0))
        )

    pooled = jnp.concatenate(
        [work[index * 8 : index * 8 + CHUNK // TEXT_LEN] for index in range(rows // CHUNK)], axis=0
    )
    pooled = low(pooled * (1.0 / TEXT_LEN) * end_gain + end_offset)
    loads[4].wait()
    embedding = product(pooled, project[...])
    length_rate = lax.rsqrt(jnp.sum(embedding * embedding, axis=-1, keepdims=True) + EPSILON)
    text_unit = embedding * length_rate
    text_low = low(text_unit)
    core_send.wait()

    every = images[...].reshape(2 * 2 * 2 * 4 * SLOT_ROWS, width)
    live = live_ref[...]
    own_live = own_live_ref[...]
    temper = jnp.exp(scale_ref[...])
    live_total = jnp.sum(live, axis=1, keepdims=True)
    half_inverse = 0.5 / live_total
    cosine = contract_last(text_low, every)
    scaled = jnp.exp(temper * cosine - temper)
    row_sum = jnp.sum(scaled * live, axis=1, keepdims=True)
    near_place = x + 2 * y + 4 * core
    near_sums[near_place] = column_sum(scaled * own_live)
    near_sends = [
        send(near_sums.at[near_place], near_sums.at[near_place], near_sem, k, near[k])
        for k in range(NEAR - 1)
    ]
    for copy in near_sends:
        copy.start()
    image_own = wide(image_ref[:seqs])
    diagonal_cos = jnp.sum(wide(text_low) * image_own, axis=1, keepdims=True)
    row_part = scaled * (own_live / row_sum) * live
    for copy in near_sends:
        copy.wait()
    far_sums[z] = (
        ((near_sums[0] + near_sums[1]) + (near_sums[2] + near_sums[3]))
        + ((near_sums[4] + near_sums[5]) + (near_sums[6] + near_sums[7]))
    )
    far_sends = [
        send(far_sums.at[z], far_sums.at[z], far_sem, k, far[k]) for k in range(3)
    ]
    for copy in far_sends:
        copy.start()
    for copy in far_sends:
        copy.wait()
    columns = (far_sums[0] + far_sums[1]) + (far_sums[2] + far_sums[3])
    coupling = (row_part + scaled * own_live * (live / columns)) * half_inverse
    column_log = jnp.where(live > 0.0, temper + jnp.log(columns), 0.0)
    row_log = temper + jnp.log(row_sum)
    loss_own = column_sum(own_live * (row_log - 2.0 * temper * diagonal_cos))
    loss_shared = jnp.sum(live * column_log, axis=1, keepdims=True)
    devices = lax.axis_size("dp") * lax.axis_size("fsdp")
    loss_part = (loss_own + loss_shared * (1.0 / devices)) * half_inverse
    temper_grad = (
        jnp.sum(column_sum(coupling * cosine), axis=1, keepdims=True)
        - column_sum(own_live * diagonal_cos) / live_total
    )
    unit_grad = product(low(temper * coupling), every)
    unit_grad = unit_grad - (temper / live_total) * own_live * image_own
    embed_grad = low(
        (unit_grad - text_unit * jnp.sum(text_unit * unit_grad, axis=-1, keepdims=True))
        * length_rate
    )
    left[7] = jnp.zeros((rows, width), jnp.bfloat16)
    left[7, :SLOT_ROWS] = jnp.pad(pooled, ((0, SLOT_ROWS - seqs), (0, 0)))
    right[9] = jnp.zeros((rows, width), jnp.bfloat16)
    right[9, :SLOT_ROWS] = jnp.pad(embed_grad, ((0, SLOT_ROWS - seqs), (0, 0)))
    pooled_grad = contract_last(embed_grad, project[...]) * (1.0 / TEXT_LEN)
    for index in range(rows // CHUNK):
        work[index * 8 : index * 8 + CHUNK // TEXT_LEN] = pooled_grad[
            index * (CHUNK // TEXT_LEN) : (index + 1) * (CHUNK // TEXT_LEN)
        ]

    vector_out[...] = jnp.zeros(vector_out.shape, jnp.float32)
    column = lax.broadcasted_iota(jnp.int32, (1, width), 1)
    vector_out[12:13] = jnp.where(
        column == 0, loss_part, jnp.where(column == 1, temper * temper_grad, 0.0)
    )
    vector_out[11:12] = column_sum(pooled_grad) * float(TEXT_LEN)

    def gather(index, value):
        vector_out[index : index + 1] = vector_out[index : index + 1] + value

    @pl.loop(0, rows // CHUNK)
    def _(index):
        chunk = span(index, CHUNK)
        grad = work[span(index, 8)][: CHUNK // TEXT_LEN]
        grad = jnp.broadcast_to(
            grad[:, None, :], (CHUNK // TEXT_LEN, TEXT_LEN, width)
        ).reshape(CHUNK, width)
        value, gain_part = norm_back(output[chunk], grad, end_gain)
        output[chunk] = value
        right[0, chunk] = low(value)
        gather(10, column_sum(gain_part))
        gather(9, column_sum(value))

    stores = []

    def store(source, target):
        copy = pltpu.make_async_copy(source, target, store_sem.at[len(stores)])
        copy.start()
        stores.append(copy)

    for slab in (0, 1, 2, 3, 4, 5, 6, 7):
        store(left.at[slab], left_hbm.at[slab])
    for slab in (0, 9):
        store(right.at[slab], right_hbm.at[slab])

    for index in range(feed // width):
        cols = pl.ds(index * width, width)
        values = contract_last(right[0], down[cols]) * gelu_slope(active_in[:, cols])
        vector_out[5 + index : 6 + index] = column_sum(values)
        right[1 + index] = low(values)
        store(right.at[1 + index], right_hbm.at[1 + index])

    total = None
    for index in range(feed // width):
        term = contract_last(right[1 + index], up[:, pl.ds(index * width, width)])
        total = term if total is None else total + term
    active_in[:, :width] = total

    @pl.loop(0, rows // CHUNK)
    def _(index):
        chunk = span(index, CHUNK)
        grad = active_in[chunk, :width]
        value, gain_part = norm_back(residual[chunk], grad, feed_gain)
        value = value + output[chunk]
        output[chunk] = value
        right[5, chunk] = low(value)
        gather(3, column_sum(gain_part))
        gather(4, column_sum(grad))
        gather(2, column_sum(value))

    store(right.at[5], right_hbm.at[5])
    active_in[:, width : 2 * width] = contract_last(right[5], mixer[...])

    @pl.loop(0, rows // TEXT_GROUP)
    def _(index):
        group = span(index, TEXT_GROUP)
        for pair in range(pairs):
            cols = pl.ds(pair * PAIR, PAIR)
            query, keys, values, soft = head_scores(group, pair)
            soft = soft / jnp.sum(soft, axis=-1, keepdims=True)
            outer = split_heads(active_in[group, pl.ds(width + pair * PAIR, PAIR)])
            soft_grad = contract_last(outer, values)
            score_grad = low(
                soft * (soft_grad - jnp.sum(soft * soft_grad, axis=-1, keepdims=True))
            )
            right[6, group, cols] = low(join_heads(product(score_grad, keys)) * ROOT_SCALE)
            right[7, group, cols] = low(contract_first(score_grad, query))
            right[8, group, cols] = low(contract_first(low(soft), outer))

    for index in range(3):
        store(right.at[6 + index], right_hbm.at[6 + index])
    total = None
    for index in range(3):
        term = contract_last(right[6 + index], joint[:, pl.ds(index * width, width)])
        total = term if total is None else total + term
    active_in[:, :width] = total

    @pl.loop(0, rows // CHUNK)
    def _(index):
        chunk = span(index, CHUNK)
        grad = active_in[chunk, :width]
        value, gain_part = norm_back(wide(token_ref[chunk]), grad, gain)
        token_out[chunk] = value + output[chunk]
        gather(0, column_sum(gain_part))
        gather(1, column_sum(grad))

    for copy in stores:
        copy.wait()


def text_kernel(tokens, vectors, image_low, live, own_live, log_scale, weights):
    rows, width = tokens.shape
    joint, mixer, up, down, project = weights
    any_spec = pl.BlockSpec(memory_space=pl.ANY)
    vmem_spec = pl.BlockSpec(memory_space=pltpu.VMEM)
    dma = pltpu.SemaphoreType.DMA
    low_type = jnp.bfloat16
    padded = jnp.pad(image_low, ((0, SLOT_ROWS - image_low.shape[0]), (0, 0)))
    slots = 2 * 2 * 2 * 4 * SLOT_ROWS
    return pl.pallas_call(
        text_body,
        out_shape=(
            jax.ShapeDtypeStruct((FACTOR_A, rows, width), low_type),
            jax.ShapeDtypeStruct((FACTOR_B, rows, width), low_type),
            jax.ShapeDtypeStruct((VECTOR_ROWS, width), jnp.float32),
            jax.ShapeDtypeStruct((rows, width), jnp.float32),
        ),
        in_specs=[vmem_spec] * 6 + [any_spec] * 5,
        out_specs=(any_spec, any_spec, vmem_spec, vmem_spec),
        scratch_shapes=[pltpu.VMEM(weight.shape, low_type) for weight in weights]
        + [
            pltpu.VMEM((FACTOR_A, rows, width), low_type),
            pltpu.VMEM((FACTOR_B, rows, width), low_type),
            pltpu.VMEM((rows, 3 * width), low_type),
            pltpu.VMEM((rows, width), jnp.float32),
            pltpu.VMEM((rows, up.shape[1]), jnp.float32),
            pltpu.VMEM((rows, width), jnp.float32),
            pltpu.VMEM((rows // CHUNK * 8, width), jnp.float32),
            pltpu.VMEM((2, 2, 2, 4, SLOT_ROWS, width), low_type),
            pltpu.VMEM((NEAR, 1, slots), jnp.float32),
            pltpu.VMEM((4, 1, slots), jnp.float32),
            dma((5,)),
            dma((2, 7)),
            dma((2, NEAR - 1)),
            dma((2, 3)),
            dma((FACTOR_A + FACTOR_B,)),
        ],
        compiler_params=pltpu.CompilerParams(
            collective_id=1, has_side_effects=True, vmem_limit_bytes=62 * 1024 * 1024
        ),
    )(tokens, vectors, padded, live, own_live, log_scale.reshape(1, 1), *weights)


IMAGE_GROUP = 4
IMAGE_BLOCK = 12
IMAGE_CHUNK = 120
IMAGE_ROWS = 104
IMAGE_KEYS = 128


def image_body(
    token_ref,
    vector_ref,
    bias_ref,
    shard_vector,
    joint_hbm,
    mixer_hbm,
    up_hbm,
    down_hbm,
    project_hbm,
    joint_shard,
    mixer_shard,
    up_shard,
    down_shard,
    project_shard,
    image_out,
    vector_out,
    joint_full,
    mixer_full,
    up_full,
    down_full,
    project_full,
    joint,
    mixer,
    up,
    down,
    project,
    normed,
    triple,
    attended,
    residual,
    hidden,
    pooled,
    load_sem,
    own_sem,
    x_sem,
    y_sem,
    core_sem,
):
    dp = lax.axis_index("dp")
    x = lax.axis_index("fsdp")
    y, core = (dp // 2) % 2, dp % 2
    x_peer, y_peer, core_peer = (dp, 1 - x), (dp + 2 - 4 * y, x), (dp + 1 - 2 * core, x)
    loads = [
        pltpu.make_async_copy(source, target, load_sem.at[index])
        for index, (source, target) in enumerate(
            (
                (joint_hbm, joint),
                (mixer_hbm, mixer),
                (up_hbm, up),
                (down_hbm, down),
                (project_hbm, project),
            )
        )
    ]
    for load in loads:
        load.start()
    barrier = pltpu.get_barrier_semaphore()
    for peer in (x_peer, y_peer, core_peer):
        pl.semaphore_signal(barrier, inc=1, device_id=peer, device_id_type=MESH)
    vector_out[x] = shard_vector[...]
    pl.semaphore_wait(barrier, 3)

    def send(source, target, sems, index, peer):
        return pltpu.make_async_remote_copy(
            src_ref=source,
            dst_ref=target,
            send_sem=sems.at[0, index],
            recv_sem=sems.at[1, index],
            device_id=peer,
            device_id_type=MESH,
        )

    shards = (joint_shard, mixer_shard, up_shard, down_shard, project_shard)
    fulls = (joint_full, mixer_full, up_full, down_full, project_full)
    own_copies, x_sends, y_sends, core_sends = [], [], [], []
    for index, (shard, full) in enumerate(zip(shards, fulls)):
        half = shard.shape[0]
        quarter = half // 4
        piece = core * 2 + y

        def rows(start, size):
            return pl.ds(pl.multiple_of(start, quarter), size)

        own_copies.append(
            pltpu.make_async_copy(shard, full.at[rows(x * half, half)], own_sem.at[index])
        )
        x_sends.append(
            send(
                shard.at[rows(piece * quarter, quarter)],
                full.at[rows(x * half + piece * quarter, quarter)],
                x_sem,
                index,
                x_peer,
            )
        )
        got = full.at[rows((1 - x) * half + piece * quarter, quarter)]
        y_sends.append(send(got, got, y_sem, index, y_peer))
        pair = full.at[rows((1 - x) * half + core * 2 * quarter, 2 * quarter)]
        core_sends.append(send(pair, pair, core_sem, index, core_peer))
    x_sends.append(send(vector_out.at[x], vector_out.at[x], x_sem, 5, x_peer))
    for copy in x_sends:
        copy.start()
    for copy in own_copies:
        copy.start()

    def pass_y(index):
        x_sends[index].wait()
        y_sends[index].start()

    def pass_core(index):
        y_sends[index].wait()
        core_sends[index].start()

    blocks, rows, width = token_ref.shape
    feed = up.shape[1]
    gain, offset, mix_bias, feed_gain, feed_offset, down_bias, end_gain, end_offset = (
        wide(vector_ref[index : index + 1]) for index in range(8)
    )

    def span(index, size):
        return pl.ds(pl.multiple_of(index * size, 8), size)

    seqs = rows // IMAGE_LEN
    pool_row = lax.broadcasted_iota(jnp.int32, (seqs, rows), 0)
    pool_col = lax.broadcasted_iota(jnp.int32, (seqs, rows), 1) // IMAGE_LEN
    pool = low(jnp.where(pool_row == pool_col, 1.0, 0.0))
    group_rows = IMAGE_GROUP * IMAGE_LEN
    lane = lax.broadcasted_iota(jnp.int32, (IMAGE_ROWS, PAIR), 1) < HEAD_DIM
    seam = lax.broadcasted_iota(jnp.int32, (8, PAIR), 0) < 4
    windows = []
    for row_start, key_start in (
        (0, 0),
        (group_rows - IMAGE_ROWS, group_rows - IMAGE_KEYS),
    ):
        row = lax.broadcasted_iota(jnp.int32, (2 * IMAGE_ROWS, IMAGE_KEYS), 0)
        row = jnp.where(row >= IMAGE_ROWS, row - IMAGE_ROWS, row) + row_start
        col = lax.broadcasted_iota(jnp.int32, (2 * IMAGE_ROWS, IMAGE_KEYS), 1) + key_start
        same = jnp.where(row // IMAGE_LEN == col // IMAGE_LEN, 0.0, CUT)
        windows.append((row_start, key_start, same))

    def attend(start, pair):
        cols = pair * PAIR
        parts = []
        for row_start, key_start, same in windows:
            query = (
                wide(triple[pl.ds(start + row_start, IMAGE_ROWS), pl.ds(cols, PAIR)]) * ROOT_SCALE
            )
            keys = triple[pl.ds(start + key_start, IMAGE_KEYS), pl.ds(width + cols, PAIR)]
            values = triple[pl.ds(start + key_start, IMAGE_KEYS), pl.ds(2 * width + cols, PAIR)]
            heads = low(
                jnp.concatenate([jnp.where(lane, query, 0.0), jnp.where(lane, 0.0, query)], axis=0)
            )
            scores = contract_last(heads, keys) + same
            soft = low(jnp.exp(scores - jnp.max(scores, axis=-1, keepdims=True)))
            mixed = product(soft, jnp.concatenate([values, jnp.ones_like(values)], axis=1))
            mixed = mixed[:, :PAIR] / mixed[:, PAIR:]
            parts.append(jnp.where(lane, mixed[:IMAGE_ROWS], mixed[IMAGE_ROWS:]))
        first, second = parts
        edge = IMAGE_ROWS - 8
        attended[pl.ds(start, edge), pl.ds(cols, PAIR)] = low(first[:edge])
        attended[pl.ds(start + edge, 8), pl.ds(cols, PAIR)] = low(
            jnp.where(seam, first[edge:], second[:8])
        )
        attended[pl.ds(start + IMAGE_ROWS, edge), pl.ds(cols, PAIR)] = low(second[8:])

    @pl.loop(0, blocks)
    def _(block):
        @pl.loop(0, rows // IMAGE_CHUNK)
        def _(index):
            chunk = span(index, IMAGE_CHUNK)
            normed[chunk] = low(
                centred_scale(wide(token_ref[block, chunk]))[0] * gain + offset
            )

        @pl.when(block == 0)
        def _():
            loads[0].wait()

        @pl.when(block == 1)
        def _():
            pass_y(1)

        @pl.when(block == 2)
        def _():
            pass_y(3)

        for index in range(3):
            cols = pl.ds(index * width, width)
            triple[:, cols] = low(product(normed[...], joint[:, cols]))

        @pl.loop(0, rows // group_rows)
        def _(group):
            start = pl.multiple_of(group * group_rows, 8)
            for pair in range(width // PAIR):
                attend(start, pair)

        @pl.when(block == 0)
        def _():
            loads[1].wait()

        @pl.when(block == 1)
        def _():
            pass_y(2)
            pass_core(0)

        @pl.when(block == 2)
        def _():
            pass_y(4)
            pass_core(1)
            pass_core(2)

        residual[...] = product(attended[...], mixer[...])

        @pl.loop(0, rows // IMAGE_CHUNK)
        def _(index):
            chunk = span(index, IMAGE_CHUNK)
            values = wide(token_ref[block, chunk]) + residual[chunk] + mix_bias
            residual[chunk] = values
            normed[chunk] = low(centred_scale(values)[0] * feed_gain + feed_offset)

        @pl.when(block == 0)
        def _():
            loads[2].wait()

        for index in range(feed // width):
            cols = pl.ds(index * width, width)
            hidden[:, cols] = low(
                gelu_value(product(normed[...], up[:, cols]) + wide(bias_ref[:, cols]))
            )

        @pl.when(block == 0)
        def _():
            loads[3].wait()
            pass_y(0)

        @pl.when(block == 2)
        def _():
            pass_core(3)

        normed_sum = product(hidden[...], down[...])
        residual[...] = residual[...] + normed_sum

        @pl.loop(0, rows // IMAGE_CHUNK)
        def _(index):
            chunk = span(index, IMAGE_CHUNK)
            normed[chunk] = low(centred_scale(residual[chunk] + down_bias)[0])

        mean = product(pool, normed[...]) * (1.0 / IMAGE_LEN)
        pooled[block] = mean * end_gain + end_offset

    pass_core(4)
    loads[4].wait()
    for block in range(blocks):
        embedding = product(low(pooled[block]), project[...])
        image_out[block] = low(
            embedding
            * lax.rsqrt(jnp.sum(embedding * embedding, axis=-1, keepdims=True) + EPSILON)
        )
    for copy in core_sends + own_copies:
        copy.wait()
    x_sends[5].wait()


def image_kernel(tokens, weights, shard_vector, shards):
    (
        norm_gain,
        norm_offset,
        joint,
        mixer,
        mixer_bias,
        feed_gain,
        feed_offset,
        up,
        up_bias,
        down,
        down_bias,
        end_gain,
        end_offset,
        project,
    ) = weights
    total, width = tokens.shape
    rows = IMAGE_BLOCK * IMAGE_LEN
    blocks = total // rows
    feed = up.shape[1]
    vectors = jnp.stack(
        [
            norm_gain,
            norm_offset,
            mixer_bias,
            feed_gain,
            feed_offset,
            down_bias,
            end_gain,
            end_offset,
        ]
    )
    any_spec = pl.BlockSpec(memory_space=pl.ANY)
    vmem_spec = pl.BlockSpec(memory_space=pltpu.VMEM)
    dma = pltpu.SemaphoreType.DMA
    low_type = jnp.bfloat16
    matrices = (joint, mixer, up, down, project)
    image_out, vector_out, *fulls = pl.pallas_call(
        image_body,
        out_shape=(
            jax.ShapeDtypeStruct((blocks, IMAGE_BLOCK, width), low_type),
            jax.ShapeDtypeStruct((2, *shard_vector.shape), low_type),
            *(
                jax.ShapeDtypeStruct((2 * shard.shape[0], shard.shape[1]), low_type)
                for shard in shards
            ),
        ),
        in_specs=[vmem_spec] * 4 + [any_spec] * 10,
        out_specs=(vmem_spec, vmem_spec, *([any_spec] * 5)),
        scratch_shapes=[pltpu.VMEM(matrix.shape, low_type) for matrix in matrices]
        + [
            pltpu.VMEM((rows, width), low_type),
            pltpu.VMEM((rows, 3 * width), low_type),
            pltpu.VMEM((rows, width), low_type),
            pltpu.VMEM((rows, width), jnp.float32),
            pltpu.VMEM((rows, feed), low_type),
            pltpu.VMEM((blocks, IMAGE_BLOCK, width), jnp.float32),
            dma((5,)),
            dma((5,)),
            dma((2, 6)),
            dma((2, 5)),
            dma((2, 5)),
        ],
        compiler_params=pltpu.CompilerParams(
            collective_id=2, has_side_effects=True, vmem_limit_bytes=60 * 1024 * 1024
        ),
    )(
        tokens.reshape(blocks, rows, width),
        vectors,
        up_bias.reshape(1, feed),
        shard_vector,
        *matrices,
        *shards,
    )
    return image_out.reshape(total // IMAGE_LEN, width), vector_out, fulls


def factor_a(unit):
    return jnp.minimum(unit, 4) + jnp.clip(unit - 7, 0, 2) + jnp.maximum(unit - 11, 0)


def factor_b(unit):
    return jnp.maximum(unit - 3, 0)


def reduce_body(
    a_hbm,
    b_hbm,
    vector_ref,
    grad_hbm,
    vector_out,
    a_raw,
    a_vmem,
    b_vmem,
    core_out,
    part,
    core_in,
    x_in,
    y_in,
    end_in,
    mid_in,
    total,
    vector_core,
    vector_x,
    vector_y,
    vector_z,
    vector_sum,
    a_sem,
    b_sem,
    core_sems,
    x_sems,
    y_sems,
    end_sems,
    mid_sems,
    back_sems,
    wide_sems,
    twin_sems,
    out_sem,
    vector_sems,
):
    dp = lax.axis_index("dp")
    x = lax.axis_index("fsdp")
    z = dp // 4
    y = (dp // 2) % 2
    core = dp % 2
    at_end = (z == 0) | (z == 3)
    at_mid = (z == 1) | (z == 2)
    z_pair = z + 1 - 2 * (z % 2)
    core_peer = (dp + 1 - 2 * core, x)
    x_peer = (dp, 1 - x)
    y_peer = (dp + 2 - 4 * y, x)
    pair_peer = (z_pair * 4 + y * 2 + core, x)
    mid_peer = ((3 - z) * 4 + y * 2 + core, x)

    pltpu.make_async_copy(a_hbm.at[0], a_raw, a_sem).start()
    for slot in range(FACTOR_B):
        pltpu.make_async_copy(b_hbm.at[slot], b_vmem.at[slot], b_sem.at[slot]).start()

    barrier = pltpu.get_barrier_semaphore()
    for peer in (core_peer, x_peer, y_peer):
        pl.semaphore_signal(barrier, inc=1, device_id=peer, device_id_type=MESH)
    for step in range(1, 4):
        other = ((z + step) % 4) * 4 + y * 2 + core
        pl.semaphore_signal(barrier, inc=1, device_id=(other, x), device_id_type=MESH)
    pl.semaphore_wait(barrier, 6)

    def remote(source, target, sems, index, peer):
        return pltpu.make_async_remote_copy(
            src_ref=source,
            dst_ref=target,
            send_sem=sems.at[0, index],
            recv_sem=sems.at[1, index],
            device_id=peer,
            device_id_type=MESH,
        )

    def core_copy(step):
        return remote(core_out.at[step % 2], core_in.at[step], core_sems, step, core_peer)

    def x_copy(step):
        return remote(part.at[step, 1 - x], x_in.at[step], x_sems, step, x_peer)

    def y_copy(step):
        rows = pl.ds(pl.multiple_of((1 - y) * PART, PART), PART)
        return remote(part.at[step, x, rows], y_in.at[step], y_sems, step, y_peer)

    def own_rows():
        return pl.ds(pl.multiple_of(y * PART, PART), PART)

    def end_copy(step):
        return remote(part.at[step, x, own_rows()], end_in.at[step], end_sems, step, pair_peer)

    def mid_copy(step):
        return remote(part.at[step, x, own_rows()], mid_in.at[step], mid_sems, step, mid_peer)

    def total_rows(step):
        return pl.ds(pl.multiple_of(y * PART, PART), PART)

    def back_copy(step):
        piece = total.at[step, core, total_rows(step)]
        return remote(piece, piece, back_sems, step, pair_peer)

    def wide_copy(step):
        piece = total.at[step, core, total_rows(step)]
        return remote(piece, piece, wide_sems, step, y_peer)

    def twin_copy(step):
        piece = total.at[step, core]
        return remote(piece, piece, twin_sems, step, core_peer)

    def out_copy(step, which):
        unit = step // SUB
        offset = pl.multiple_of(which * QUARTER + (step % SUB) * ROWS, ROWS)
        return pltpu.make_async_copy(
            total.at[step, which], grad_hbm.at[unit, pl.ds(offset, ROWS)], out_sem.at[step, which]
        )

    vector_first = remote(vector_ref, vector_core, vector_sems, 0, core_peer)
    vector_second = remote(vector_sum.at[0], vector_x, vector_sems, 1, x_peer)
    vector_third = remote(vector_sum.at[1], vector_y, vector_sems, 2, y_peer)
    vector_last = []
    for step in range(1, 4):
        other = ((z + step) % 4) * 4 + y * 2 + core
        vector_last.append(
            remote(vector_sum.at[2], vector_z.at[step - 1], vector_sems, 2 + step, (other, x))
        )

    @pl.loop(0, STEPS + 8)
    def _(time):
        @pl.when((time >= 1) & (time - 1 < STEPS))
        def _():
            step = time - 1
            core_copy(step).wait()
            part[step, 1 - x] = low(wide(part[step, 1 - x]) + wide(core_in[step, 1 - x]))
            x_copy(step).start()
            part[step, x] = low(wide(part[step, x]) + wide(core_in[step, x]))

        @pl.when(time < STEPS)
        def _():
            step = time
            unit = step // SUB
            half = step % SUB
            slot_a = factor_a(unit)
            slot_b = factor_b(unit)

            @pl.when((half == 0) & ((unit < 5) | (unit == 8) | (unit == 9) | (unit == 12)))
            def _():
                pltpu.make_async_copy(a_hbm.at[slot_a], a_raw, a_sem).wait()
                a_vmem[...] = a_raw[...].T

                @pl.when(slot_a + 1 < FACTOR_A)
                def _():
                    pltpu.make_async_copy(a_hbm.at[slot_a + 1], a_raw, a_sem).start()

            @pl.when((half == 0) & ((unit == 0) | (unit >= 4)))
            def _():
                pltpu.make_async_copy(b_hbm.at[slot_b], b_vmem.at[slot_b], b_sem.at[slot_b]).wait()

            right = b_vmem[slot_b]
            for which in range(2):
                rows = pl.ds(
                    pl.multiple_of(which * HALF + (1 - core) * QUARTER + half * ROWS, ROWS), ROWS
                )
                core_out[step % 2, which] = low(product(a_vmem[rows], right))
            core_copy(step).start()
            for which in range(2):
                rows = pl.ds(
                    pl.multiple_of(which * HALF + core * QUARTER + half * ROWS, ROWS), ROWS
                )
                part[step, which] = low(product(a_vmem[rows], right))

        @pl.when((time >= 2) & (time - 2 < STEPS))
        def _():
            step = time - 2
            x_copy(step).wait()
            rows = pl.ds(pl.multiple_of((1 - y) * PART, PART), PART)
            part[step, x, rows] = low(wide(part[step, x, rows]) + wide(x_in[step, rows]))
            y_copy(step).start()
            part[step, x, own_rows()] = low(
                wide(part[step, x, own_rows()]) + wide(x_in[step, own_rows()])
            )

        @pl.when((time >= 3) & (time - 3 < STEPS))
        def _():
            step = time - 3
            y_copy(step).wait()
            part[step, x, own_rows()] = low(
                wide(part[step, x, own_rows()]) + wide(y_in[step])
            )

            @pl.when(at_end)
            def _():
                end_copy(step).start()

        @pl.when((time >= 4) & (time - 4 < STEPS))
        def _():
            step = time - 4

            @pl.when(at_end)
            def _():
                end_copy(step).wait_send()

            @pl.when(at_mid)
            def _():
                end_copy(step).wait_recv()
                part[step, x, own_rows()] = low(
                    wide(part[step, x, own_rows()]) + wide(end_in[step])
                )
                mid_copy(step).start()

        @pl.when((time >= 5) & (time - 5 < STEPS) & at_mid)
        def _():
            step = time - 5
            mid_copy(step).wait()
            total[step, core, total_rows(step)] = low(
                wide(part[step, x, own_rows()]) + wide(mid_in[step])
            )
            back_copy(step).start()
            wide_copy(step).start()

        @pl.when((time >= 6) & (time - 6 < STEPS))
        def _():
            step = time - 6

            @pl.when(at_end)
            def _():
                back_copy(step).wait_recv()
                wide_copy(step).start()

            @pl.when(at_mid)
            def _():
                back_copy(step).wait_send()

        @pl.when((time >= 7) & (time - 7 < STEPS))
        def _():
            step = time - 7
            wide_copy(step).wait()
            twin_copy(step).start()
            out_copy(step, core).start()

        @pl.when((time >= 8) & (time - 8 < STEPS))
        def _():
            step = time - 8
            twin_copy(step).wait()
            out_copy(step, 1 - core).start()

        @pl.when(time == 0)
        def _():
            vector_first.start()

        @pl.when(time == 1)
        def _():
            vector_first.wait()
            vector_sum[0] = vector_ref[...] + vector_core[...]
            vector_second.start()

        @pl.when(time == 3)
        def _():
            vector_second.wait()
            vector_sum[1] = vector_sum[0] + vector_x[...]
            vector_third.start()

        @pl.when(time == 5)
        def _():
            vector_third.wait()
            vector_sum[2] = vector_sum[1] + vector_y[...]
            for copy in vector_last:
                copy.start()

        @pl.when(time == 7)
        def _():
            for copy in vector_last:
                copy.wait()
            order = lax.broadcasted_iota(jnp.int32, (VECTOR_ROWS, WIDTH), 0) * 0 + z
            own = vector_sum[2]
            before_one = vector_z[0]
            before_two = vector_z[1]
            before_three = vector_z[2]

            def pick(where):
                shift = (order - where + 4) % 4
                return jnp.where(
                    shift == 0,
                    own,
                    jnp.where(
                        shift == 1,
                        before_one,
                        jnp.where(shift == 2, before_two, before_three),
                    ),
                )

            vector_out[...] = (pick(0) + pick(1)) + (pick(2) + pick(3))

    @pl.loop(0, STEPS)
    def _(step):
        out_copy(step, core).wait()
        out_copy(step, 1 - core).wait()


def reduce_kernel(left, right, packed):
    rows = left.shape[1]
    any_spec = pl.BlockSpec(memory_space=pl.ANY)
    vmem_spec = pl.BlockSpec(memory_space=pltpu.VMEM)
    dma = pltpu.SemaphoreType.DMA
    low_type = jnp.bfloat16
    return pl.pallas_call(
        reduce_body,
        out_shape=(
            jax.ShapeDtypeStruct((UNITS, HALF, WIDTH), low_type),
            jax.ShapeDtypeStruct((VECTOR_ROWS, WIDTH), jnp.float32),
        ),
        in_specs=[any_spec, any_spec, vmem_spec],
        out_specs=(any_spec, vmem_spec),
        scratch_shapes=[
            pltpu.VMEM((rows, WIDTH), low_type),
            pltpu.VMEM((WIDTH, rows), low_type),
            pltpu.VMEM((FACTOR_B, rows, WIDTH), low_type),
            pltpu.VMEM((2, 2, ROWS, WIDTH), low_type),
            pltpu.VMEM((STEPS, 2, ROWS, WIDTH), low_type),
            pltpu.VMEM((STEPS, 2, ROWS, WIDTH), low_type),
            pltpu.VMEM((STEPS, ROWS, WIDTH), low_type),
            pltpu.VMEM((STEPS, PART, WIDTH), low_type),
            pltpu.VMEM((STEPS, PART, WIDTH), low_type),
            pltpu.VMEM((STEPS, PART, WIDTH), low_type),
            pltpu.VMEM((STEPS, 2, ROWS, WIDTH), low_type),
            pltpu.VMEM((VECTOR_ROWS, WIDTH), jnp.float32),
            pltpu.VMEM((VECTOR_ROWS, WIDTH), jnp.float32),
            pltpu.VMEM((VECTOR_ROWS, WIDTH), jnp.float32),
            pltpu.VMEM((3, VECTOR_ROWS, WIDTH), jnp.float32),
            pltpu.VMEM((3, VECTOR_ROWS, WIDTH), jnp.float32),
            dma(()),
            dma((FACTOR_B,)),
            dma((2, STEPS)),
            dma((2, STEPS)),
            dma((2, STEPS)),
            dma((2, STEPS)),
            dma((2, STEPS)),
            dma((2, STEPS)),
            dma((2, STEPS)),
            dma((2, STEPS)),
            dma((STEPS, 2)),
            dma((2, 6)),
        ],
        compiler_params=pltpu.CompilerParams(
            collective_id=0, has_side_effects=True, vmem_limit_bytes=60 * 1024 * 1024
        ),
    )(left, right, packed)


def finish_body(grad_hbm, packed_ref, *refs):
    (
        gain,
        offset,
        joint,
        mixer,
        mix_bias,
        feed_gain,
        feed_offset,
        up,
        up_bias,
        down,
        down_bias,
        end_gain,
        end_offset,
        project,
        scale_out,
        loss_out,
        low_values,
        wide_values,
        load_sem,
        store_sem,
    ) = refs
    shard = lax.axis_index("fsdp")
    loads = [
        pltpu.make_async_copy(grad_hbm.at[unit], low_values.at[unit], load_sem.at[unit])
        for unit in range(UNITS)
    ]
    for load in loads:
        load.start()
    for row, target in (
        (0, gain),
        (1, offset),
        (2, mix_bias),
        (3, feed_gain),
        (4, feed_offset),
        (9, down_bias),
        (10, end_gain),
        (11, end_offset),
    ):
        cols = pl.ds(pl.multiple_of(shard * HALF, HALF), HALF)
        target[...] = packed_ref[pl.ds(row, 1), cols].reshape(HALF)
    for part in range(2):
        up_bias[pl.ds(part * WIDTH, WIDTH)] = packed_ref[
            pl.ds(5 + 2 * shard + part, 1), :
        ].reshape(WIDTH)
    loss_out[...] = packed_ref[12:13, 0:1]
    scale_out[...] = packed_ref[12:13, 1:2]
    places = (
        [(down, pl.ds(unit * HALF, HALF), pl.ds(0, WIDTH)) for unit in range(4)]
        + [(up, pl.ds(0, HALF), pl.ds(unit * WIDTH, WIDTH)) for unit in range(4)]
        + [(mixer, pl.ds(0, HALF), pl.ds(0, WIDTH))]
        + [(joint, pl.ds(0, HALF), pl.ds(unit * WIDTH, WIDTH)) for unit in range(3)]
        + [(project, pl.ds(0, HALF), pl.ds(0, WIDTH))]
    )
    stores = []
    for unit, (target, rows, cols) in enumerate(places):
        loads[unit].wait()
        wide_values[unit] = wide(low_values[unit])
        copy = pltpu.make_async_copy(wide_values.at[unit], target.at[rows, cols], store_sem.at[unit])
        copy.start()
        stores.append(copy)
    for copy in stores:
        copy.wait()


def finish_kernel(grads, packed):
    single = jnp.float32
    any_spec = pl.BlockSpec(memory_space=pl.ANY)
    vmem_spec = pl.BlockSpec(memory_space=pltpu.VMEM)
    vector = (jax.ShapeDtypeStruct((HALF,), single), vmem_spec)
    scalar = (jax.ShapeDtypeStruct((1, 1), single), vmem_spec)

    def matrix(rows, cols):
        return (jax.ShapeDtypeStruct((rows, cols), single), any_spec)

    outs = (
        vector,
        vector,
        matrix(HALF, 3 * WIDTH),
        matrix(HALF, WIDTH),
        vector,
        vector,
        vector,
        matrix(HALF, 4 * WIDTH),
        (jax.ShapeDtypeStruct((4 * HALF,), single), vmem_spec),
        matrix(4 * HALF, WIDTH),
        vector,
        vector,
        vector,
        matrix(HALF, WIDTH),
        scalar,
        scalar,
    )
    return pl.pallas_call(
        finish_body,
        out_shape=tuple(shape for shape, spec in outs),
        in_specs=[any_spec, vmem_spec],
        out_specs=tuple(spec for shape, spec in outs),
        scratch_shapes=[
            pltpu.VMEM((UNITS, HALF, WIDTH), jnp.bfloat16),
            pltpu.VMEM((UNITS, HALF, WIDTH), single),
            pltpu.SemaphoreType.DMA((UNITS,)),
            pltpu.SemaphoreType.DMA((UNITS,)),
        ],
        compiler_params=pltpu.CompilerParams(vmem_limit_bytes=48 * 1024 * 1024),
    )(grads, packed)


def reduce_plain(factors, vectors):
    terms = [contract_first(left, right) for left, right in factors]
    joint, mixer, upward, downward, project = terms
    gain, offset, mixbias, feedgain, feedoffset, upbias, downbias, endgain, endoffset = vectors
    ordered = (
        gain,
        offset,
        joint,
        mixer,
        mixbias,
        feedgain,
        feedoffset,
        upward,
        upbias,
        downward,
        downbias,
        endgain,
        endoffset,
        project,
    )
    shards = tuple(
        lax.psum_scatter(term, "fsdp", scatter_dimension=0, tiled=True) for term in ordered
    )
    return lax.psum(shards, "dp")


def on_device_plain(*arrays):
    (
        text_tokens,
        image_tokens,
        pair_counts,
        log_scale,
        text_gain,
        text_offset,
        text_joint,
        text_mixer,
        text_mixbias,
        text_feedgain,
        text_feedoffset,
        text_upward,
        text_upbias,
        text_downward,
        text_downbias,
        text_endgain,
        text_endoffset,
        text_project,
        image_gain,
        image_offset,
        image_joint,
        image_mixer,
        image_mixbias,
        image_feedgain,
        image_feedoffset,
        image_upward,
        image_upbias,
        image_downward,
        image_downbias,
        image_endgain,
        image_endoffset,
        image_project,
    ) = arrays
    image_weights = (
        image_gain,
        image_offset,
        image_joint,
        image_mixer,
        image_mixbias,
        image_feedgain,
        image_feedoffset,
        image_upward,
        image_upbias,
        image_downward,
        image_downbias,
        image_endgain,
        image_endoffset,
        image_project,
    )
    group_count = lax.axis_size("dp") * lax.axis_size("fsdp")
    device = lax.axis_index("dp") * lax.axis_size("fsdp") + lax.axis_index("fsdp")
    pair_total = group_count * SLOTS
    live_all = (
        (jnp.arange(SLOTS)[None, :] < pair_counts[:, None]).astype(jnp.float32).reshape(pair_total)
    )
    live_total = jnp.sum(live_all)
    text_live = lax.dynamic_slice_in_dim(live_all, device * SLOTS, SLOTS)
    temper = jnp.exp(log_scale[0])
    half_inverse = 1.0 / (2.0 * live_total)
    image_unit = forward_block(image_tokens, image_weights, IMAGE_LEN)[0]
    image_low = image_unit.astype(jnp.bfloat16)
    shard_piece = lax.all_gather(image_low, ("dp", "fsdp"), axis=0, tiled=True)
    text_weights = tuple(
        lax.all_gather(shard, "fsdp", axis=0, tiled=True)
        for shard in (
            text_gain,
            text_offset,
            text_joint,
            text_mixer,
            text_mixbias,
            text_feedgain,
            text_feedoffset,
            text_upward,
            text_upbias,
            text_downward,
            text_downbias,
            text_endgain,
            text_endoffset,
            text_project,
        )
    )
    text_unit, kept_values = forward_block(text_tokens, text_weights, TEXT_LEN)
    text_low = text_unit.astype(jnp.bfloat16)
    cosine = contract_last(text_low, shard_piece)
    scaled = jnp.exp(temper * cosine - temper)
    image_live = live_all
    forward_row_sum = jnp.sum(scaled * image_live[None, :], axis=1)
    forward_column_sum = jnp.sum(scaled * text_live[:, None], axis=0)
    column_sum = forward_column_sum
    column_sum = lax.psum(column_sum, ("dp", "fsdp"))
    diagonal_cos = jnp.sum(text_low.astype(jnp.float32) * image_low.astype(jnp.float32), axis=1)
    row_log = temper + jnp.log(forward_row_sum)
    column_log = temper + jnp.log(lax.dynamic_slice_in_dim(column_sum, device * SLOTS, SLOTS))
    diagonal = temper * diagonal_cos
    loss_part = jnp.sum(text_live * (row_log - diagonal) + text_live * (column_log - diagonal)) / (
        2.0 * live_total
    )
    coupling = (
        scaled * (text_live / forward_row_sum)[:, None] * image_live[None, :]
        + scaled * text_live[:, None] * (image_live / column_sum)[None, :]
    ) * half_inverse
    temper_grad = jnp.sum(coupling * cosine)
    unit_grad = product((temper * coupling).astype(jnp.bfloat16), shard_piece)
    unit_grad, temper_grad = (unit_grad, temper_grad)
    unit_grad = unit_grad - temper / live_total * text_live[:, None] * image_low.astype(jnp.float32)
    temper_grad = temper_grad - jnp.sum(text_live * diagonal_cos) / live_total
    loss_total, scale_total = lax.psum((loss_part, temper * temper_grad), ("dp", "fsdp"))
    factors, vectors, token_grad = backward_block(
        kept_values, text_weights, unit_grad, TEXT_LEN
    )
    final_grads = reduce_plain(factors, vectors)
    return (
        *final_grads,
        jnp.reshape(scale_total, (1,)),
        token_grad,
        jnp.reshape(loss_total, (1,)),
    )


def on_device(*arrays):
    if (lax.axis_size("dp"), lax.axis_size("fsdp")) != (16, 2):
        return on_device_plain(*arrays)
    text_tokens, image_tokens, pair_counts, log_scale = arrays[:4]
    text_weights, image_weights = arrays[4:18], arrays[18:32]
    matrix_places = (2, 3, 7, 9, 13)
    vector_places = (0, 1, 4, 5, 6, 10, 11, 12)
    shard_vector = jnp.concatenate(
        [jnp.stack([text_weights[place] for place in vector_places])]
        + [text_weights[8].reshape(4, HALF), jnp.zeros((4, HALF), jnp.bfloat16)],
        axis=0,
    ).reshape(VECTOR_ROWS, 1, HALF)
    shards = tuple(text_weights[place] for place in matrix_places)
    image_low, vectors, matrices = image_kernel(image_tokens, image_weights, shard_vector, shards)
    slots = jnp.arange(SLOT_ROWS)[None, :]
    counts = pair_counts.reshape(4, 2, 2, 2).transpose(2, 1, 3, 0).reshape(-1)
    live = ((slots < SLOTS) & (slots < counts[:, None])).astype(jnp.float32).reshape(1, -1)
    device = lax.axis_index("dp") * lax.axis_size("fsdp") + lax.axis_index("fsdp")
    own_count = lax.dynamic_index_in_dim(pair_counts, device, 0, keepdims=False)
    own_live = (jnp.arange(SLOTS) < own_count).astype(jnp.float32)[:, None]
    left, right, packed, token_grad = text_kernel(
        text_tokens, vectors, image_low, live, own_live, log_scale, matrices
    )
    grads, packed = reduce_kernel(left, right, packed)
    *final_grads, scale_total, loss_total = finish_kernel(grads, packed)
    return (*final_grads, scale_total.reshape(1), token_grad, loss_total.reshape(1))


def solution(mesh):
    return jax.shard_map(
        on_device,
        mesh=mesh,
        in_specs=(
            P(("dp", "fsdp"), None),
            P(("dp", "fsdp"), None),
            P(),
            P(),
            P("fsdp"),
            P("fsdp"),
            P("fsdp", None),
            P("fsdp", None),
            P("fsdp"),
            P("fsdp"),
            P("fsdp"),
            P("fsdp", None),
            P("fsdp"),
            P("fsdp", None),
            P("fsdp"),
            P("fsdp"),
            P("fsdp"),
            P("fsdp", None),
            P(),
            P(),
            P(),
            P(),
            P(),
            P(),
            P(),
            P(),
            P(),
            P(),
            P(),
            P(),
            P(),
            P(),
        ),
        out_specs=(
            P("fsdp"),
            P("fsdp"),
            P("fsdp", None),
            P("fsdp", None),
            P("fsdp"),
            P("fsdp"),
            P("fsdp"),
            P("fsdp", None),
            P("fsdp"),
            P("fsdp", None),
            P("fsdp"),
            P("fsdp"),
            P("fsdp"),
            P("fsdp", None),
            P(),
            P(("dp", "fsdp"), None),
            P(),
        ),
        check_vma=False,
    )
```

```python
import jax
import jax.numpy as jnp
from jax import lax
from jax.experimental import pallas as pl
from jax.experimental.pallas import tpu as pltpu
from jax.sharding import PartitionSpec as P

HEADS = 12
HEAD_DIM = 64
TEXT_LEN = 16
IMAGE_LEN = 50
SLOTS = 36


EPSILON = 1e-06


def product(left_side, right_side):
    return jnp.dot(left_side, right_side, preferred_element_type=jnp.float32)


def contract_last(left_side, right_side):
    return lax.dot_general(
        left_side, right_side, (((1,), (1,)), ((), ())), preferred_element_type=jnp.float32
    )


def contract_first(left_side, right_side):
    return lax.dot_general(
        left_side, right_side, (((0,), (0,)), ((), ())), preferred_element_type=jnp.float32
    )


def layer_norm(values, gain_vector, offset):
    centred = values - jnp.mean(values, axis=-1, keepdims=True)
    variance = jnp.mean(centred * centred, axis=-1, keepdims=True)
    return centred * lax.rsqrt(variance + EPSILON) * gain_vector.astype(
        jnp.float32
    ) + offset.astype(jnp.float32)


def normalize(embedding):
    return embedding * lax.rsqrt(jnp.sum(embedding * embedding, axis=-1, keepdims=True) + EPSILON)


def forward_block(tokens, weights, length):
    (
        norm_gain,
        norm_offset,
        joint_weight,
        mixer_weight,
        mixer_bias,
        feed_gain,
        feed_offset,
        up_weight,
        up_bias,
        down_weight,
        down_bias,
        end_gain,
        end_offset,
        projection,
    ) = weights
    inputs = tokens.astype(jnp.float32)
    total_rows, model_width = inputs.shape
    seq_count = total_rows // length
    factor = HEAD_DIM ** (-0.5)
    normed = layer_norm(inputs, norm_gain, norm_offset).astype(jnp.bfloat16)
    triple = (
        product(normed, joint_weight)
        .astype(jnp.bfloat16)
        .reshape(seq_count, length, 3, HEADS, HEAD_DIM)
    )
    queries = triple[:, :, 0]
    keyset = triple[:, :, 1]
    valueset = triple[:, :, 2]
    scores = (
        jnp.einsum("sqhd,skhd->shqk", queries, keyset, preferred_element_type=jnp.float32) * factor
    )
    soft_weights = jax.nn.softmax(scores, axis=-1)
    soft_low = soft_weights.astype(jnp.bfloat16)
    attended = jnp.einsum("shqk,skhd->sqhd", soft_low, valueset, preferred_element_type=jnp.float32)
    attended = attended.reshape(total_rows, model_width).astype(jnp.bfloat16)
    residual = inputs + product(attended, mixer_weight) + mixer_bias.astype(jnp.float32)
    normed_two = layer_norm(residual, feed_gain, feed_offset).astype(jnp.bfloat16)
    pre_active = product(normed_two, up_weight) + up_bias.astype(jnp.float32)
    active = jax.nn.gelu(pre_active).astype(jnp.bfloat16)
    output = residual + product(active, down_weight) + down_bias.astype(jnp.float32)
    final_norm = layer_norm(output, end_gain, end_offset)
    pooled = jnp.mean(final_norm.reshape(seq_count, length, model_width), axis=1)
    embedding = product(pooled.astype(jnp.bfloat16), projection)
    unit_vector = normalize(embedding)
    kept_values = (
        inputs,
        normed,
        triple,
        soft_weights,
        soft_low,
        attended,
        residual,
        normed_two,
        pre_active,
        active,
        output,
        pooled,
        embedding,
    )
    return (unit_vector, kept_values)


def backward_block(kept_values, weights, unit_grad, length):
    (
        norm_gain,
        norm_offset,
        joint_weight,
        mixer_weight,
        mixer_bias,
        feed_gain,
        feed_offset,
        up_weight,
        up_bias,
        down_weight,
        down_bias,
        end_gain,
        end_offset,
        projection,
    ) = weights
    (
        inputs,
        normed,
        triple,
        soft_weights,
        soft_low,
        attended,
        residual,
        normed_two,
        pre_active,
        active,
        output,
        pooled,
        embedding,
    ) = kept_values
    total_rows, model_width = inputs.shape
    seq_count = total_rows // length
    factor = HEAD_DIM ** (-0.5)
    unused_unit, norm_back = jax.vjp(normalize, embedding)
    embed_grad = norm_back(unit_grad)[0].astype(jnp.bfloat16)
    pooled_grad = contract_last(embed_grad, projection)
    final_grad = jnp.broadcast_to(
        pooled_grad[:, None, :] / length, (seq_count, length, model_width)
    ).reshape(total_rows, model_width)
    unused_final, end_back = jax.vjp(
        layer_norm, output, end_gain.astype(jnp.float32), end_offset.astype(jnp.float32)
    )
    output_grad, endgain_grad, endoffset_grad = end_back(final_grad)
    down_low = output_grad.astype(jnp.bfloat16)
    downbias_grad = jnp.sum(output_grad, axis=0)
    active_grad = contract_last(down_low, down_weight)
    unused_active, gelu_back = jax.vjp(jax.nn.gelu, pre_active)
    pre_grad = gelu_back(active_grad)[0]
    upbias_grad = jnp.sum(pre_grad, axis=0)
    pre_low = pre_grad.astype(jnp.bfloat16)
    normed_grad = contract_last(pre_low, up_weight)
    unused_feed, feed_back = jax.vjp(
        layer_norm, residual, feed_gain.astype(jnp.float32), feed_offset.astype(jnp.float32)
    )
    residual_part, feedgain_grad, feedoffset_grad = feed_back(normed_grad)
    residual_grad = output_grad + residual_part
    mixbias_grad = jnp.sum(residual_grad, axis=0)
    mix_low = residual_grad.astype(jnp.bfloat16)
    attended_grad = contract_last(mix_low, mixer_weight).astype(jnp.bfloat16)
    attended_grad = attended_grad.reshape(seq_count, length, HEADS, HEAD_DIM)
    queries = triple[:, :, 0]
    keyset = triple[:, :, 1]
    valueset = triple[:, :, 2]
    soft_grad = jnp.einsum(
        "sqhd,skhd->shqk", attended_grad, valueset, preferred_element_type=jnp.float32
    )
    value_grad = jnp.einsum(
        "shqk,sqhd->skhd", soft_low, attended_grad, preferred_element_type=jnp.float32
    )
    score_grad = soft_weights * (
        soft_grad - jnp.sum(soft_weights * soft_grad, axis=-1, keepdims=True)
    )
    score_grad = score_grad.astype(jnp.bfloat16)
    query_grad = (
        jnp.einsum("shqk,skhd->sqhd", score_grad, keyset, preferred_element_type=jnp.float32)
        * factor
    )
    key_grad = (
        jnp.einsum("shqk,sqhd->skhd", score_grad, queries, preferred_element_type=jnp.float32)
        * factor
    )
    triple_grad = jnp.stack([query_grad, key_grad, value_grad], axis=2)
    triple_grad = triple_grad.reshape(total_rows, 3 * model_width).astype(jnp.bfloat16)
    first_grad = contract_last(triple_grad, joint_weight)
    unused_first, first_back = jax.vjp(
        layer_norm, inputs, norm_gain.astype(jnp.float32), norm_offset.astype(jnp.float32)
    )
    input_part, gain_grad, offset_grad = first_back(first_grad)
    input_grad = residual_grad + input_part
    factors = (
        (normed, triple_grad),
        (attended, mix_low),
        (normed_two, pre_low),
        (active, down_low),
        (pooled.astype(jnp.bfloat16), embed_grad),
    )
    vectors = (
        gain_grad,
        offset_grad,
        mixbias_grad,
        feedgain_grad,
        feedoffset_grad,
        upbias_grad,
        downbias_grad,
        endgain_grad,
        endoffset_grad,
    )
    return (factors, vectors, input_grad)


WIDTH = 768
HALF = 384
QUARTER = 192
SUB = 2
ROWS = QUARTER // SUB
PART = ROWS // 2
UNITS = 13
STEPS = UNITS * SUB
TILE = 256
POOL_ROWS = 128
VECTOR_ROWS = 16
PART_RING = 8
CORE_RING = 4
RING = 6
TOTAL_RING = 4
VECTOR_START = 20
TAIL = 8
MESH = pl.DeviceIdType.MESH


ROOT_SCALE = 0.125
PAIR = 128
CUT = -1e30
TEXT_GROUP = 96
CHUNK = 96
SLOT_ROWS = 40
NEAR = 8
GELU_ROOT = 0.7978845608028654
GELU_CUBE = 0.044715


def wide(values):
    return values.astype(jnp.float32)


def low(values):
    return values.astype(jnp.bfloat16)


def centred_scale(values):
    centred = values - jnp.mean(values, axis=-1, keepdims=True)
    variance = jnp.mean(centred * centred, axis=-1, keepdims=True)
    rate = lax.rsqrt(variance + EPSILON)
    return centred * rate, rate


def gelu_value(values):
    inner = GELU_ROOT * (values + GELU_CUBE * (values * values * values))
    half = 0.5 * values
    return half + half * jnp.tanh(inner)


def gelu_slope(values):
    square = values * values
    bend = jnp.tanh(GELU_ROOT * values * (1.0 + GELU_CUBE * square))
    inner_slope = GELU_ROOT * (1.0 + (3.0 * GELU_CUBE) * square)
    return 0.5 * (1.0 + bend) + 0.5 * values * (1.0 - bend * bend) * inner_slope


def norm_back(values, grad, gain):
    unit, rate = centred_scale(values)
    scaled = grad * gain
    mean = jnp.mean(scaled, axis=-1, keepdims=True)
    slope = jnp.mean(scaled * unit, axis=-1, keepdims=True)
    return rate * (scaled - mean - unit * slope), grad * unit


def column_sum(values):
    return jnp.sum(values, axis=0, keepdims=True)


def peers_of(dp, x):
    z, y, core = dp // 4, (dp // 2) % 2, dp % 2
    near = []
    for step in range(1, NEAR):
        flip_x, flip_y, flip_core = step % 2, (step // 2) % 2, step // 4
        other_y = y + flip_y - 2 * flip_y * y
        other_core = core + flip_core - 2 * flip_core * core
        other_x = x + flip_x - 2 * flip_x * x
        near.append((z * 4 + other_y * 2 + other_core, other_x))
    far = [(((z + step) % 4) * 4 + y * 2 + core, x) for step in range(1, 4)]
    return near, far


def text_body(
    token_ref,
    vector_ref,
    image_ref,
    count_ref,
    scale_ref,
    joint_own,
    mixer_own,
    up_own,
    down_own,
    project_own,
    joint_other,
    mixer_other,
    up_other,
    down_other,
    project_other,
    grad_hbm,
    vector_out,
    token_out,
    joint,
    mixer,
    up,
    down,
    project,
    normed,
    normed_two,
    attended,
    hidden,
    pooled_rows,
    embed_rows,
    down_rows,
    mix_rows,
    pre_rows,
    triple,
    residual,
    active_in,
    output,
    work,
    bias_rows,
    images,
    near_sums,
    far_sums,
    weight_sem,
    image_sem,
    near_sem,
    far_sem,
    a_vmem,
    b_vmem,
    vector_acc,
    core_out,
    part,
    core_in,
    x_in,
    y_in,
    end_in,
    mid_in,
    total,
    vector_core,
    vector_x,
    vector_y,
    vector_z,
    vector_sum,
    core_sems,
    x_sems,
    y_sems,
    end_sems,
    mid_sems,
    back_sems,
    wide_sems,
    twin_sems,
    own_sems,
    vector_sems,
):
    dp = lax.axis_index("dp")
    x = lax.axis_index("fsdp")
    z, y, core = dp // 4, (dp // 2) % 2, dp % 2
    near, far = peers_of(dp, x)
    x_peer, y_peer, core_peer = near[0], near[1], near[3]
    loads = []
    for index, (own_half, other_half, target) in enumerate(
        (
            (joint_own, joint_other, joint),
            (mixer_own, mixer_other, mixer),
            (up_own, up_other, up),
            (down_own, down_other, down),
            (project_own, project_other, project),
        )
    ):
        half = own_half.shape[0]
        pair = []
        for side, (source, place) in enumerate(((own_half, x), (other_half, 1 - x))):
            piece = target.at[pl.ds(pl.multiple_of(place * half, half), half)]
            pair.append(pltpu.make_async_copy(source, piece, weight_sem.at[index, side]))
        loads.append(pair)
    for pair in loads:
        for load in pair:
            load.start()

    def loaded(index):
        for load in loads[index]:
            load.wait()

    barrier = pltpu.get_barrier_semaphore()
    for peer in near + far:
        pl.semaphore_signal(barrier, inc=1, device_id=peer, device_id_type=MESH)

    def send(source, target, sems, index, peer):
        return pltpu.make_async_remote_copy(
            src_ref=source,
            dst_ref=target,
            send_sem=sems.at[0, index],
            recv_sem=sems.at[1, index],
            device_id=peer,
            device_id_type=MESH,
        )

    own_slot = images.at[core, y, x, z]
    z_sends = [send(own_slot, own_slot, image_sem, k, far[k]) for k in range(3)]
    line = images.at[core, y, x]
    y_send = send(line, line, image_sem, 3, y_peer)
    x_send = send(line, line, image_sem, 4, x_peer)
    other_line = images.at[core, 1 - y, x]
    x_again = send(other_line, other_line, image_sem, 5, x_peer)
    plane = images.at[core]
    core_send = send(plane, plane, image_sem, 6, core_peer)

    rows, width = token_ref.shape
    feed = up.shape[1]
    seqs = rows // TEXT_LEN

    def vector(index):
        return wide(
            jnp.concatenate(
                [vector_ref[0, index : index + 1], vector_ref[1, index : index + 1]], axis=1
            )
        )

    def span(index, size):
        return pl.ds(pl.multiple_of(index * size, size), size)

    gain, offset, mix_bias, feed_gain, feed_offset, down_bias, end_gain, end_offset = (
        vector(index) for index in range(8)
    )
    images[core, y, x, z] = image_ref[...]
    column = lax.broadcasted_iota(jnp.int32, (1, 32 * SLOT_ROWS), 1)
    limit = jnp.zeros(column.shape, jnp.int32)
    for slot in range(32):
        slot_core, slot_y, slot_x, slot_z = slot // 16, (slot // 8) % 2, (slot // 4) % 2, slot % 4
        owner = (slot_z * 4 + slot_y * 2 + slot_core) * 2 + slot_x
        limit = jnp.where(
            (column >= slot * SLOT_ROWS) & (column < (slot + 1) * SLOT_ROWS),
            slot * SLOT_ROWS + count_ref[owner],
            limit,
        )
    live = jnp.where(column < limit, 1.0, 0.0)
    own_limit = count_ref[dp * 2 + x]
    own_live = jnp.where(
        lax.broadcasted_iota(jnp.int32, (rows // TEXT_LEN, 1), 0) < own_limit, 1.0, 0.0
    )

    @pl.loop(0, rows // CHUNK)
    def _(index):
        chunk = span(index, CHUNK)
        unit, rate = centred_scale(wide(token_ref[chunk]))
        normed[chunk] = low(unit * gain + offset)

    loaded(0)
    pl.semaphore_wait(barrier, 10)
    for copy in z_sends:
        copy.start()

    def tiles(base):
        for index in range(width // TILE):
            yield pl.ds(base + index * TILE, TILE)

    @pl.loop(0, 3)
    def _(index):
        for cols in tiles(pl.multiple_of(index * width, width)):
            triple[:, cols] = low(product(normed[...], joint[:, cols]))

    for copy in z_sends:
        copy.wait()
    x_send.start()
    y_send.start()

    lane = lax.broadcasted_iota(jnp.int32, (TEXT_GROUP, PAIR), 1) < HEAD_DIM
    row_seq = lax.broadcasted_iota(jnp.int32, (2 * TEXT_GROUP, TEXT_GROUP), 0)
    row_seq = jnp.where(row_seq >= TEXT_GROUP, row_seq - TEXT_GROUP, row_seq) // TEXT_LEN
    col_seq = lax.broadcasted_iota(jnp.int32, (2 * TEXT_GROUP, TEXT_GROUP), 1) // TEXT_LEN
    same = jnp.where(row_seq == col_seq, 0.0, CUT)
    pairs = width // PAIR

    def split_heads(values):
        return low(
            jnp.concatenate([jnp.where(lane, values, 0.0), jnp.where(lane, 0.0, values)], axis=0)
        )

    def join_heads(values):
        return jnp.where(lane, values[:TEXT_GROUP], values[TEXT_GROUP:])

    def head_scores(group, pair):
        query = split_heads(wide(triple[group, pl.ds(pair * PAIR, PAIR)]) * ROOT_SCALE)
        keys = triple[group, pl.ds(width + pair * PAIR, PAIR)]
        values = triple[group, pl.ds(2 * width + pair * PAIR, PAIR)]
        scores = contract_last(query, keys) + same
        return query, keys, values, jnp.exp(scores - jnp.max(scores, axis=-1, keepdims=True))

    @pl.loop(0, rows // TEXT_GROUP)
    def _(index):
        group = span(index, TEXT_GROUP)
        for pair in range(pairs):
            query, keys, values, soft = head_scores(group, pair)
            mixed = product(low(soft), jnp.concatenate([values, jnp.ones_like(values)], axis=1))
            mixed = mixed[:, :PAIR] / mixed[:, PAIR:]
            attended[group, pl.ds(pair * PAIR, PAIR)] = low(join_heads(mixed))

    x_send.wait()
    y_send.wait()
    x_again.start()
    loaded(1)
    for cols in tiles(0):
        residual[:, cols] = product(attended[...], mixer[:, cols])

    @pl.loop(0, rows // CHUNK)
    def _(index):
        chunk = span(index, CHUNK)
        values = wide(token_ref[chunk]) + residual[chunk] + mix_bias
        residual[chunk] = values
        unit, rate = centred_scale(values)
        normed_two[chunk] = low(unit * feed_gain + feed_offset)

    loaded(2)
    for index in range(8):
        bias_rows[0:1, index * HALF : (index + 1) * HALF] = wide(
            vector_ref[index // 4, 8 + index % 4 : 9 + index % 4]
        )

    @pl.loop(0, feed // width)
    def _(index):
        start = pl.multiple_of(index * width, width)
        for cols in tiles(start):
            values = product(normed_two[...], up[:, cols])
            values = values + bias_rows[0:1, cols]
            active_in[:, cols] = values
            hidden[:, cols] = low(gelu_value(values))

    x_again.wait()
    core_send.start()
    loaded(3)
    for cols in tiles(0):
        output[:, cols] = product(hidden[...], down[:, cols])

    @pl.loop(0, rows // CHUNK)
    def _(index):
        chunk = span(index, CHUNK)
        values = residual[chunk] + output[chunk] + down_bias
        output[chunk] = values
        unit, rate = centred_scale(values)
        work[span(index, 8), :] = jnp.pad(
            jnp.sum(unit.reshape(CHUNK // TEXT_LEN, TEXT_LEN, width), axis=1), ((0, 2), (0, 0))
        )

    pooled = jnp.concatenate(
        [work[index * 8 : index * 8 + CHUNK // TEXT_LEN] for index in range(rows // CHUNK)], axis=0
    )
    pooled = low(pooled * (1.0 / TEXT_LEN) * end_gain + end_offset)
    loaded(4)
    embedding = product(pooled, project[...])
    length_rate = lax.rsqrt(jnp.sum(embedding * embedding, axis=-1, keepdims=True) + EPSILON)
    text_unit = embedding * length_rate
    text_low = low(text_unit)
    core_send.wait()

    every = images[...].reshape(2 * 2 * 2 * 4 * SLOT_ROWS, width)
    temper = jnp.exp(jnp.full((1, 1), scale_ref[0], jnp.float32))
    live_total = jnp.sum(live, axis=1, keepdims=True)
    half_inverse = 0.5 / live_total
    cosine = contract_last(text_low, every)
    scaled = jnp.exp(temper * cosine - temper)
    row_sum = jnp.sum(scaled * live, axis=1, keepdims=True)
    near_place = x + 2 * y + 4 * core
    near_sums[near_place] = column_sum(scaled * own_live)
    near_sends = [
        send(near_sums.at[near_place], near_sums.at[near_place], near_sem, k, near[k])
        for k in range(NEAR - 1)
    ]
    for copy in near_sends:
        copy.start()
    image_own = wide(image_ref[:seqs])
    diagonal_cos = jnp.sum(wide(text_low) * image_own, axis=1, keepdims=True)
    row_part = scaled * (own_live / row_sum) * live
    for copy in near_sends:
        copy.wait()
    far_sums[z] = (
        ((near_sums[0] + near_sums[1]) + (near_sums[2] + near_sums[3]))
        + ((near_sums[4] + near_sums[5]) + (near_sums[6] + near_sums[7]))
    )
    far_sends = [
        send(far_sums.at[z], far_sums.at[z], far_sem, k, far[k]) for k in range(3)
    ]
    for copy in far_sends:
        copy.start()
    for copy in far_sends:
        copy.wait()
    columns = (far_sums[0] + far_sums[1]) + (far_sums[2] + far_sums[3])
    coupling = (row_part + scaled * own_live * (live / columns)) * half_inverse
    column_log = jnp.where(live > 0.0, temper + jnp.log(columns), 0.0)
    row_log = temper + jnp.log(row_sum)
    loss_own = column_sum(own_live * (row_log - 2.0 * temper * diagonal_cos))
    loss_shared = jnp.sum(live * column_log, axis=1, keepdims=True)
    devices = lax.axis_size("dp") * lax.axis_size("fsdp")
    loss_part = (loss_own + loss_shared * (1.0 / devices)) * half_inverse
    temper_grad = (
        jnp.sum(column_sum(coupling * cosine), axis=1, keepdims=True)
        - column_sum(own_live * diagonal_cos) / live_total
    )
    unit_grad = product(low(temper * coupling), every)
    unit_grad = unit_grad - (temper / live_total) * own_live * image_own
    embed_grad = low(
        (unit_grad - text_unit * jnp.sum(text_unit * unit_grad, axis=-1, keepdims=True))
        * length_rate
    )
    at_end = (z == 0) | (z == 3)
    at_mid = (z == 1) | (z == 2)
    pair_peer = ((z + 1 - 2 * (z % 2)) * 4 + y * 2 + core, x)
    mid_peer = ((3 - z) * 4 + y * 2 + core, x)

    def remote(source, target, sems, index, peer):
        return pltpu.make_async_remote_copy(
            src_ref=source,
            dst_ref=target,
            send_sem=sems.at[0, index],
            recv_sem=sems.at[1, index],
            device_id=peer,
            device_id_type=MESH,
        )

    def core_copy(step):
        return remote(core_out.at[step % 2], core_in.at[step % CORE_RING], core_sems, step, core_peer)

    def x_copy(step):
        return remote(part.at[step % PART_RING, 1 - x], x_in.at[step % RING], x_sems, step, x_peer)

    def y_copy(step):
        rows = pl.ds(pl.multiple_of((1 - y) * PART, PART), PART)
        return remote(part.at[step % PART_RING, x, rows], y_in.at[step % RING], y_sems, step, y_peer)

    def own_rows():
        return pl.ds(pl.multiple_of(y * PART, PART), PART)

    def end_copy(step):
        return remote(part.at[step % PART_RING, x, own_rows()], end_in.at[step % RING], end_sems, step, pair_peer)

    def mid_copy(step):
        return remote(part.at[step % PART_RING, x, own_rows()], mid_in.at[step % RING], mid_sems, step, mid_peer)

    def own_piece(step):
        return grad_hbm.at[step, core, own_rows()]

    def back_copy(step):
        return remote(total.at[step % TOTAL_RING], own_piece(step), back_sems, step, pair_peer)

    def wide_copy(step, source):
        return remote(source, own_piece(step), wide_sems, step, y_peer)

    def own_copy(step):
        return pltpu.make_async_copy(total.at[step % TOTAL_RING], own_piece(step), own_sems.at[step])

    def twin_copy(step):
        piece = grad_hbm.at[step, core]
        return remote(piece, piece, twin_sems, step, core_peer)

    vector_first = remote(vector_acc, vector_core, vector_sems, 0, core_peer)
    vector_second = remote(vector_sum.at[0], vector_x, vector_sems, 1, x_peer)
    vector_third = remote(vector_sum.at[1], vector_y, vector_sems, 2, y_peer)
    vector_last = []
    for step in range(1, 4):
        other = ((z + step) % 4) * 4 + y * 2 + core
        vector_last.append(
            remote(vector_sum.at[2], vector_z.at[step - 1], vector_sems, 2 + step, (other, x))
        )

    def tick(time):
        @pl.when((time >= 1) & (time - 1 < STEPS))
        def _():
            step = time - 1
            core_copy(step).wait()
            part[step % PART_RING, 1 - x] = low(wide(part[step % PART_RING, 1 - x]) + wide(core_in[step % CORE_RING, 1 - x]))
            x_copy(step).start()
            part[step % PART_RING, x] = low(wide(part[step % PART_RING, x]) + wide(core_in[step % CORE_RING, x]))

        @pl.when(time < STEPS)
        def _():
            step = time
            unit = step // SUB
            half = step % SUB
            fresh = half == 0

            @pl.when(fresh & (unit == 0))
            def _():
                a_vmem[...] = jnp.zeros(a_vmem.shape, jnp.bfloat16)
                a_vmem[:, :POOL_ROWS] = pooled_rows[...].T
                b_vmem[...] = jnp.zeros(b_vmem.shape, jnp.bfloat16)
                b_vmem[:POOL_ROWS] = embed_rows[...]

            @pl.when(fresh & (unit >= 1) & (unit <= 4))
            def _():
                block = unit - 1
                for side in range(2):
                    cols = pl.ds(pl.multiple_of(side * 2 * width + block * HALF, HALF), HALF)
                    a_vmem[pl.ds(side * HALF, HALF)] = hidden[:, cols].T

            @pl.when(fresh & (unit == 1))
            def _():
                b_vmem[...] = down_rows[...]

            @pl.when(fresh & (unit == 5))
            def _():
                a_vmem[...] = normed_two[...].T

            @pl.when(fresh & (unit >= 5) & (unit <= 8))
            def _():
                b_vmem[...] = pre_rows[:, span(unit - 5, width)]

            @pl.when(fresh & (unit == 9))
            def _():
                a_vmem[...] = attended[...].T
                b_vmem[...] = mix_rows[...]

            @pl.when(fresh & (unit == 10))
            def _():
                a_vmem[...] = normed[...].T

            @pl.when(fresh & (unit >= 10))
            def _():
                b_vmem[...] = triple[:, span(unit - 10, width)]

            term = b_vmem[...]
            for which in range(2):
                rows = pl.ds(
                    pl.multiple_of(which * HALF + (1 - core) * QUARTER + half * ROWS, ROWS), ROWS
                )
                core_out[step % 2, which] = low(product(a_vmem[rows], term))
            core_copy(step).start()
            for which in range(2):
                rows = pl.ds(
                    pl.multiple_of(which * HALF + core * QUARTER + half * ROWS, ROWS), ROWS
                )
                part[step % PART_RING, which] = low(product(a_vmem[rows], term))

        @pl.when((time >= 2) & (time - 2 < STEPS))
        def _():
            step = time - 2
            x_copy(step).wait()
            rows = pl.ds(pl.multiple_of((1 - y) * PART, PART), PART)
            part[step % PART_RING, x, rows] = low(wide(part[step % PART_RING, x, rows]) + wide(x_in[step % RING, rows]))
            y_copy(step).start()
            part[step % PART_RING, x, own_rows()] = low(
                wide(part[step % PART_RING, x, own_rows()]) + wide(x_in[step % RING, own_rows()])
            )

        @pl.when((time >= 3) & (time - 3 < STEPS))
        def _():
            step = time - 3
            y_copy(step).wait()
            part[step % PART_RING, x, own_rows()] = low(
                wide(part[step % PART_RING, x, own_rows()]) + wide(y_in[step % RING])
            )

            @pl.when(at_end)
            def _():
                end_copy(step).start()

        @pl.when((time >= 4) & (time - 4 < STEPS))
        def _():
            step = time - 4

            @pl.when(at_end)
            def _():
                end_copy(step).wait_send()

            @pl.when(at_mid)
            def _():
                end_copy(step).wait_recv()
                part[step % PART_RING, x, own_rows()] = low(
                    wide(part[step % PART_RING, x, own_rows()]) + wide(end_in[step % RING])
                )
                mid_copy(step).start()

        @pl.when((time >= 5) & (time - 5 < STEPS) & at_mid)
        def _():
            step = time - 5
            mid_copy(step).wait()
            total[step % TOTAL_RING] = low(
                wide(part[step % PART_RING, x, own_rows()]) + wide(mid_in[step % RING])
            )
            back_copy(step).start()
            wide_copy(step, total.at[step % TOTAL_RING]).start()
            own_copy(step).start()

        @pl.when((time >= 6) & (time - 6 < STEPS))
        def _():
            step = time - 6

            @pl.when(at_end)
            def _():
                back_copy(step).wait_recv()
                wide_copy(step, own_piece(step)).start()

            @pl.when(at_mid)
            def _():
                back_copy(step).wait_send()

        @pl.when((time >= 7) & (time - 7 < STEPS))
        def _():
            step = time - 7
            wide_copy(step, total.at[step % TOTAL_RING]).wait()

            @pl.when(at_mid)
            def _():
                own_copy(step).wait()

            twin_copy(step).start()

        @pl.when((time >= 8) & (time - 8 < STEPS))
        def _():
            step = time - 8
            twin_copy(step).wait()

        @pl.when(time == VECTOR_START + 0)
        def _():
            vector_first.start()

        @pl.when(time == VECTOR_START + 1)
        def _():
            vector_first.wait()
            vector_sum[0] = vector_acc[...] + vector_core[...]
            vector_second.start()

        @pl.when(time == VECTOR_START + 3)
        def _():
            vector_second.wait()
            vector_sum[1] = vector_sum[0] + vector_x[...]
            vector_third.start()

        @pl.when(time == VECTOR_START + 5)
        def _():
            vector_third.wait()
            vector_sum[2] = vector_sum[1] + vector_y[...]
            for copy in vector_last:
                copy.start()

        @pl.when(time == VECTOR_START + 7)
        def _():
            for copy in vector_last:
                copy.wait()
            order = lax.broadcasted_iota(jnp.int32, (VECTOR_ROWS, WIDTH), 0) * 0 + z
            own = vector_sum[2]
            before_one = vector_z[0]
            before_two = vector_z[1]
            before_three = vector_z[2]

            def pick(where):
                shift = (order - where + 4) % 4
                return jnp.where(
                    shift == 0,
                    own,
                    jnp.where(
                        shift == 1,
                        before_one,
                        jnp.where(shift == 2, before_two, before_three),
                    ),
                )

            vector_out[...] = (pick(0) + pick(1)) + (pick(2) + pick(3))

    pooled_rows[...] = jnp.zeros(pooled_rows.shape, jnp.bfloat16)
    pooled_rows[:SLOT_ROWS] = jnp.pad(pooled, ((0, SLOT_ROWS - seqs), (0, 0)))
    embed_rows[...] = jnp.zeros(embed_rows.shape, jnp.bfloat16)
    embed_rows[:SLOT_ROWS] = jnp.pad(embed_grad, ((0, SLOT_ROWS - seqs), (0, 0)))
    pooled_grad = contract_last(embed_grad, project[...]) * (1.0 / TEXT_LEN)
    pl.loop(0, 2)(tick)
    for index in range(rows // CHUNK):
        work[index * 8 : index * 8 + CHUNK // TEXT_LEN] = pooled_grad[
            index * (CHUNK // TEXT_LEN) : (index + 1) * (CHUNK // TEXT_LEN)
        ]

    vector_acc[...] = jnp.zeros(vector_acc.shape, jnp.float32)
    column = lax.broadcasted_iota(jnp.int32, (1, width), 1)
    vector_acc[12:13] = jnp.where(
        column == 0, loss_part, jnp.where(column == 1, temper * temper_grad, 0.0)
    )
    vector_acc[11:12] = column_sum(pooled_grad) * float(TEXT_LEN)

    def gather(index, value):
        vector_acc[index : index + 1] = vector_acc[index : index + 1] + value

    @pl.loop(0, rows // CHUNK)
    def _(index):
        chunk = span(index, CHUNK)
        grad = work[span(index, 8)][: CHUNK // TEXT_LEN]
        grad = jnp.broadcast_to(
            grad[:, None, :], (CHUNK // TEXT_LEN, TEXT_LEN, width)
        ).reshape(CHUNK, width)
        value, gain_part = norm_back(output[chunk], grad, end_gain)
        output[chunk] = value
        down_rows[chunk] = low(value)
        gather(10, column_sum(gain_part))
        gather(9, column_sum(value))

    @pl.loop(0, feed // width)
    def _(index):
        tick(2 + index)
        for cols in tiles(pl.multiple_of(index * width, width)):
            values = contract_last(down_rows[...], down[cols]) * gelu_slope(active_in[:, cols])
            pre_rows[:, cols] = low(values)
            bias_rows[:, cols] = jnp.sum(values.reshape(rows // 8, 8, TILE), axis=0)

    tick(6)
    for cols in tiles(0):
        active_in[:, cols] = contract_last(pre_rows[...], up[cols])
    tick(7)

    @pl.loop(0, rows // CHUNK)
    def _(index):
        chunk = span(index, CHUNK)
        grad = active_in[chunk, :width]
        value, gain_part = norm_back(residual[chunk], grad, feed_gain)
        value = value + output[chunk]
        output[chunk] = value
        mix_rows[chunk] = low(value)
        gather(3, column_sum(gain_part))
        gather(4, column_sum(grad))
        gather(2, column_sum(value))

    tick(8)
    for index in range(width // TILE):
        active_in[:, pl.ds(width + index * TILE, TILE)] = contract_last(
            mix_rows[...], mixer[pl.ds(index * TILE, TILE)]
        )
    tick(9)

    @pl.loop(0, rows // TEXT_GROUP)
    def _(index):
        tick(10 + index)
        group = span(index, TEXT_GROUP)
        for pair in range(pairs):
            cols = pl.ds(pair * PAIR, PAIR)
            query, keys, values, soft = head_scores(group, pair)
            soft = soft / jnp.sum(soft, axis=-1, keepdims=True)
            outer = split_heads(active_in[group, pl.ds(width + pair * PAIR, PAIR)])
            soft_grad = contract_last(outer, values)
            score_grad = low(
                soft * (soft_grad - jnp.sum(soft * soft_grad, axis=-1, keepdims=True))
            )
            triple[group, cols] = low(join_heads(product(score_grad, keys)) * ROOT_SCALE)
            triple[group, pl.ds(width + pair * PAIR, PAIR)] = low(contract_first(score_grad, query))
            triple[group, pl.ds(2 * width + pair * PAIR, PAIR)] = low(contract_first(low(soft), outer))

    tick(16)
    for cols in tiles(0):
        active_in[:, cols] = contract_last(triple[...], joint[cols])
    tick(17)

    @pl.loop(0, rows // CHUNK)
    def _(index):
        chunk = span(index, CHUNK)
        grad = active_in[chunk, :width]
        value, gain_part = norm_back(wide(token_ref[chunk]), grad, gain)
        token_out[chunk] = value + output[chunk]
        gather(0, column_sum(gain_part))
        gather(1, column_sum(grad))

    for index in range(feed // width):
        vector_acc[5 + index : 6 + index] = column_sum(
            bias_rows[:, index * width : (index + 1) * width]
        )
    pl.loop(18, STEPS + TAIL + 1)(tick)


def text_kernel(tokens, vectors, image_low, pair_counts, log_scale, shards, others):
    rows, width = tokens.shape
    feed = shards[2].shape[1]
    any_spec = pl.BlockSpec(memory_space=pl.ANY)
    vmem_spec = pl.BlockSpec(memory_space=pltpu.VMEM)
    dma = pltpu.SemaphoreType.DMA
    low_type = jnp.bfloat16
    smem_spec = pl.BlockSpec(memory_space=pltpu.SMEM)
    slots = 2 * 2 * 2 * 4 * SLOT_ROWS
    return pl.pallas_call(
        text_body,
        out_shape=(
            jax.ShapeDtypeStruct((STEPS, 2, ROWS, width), low_type),
            jax.ShapeDtypeStruct((VECTOR_ROWS, width), jnp.float32),
            jax.ShapeDtypeStruct((rows, width), jnp.float32),
        ),
        in_specs=[vmem_spec] * 3 + [smem_spec] * 2 + [any_spec] * 10,
        out_specs=(any_spec, vmem_spec, vmem_spec),
        scratch_shapes=[
            pltpu.VMEM((2 * shard.shape[0], shard.shape[1]), low_type) for shard in shards
        ]
        + [
            pltpu.VMEM((rows, width), low_type),
            pltpu.VMEM((rows, width), low_type),
            pltpu.VMEM((rows, width), low_type),
            pltpu.VMEM((rows, feed), low_type),
            pltpu.VMEM((POOL_ROWS, width), low_type),
            pltpu.VMEM((POOL_ROWS, width), low_type),
            pltpu.VMEM((rows, width), low_type),
            pltpu.VMEM((rows, width), low_type),
            pltpu.VMEM((rows, feed), low_type),
            pltpu.VMEM((rows, 3 * width), low_type),
            pltpu.VMEM((rows, width), jnp.float32),
            pltpu.VMEM((rows, feed), jnp.float32),
            pltpu.VMEM((rows, width), jnp.float32),
            pltpu.VMEM((rows // CHUNK * 8, width), jnp.float32),
            pltpu.VMEM((8, feed), jnp.float32),
            pltpu.VMEM((2, 2, 2, 4, SLOT_ROWS, width), low_type),
            pltpu.VMEM((NEAR, 1, slots), jnp.float32),
            pltpu.VMEM((4, 1, slots), jnp.float32),
            dma((5, 2)),
            dma((2, 7)),
            dma((2, NEAR - 1)),
            dma((2, 3)),
            pltpu.VMEM((width, rows), low_type),
            pltpu.VMEM((rows, width), low_type),
            pltpu.VMEM((VECTOR_ROWS, width), jnp.float32),
            pltpu.VMEM((2, 2, ROWS, width), low_type),
            pltpu.VMEM((PART_RING, 2, ROWS, width), low_type),
            pltpu.VMEM((CORE_RING, 2, ROWS, width), low_type),
            pltpu.VMEM((RING, ROWS, width), low_type),
            pltpu.VMEM((RING, PART, width), low_type),
            pltpu.VMEM((RING, PART, width), low_type),
            pltpu.VMEM((RING, PART, width), low_type),
            pltpu.VMEM((TOTAL_RING, PART, width), low_type),
            pltpu.VMEM((VECTOR_ROWS, width), jnp.float32),
            pltpu.VMEM((VECTOR_ROWS, width), jnp.float32),
            pltpu.VMEM((VECTOR_ROWS, width), jnp.float32),
            pltpu.VMEM((3, VECTOR_ROWS, width), jnp.float32),
            pltpu.VMEM((3, VECTOR_ROWS, width), jnp.float32),
        ]
        + [dma((2, STEPS)) for _ in range(8)]
        + [
            dma((STEPS,)),
            dma((2, 6)),
        ],
        compiler_params=pltpu.CompilerParams(
            collective_id=1, has_side_effects=True, vmem_limit_bytes=62 * 1024 * 1024
        ),
    )(tokens, vectors, image_low, pair_counts, log_scale, *shards, *others)


def pack_rows(vectors):
    index = lax.broadcasted_iota(jnp.int32, (VECTOR_ROWS, vectors[0].shape[0]), 0)
    packed = jnp.zeros(index.shape, vectors[0].dtype)
    for row, vector in enumerate(vectors):
        packed = jnp.where(index == row, vector[None, :], packed)
    return packed


IMAGE_GROUP = 4
IMAGE_BLOCK = 12
IMAGE_CHUNK = 120
IMAGE_ROWS = 104
IMAGE_KEYS = 128


def image_body(
    token_ref,
    vector_ref,
    shard_vector,
    joint_hbm,
    mixer_hbm,
    up_hbm,
    down_hbm,
    project_hbm,
    joint_shard,
    mixer_shard,
    up_shard,
    down_shard,
    project_shard,
    image_out,
    vector_out,
    joint_other,
    mixer_other,
    up_other,
    down_other,
    project_other,
    joint,
    mixer,
    up,
    down,
    project,
    normed,
    triple,
    attended,
    residual,
    hidden,
    pooled,
    load_sem,
    x_sem,
    y_sem,
    core_sem,
):
    dp = lax.axis_index("dp")
    x = lax.axis_index("fsdp")
    y, core = (dp // 2) % 2, dp % 2
    x_peer, y_peer, core_peer = (dp, 1 - x), (dp + 2 - 4 * y, x), (dp + 1 - 2 * core, x)
    loads = [
        pltpu.make_async_copy(source, target, load_sem.at[index])
        for index, (source, target) in enumerate(
            (
                (joint_hbm, joint),
                (mixer_hbm, mixer),
                (up_hbm, up),
                (down_hbm, down),
                (project_hbm, project),
            )
        )
    ]
    for load in loads:
        load.start()
    barrier = pltpu.get_barrier_semaphore()
    for peer in (x_peer, y_peer, core_peer):
        pl.semaphore_signal(barrier, inc=1, device_id=peer, device_id_type=MESH)
    vector_out[x] = shard_vector[...]
    pl.semaphore_wait(barrier, 3)

    def send(source, target, sems, index, peer):
        return pltpu.make_async_remote_copy(
            src_ref=source,
            dst_ref=target,
            send_sem=sems.at[0, index],
            recv_sem=sems.at[1, index],
            device_id=peer,
            device_id_type=MESH,
        )

    shards = (joint_shard, mixer_shard, up_shard, down_shard, project_shard)
    others = (joint_other, mixer_other, up_other, down_other, project_other)
    x_sends, y_sends, core_sends = [], [], []
    for index, (shard, other) in enumerate(zip(shards, others)):
        half = shard.shape[0]
        quarter = half // 4
        piece = core * 2 + y

        def rows(start, size):
            return pl.ds(pl.multiple_of(start, quarter), size)

        x_sends.append(
            send(
                shard.at[rows(piece * quarter, quarter)],
                other.at[rows(piece * quarter, quarter)],
                x_sem,
                index,
                x_peer,
            )
        )
        got = other.at[rows(piece * quarter, quarter)]
        y_sends.append(send(got, got, y_sem, index, y_peer))
        pair = other.at[rows(core * 2 * quarter, 2 * quarter)]
        core_sends.append(send(pair, pair, core_sem, index, core_peer))
    x_sends.append(send(vector_out.at[x], vector_out.at[x], x_sem, 5, x_peer))
    for copy in x_sends:
        copy.start()

    def pass_y(index):
        x_sends[index].wait()
        y_sends[index].start()

    def pass_core(index):
        y_sends[index].wait()
        core_sends[index].start()

    blocks, rows, width = token_ref.shape
    feed = up.shape[1]
    gain, offset, mix_bias, feed_gain, feed_offset, down_bias, end_gain, end_offset = (
        wide(vector_ref[index : index + 1]) for index in range(8)
    )

    def span(index, size):
        return pl.ds(pl.multiple_of(index * size, 8), size)

    seqs = rows // IMAGE_LEN
    pool_row = lax.broadcasted_iota(jnp.int32, (seqs, rows), 0)
    pool_col = lax.broadcasted_iota(jnp.int32, (seqs, rows), 1) // IMAGE_LEN
    pool = low(jnp.where(pool_row == pool_col, 1.0, 0.0))
    group_rows = IMAGE_GROUP * IMAGE_LEN
    lane = lax.broadcasted_iota(jnp.int32, (IMAGE_ROWS, PAIR), 1) < HEAD_DIM
    seam = lax.broadcasted_iota(jnp.int32, (8, PAIR), 0) < 4
    windows = []
    for row_start, key_start in (
        (0, 0),
        (group_rows - IMAGE_ROWS, group_rows - IMAGE_KEYS),
    ):
        row = lax.broadcasted_iota(jnp.int32, (2 * IMAGE_ROWS, IMAGE_KEYS), 0)
        row = jnp.where(row >= IMAGE_ROWS, row - IMAGE_ROWS, row) + row_start
        col = lax.broadcasted_iota(jnp.int32, (2 * IMAGE_ROWS, IMAGE_KEYS), 1) + key_start
        same = jnp.where(row // IMAGE_LEN == col // IMAGE_LEN, 0.0, CUT)
        windows.append((row_start, key_start, same))

    def attend(start, pair):
        cols = pair * PAIR
        parts = []
        for row_start, key_start, same in windows:
            query = (
                wide(triple[pl.ds(start + row_start, IMAGE_ROWS), pl.ds(cols, PAIR)]) * ROOT_SCALE
            )
            keys = triple[pl.ds(start + key_start, IMAGE_KEYS), pl.ds(width + cols, PAIR)]
            values = triple[pl.ds(start + key_start, IMAGE_KEYS), pl.ds(2 * width + cols, PAIR)]
            heads = low(
                jnp.concatenate([jnp.where(lane, query, 0.0), jnp.where(lane, 0.0, query)], axis=0)
            )
            scores = contract_last(heads, keys) + same
            soft = low(jnp.exp(scores - jnp.max(scores, axis=-1, keepdims=True)))
            mixed = product(soft, jnp.concatenate([values, jnp.ones_like(values)], axis=1))
            mixed = mixed[:, :PAIR] / mixed[:, PAIR:]
            parts.append(jnp.where(lane, mixed[:IMAGE_ROWS], mixed[IMAGE_ROWS:]))
        first, second = parts
        edge = IMAGE_ROWS - 8
        attended[pl.ds(start, edge), pl.ds(cols, PAIR)] = low(first[:edge])
        attended[pl.ds(start + edge, 8), pl.ds(cols, PAIR)] = low(
            jnp.where(seam, first[edge:], second[:8])
        )
        attended[pl.ds(start + IMAGE_ROWS, edge), pl.ds(cols, PAIR)] = low(second[8:])

    @pl.loop(0, blocks)
    def _(block):
        @pl.loop(0, rows // IMAGE_CHUNK)
        def _(index):
            chunk = span(index, IMAGE_CHUNK)
            normed[chunk] = low(
                centred_scale(wide(token_ref[block, chunk]))[0] * gain + offset
            )

        @pl.when(block == 0)
        def _():
            loads[0].wait()

        @pl.when(block == 1)
        def _():
            pass_y(1)

        @pl.when(block == 2)
        def _():
            pass_y(3)

        for index in range(3):
            cols = pl.ds(index * width, width)
            triple[:, cols] = low(product(normed[...], joint[:, cols]))

        @pl.loop(0, rows // group_rows)
        def _(group):
            start = pl.multiple_of(group * group_rows, 8)
            for pair in range(width // PAIR):
                attend(start, pair)

        @pl.when(block == 0)
        def _():
            loads[1].wait()

        @pl.when(block == 1)
        def _():
            pass_y(2)
            pass_core(0)

        @pl.when(block == 2)
        def _():
            pass_y(4)
            pass_core(1)
            pass_core(2)

        residual[...] = product(attended[...], mixer[...])

        @pl.loop(0, rows // IMAGE_CHUNK)
        def _(index):
            chunk = span(index, IMAGE_CHUNK)
            values = wide(token_ref[block, chunk]) + residual[chunk] + mix_bias
            residual[chunk] = values
            normed[chunk] = low(centred_scale(values)[0] * feed_gain + feed_offset)

        @pl.when(block == 0)
        def _():
            loads[2].wait()

        for index in range(feed // width):
            cols = pl.ds(index * width, width)
            hidden[:, cols] = low(
                gelu_value(product(normed[...], up[:, cols]) + wide(vector_ref[8 + index : 9 + index]))
            )

        @pl.when(block == 0)
        def _():
            loads[3].wait()
            pass_y(0)

        @pl.when(block == 2)
        def _():
            pass_core(3)

        normed_sum = product(hidden[...], down[...])
        residual[...] = residual[...] + normed_sum

        @pl.loop(0, rows // IMAGE_CHUNK)
        def _(index):
            chunk = span(index, IMAGE_CHUNK)
            normed[chunk] = low(centred_scale(residual[chunk] + down_bias)[0])

        mean = product(pool, normed[...]) * (1.0 / IMAGE_LEN)
        pooled[block] = mean * end_gain + end_offset

    pass_core(4)
    loads[4].wait()
    rest = jnp.zeros((SLOT_ROWS - blocks * IMAGE_BLOCK, width), jnp.float32)
    means = jnp.concatenate([pooled[block] for block in range(blocks)] + [rest], axis=0)
    embedding = product(low(means), project[...])
    image_out[...] = low(
        embedding * lax.rsqrt(jnp.sum(embedding * embedding, axis=-1, keepdims=True) + EPSILON)
    )
    for copy in core_sends:
        copy.wait()
    x_sends[5].wait()


def image_kernel(tokens, weights, shard_vector, shards):
    (
        norm_gain,
        norm_offset,
        joint,
        mixer,
        mixer_bias,
        feed_gain,
        feed_offset,
        up,
        up_bias,
        down,
        down_bias,
        end_gain,
        end_offset,
        project,
    ) = weights
    total, width = tokens.shape
    rows = IMAGE_BLOCK * IMAGE_LEN
    blocks = total // rows
    feed = up.shape[1]
    vectors = pack_rows(
        [
            norm_gain,
            norm_offset,
            mixer_bias,
            feed_gain,
            feed_offset,
            down_bias,
            end_gain,
            end_offset,
        ]
        + [up_bias[start : start + width] for start in range(0, feed, width)],
    )
    any_spec = pl.BlockSpec(memory_space=pl.ANY)
    vmem_spec = pl.BlockSpec(memory_space=pltpu.VMEM)
    dma = pltpu.SemaphoreType.DMA
    low_type = jnp.bfloat16
    matrices = (joint, mixer, up, down, project)
    image_out, vector_out, *others = pl.pallas_call(
        image_body,
        out_shape=(
            jax.ShapeDtypeStruct((SLOT_ROWS, width), low_type),
            jax.ShapeDtypeStruct((2, *shard_vector.shape), low_type),
            *(
                jax.ShapeDtypeStruct(shard.shape, low_type)
                for shard in shards
            ),
        ),
        in_specs=[vmem_spec] * 3 + [any_spec] * 10,
        out_specs=(vmem_spec, vmem_spec, *([any_spec] * 5)),
        scratch_shapes=[pltpu.VMEM(matrix.shape, low_type) for matrix in matrices]
        + [
            pltpu.VMEM((rows, width), low_type),
            pltpu.VMEM((rows, 3 * width), low_type),
            pltpu.VMEM((rows, width), low_type),
            pltpu.VMEM((rows, width), jnp.float32),
            pltpu.VMEM((rows, feed), low_type),
            pltpu.VMEM((blocks, IMAGE_BLOCK, width), jnp.float32),
            dma((5,)),
            dma((2, 6)),
            dma((2, 5)),
            dma((2, 5)),
        ],
        compiler_params=pltpu.CompilerParams(
            collective_id=2, has_side_effects=True, vmem_limit_bytes=60 * 1024 * 1024
        ),
    )(
        tokens.reshape(blocks, rows, width),
        vectors,
        shard_vector,
        *matrices,
        *shards,
    )
    return image_out, vector_out, others


def finish_body(grad_hbm, packed_ref, *refs):
    (
        gain,
        offset,
        joint,
        mixer,
        mix_bias,
        feed_gain,
        feed_offset,
        up,
        up_bias,
        down,
        down_bias,
        end_gain,
        end_offset,
        project,
        scale_out,
        loss_out,
        low_values,
        wide_values,
        load_sem,
        store_sem,
    ) = refs
    shard = lax.axis_index("fsdp")
    loads = [
        pltpu.make_async_copy(
            grad_hbm.at[pl.ds(unit * SUB, SUB)],
            low_values.at[pl.ds(unit * SUB, SUB)],
            load_sem.at[unit],
        )
        for unit in range(UNITS)
    ]
    for load in loads:
        load.start()
    for row, target in (
        (0, gain),
        (1, offset),
        (2, mix_bias),
        (3, feed_gain),
        (4, feed_offset),
        (9, down_bias),
        (10, end_gain),
        (11, end_offset),
    ):
        cols = pl.ds(pl.multiple_of(shard * HALF, HALF), HALF)
        target[...] = packed_ref[pl.ds(row, 1), cols].reshape(HALF)
    for part in range(2):
        up_bias[pl.ds(part * WIDTH, WIDTH)] = packed_ref[
            pl.ds(5 + 2 * shard + part, 1), :
        ].reshape(WIDTH)
    loss_out[...] = packed_ref[12:13, 0:1]
    scale_out[...] = packed_ref[12:13, 1:2]
    places = (
        [(project, pl.ds(0, HALF), pl.ds(0, WIDTH))]
        + [(down, pl.ds(unit * HALF, HALF), pl.ds(0, WIDTH)) for unit in range(4)]
        + [(up, pl.ds(0, HALF), pl.ds(unit * WIDTH, WIDTH)) for unit in range(4)]
        + [(mixer, pl.ds(0, HALF), pl.ds(0, WIDTH))]
        + [(joint, pl.ds(0, HALF), pl.ds(unit * WIDTH, WIDTH)) for unit in range(3)]
    )
    stores = []
    for unit, (target, rows, cols) in enumerate(places):
        loads[unit].wait()
        for core in range(2):
            for half in range(SUB):
                rows_here = pl.ds(core * QUARTER + half * ROWS, ROWS)
                wide_values[unit, rows_here] = wide(low_values[unit * SUB + half, core])
        copy = pltpu.make_async_copy(wide_values.at[unit], target.at[rows, cols], store_sem.at[unit])
        copy.start()
        stores.append(copy)
    for copy in stores:
        copy.wait()


def finish_kernel(grads, packed):
    single = jnp.float32
    any_spec = pl.BlockSpec(memory_space=pl.ANY)
    vmem_spec = pl.BlockSpec(memory_space=pltpu.VMEM)
    vector = (jax.ShapeDtypeStruct((HALF,), single), vmem_spec)
    scalar = (jax.ShapeDtypeStruct((1, 1), single), vmem_spec)

    def matrix(rows, cols):
        return (jax.ShapeDtypeStruct((rows, cols), single), any_spec)

    outs = (
        vector,
        vector,
        matrix(HALF, 3 * WIDTH),
        matrix(HALF, WIDTH),
        vector,
        vector,
        vector,
        matrix(HALF, 4 * WIDTH),
        (jax.ShapeDtypeStruct((4 * HALF,), single), vmem_spec),
        matrix(4 * HALF, WIDTH),
        vector,
        vector,
        vector,
        matrix(HALF, WIDTH),
        scalar,
        scalar,
    )
    return pl.pallas_call(
        finish_body,
        out_shape=tuple(shape for shape, spec in outs),
        in_specs=[any_spec, vmem_spec],
        out_specs=tuple(spec for shape, spec in outs),
        scratch_shapes=[
            pltpu.VMEM((STEPS, 2, ROWS, WIDTH), jnp.bfloat16),
            pltpu.VMEM((UNITS, HALF, WIDTH), single),
            pltpu.SemaphoreType.DMA((UNITS,)),
            pltpu.SemaphoreType.DMA((UNITS,)),
        ],
        compiler_params=pltpu.CompilerParams(vmem_limit_bytes=48 * 1024 * 1024),
    )(grads, packed)


def reduce_plain(factors, vectors):
    terms = [contract_first(left, right) for left, right in factors]
    joint, mixer, upward, downward, project = terms
    gain, offset, mixbias, feedgain, feedoffset, upbias, downbias, endgain, endoffset = vectors
    ordered = (
        gain,
        offset,
        joint,
        mixer,
        mixbias,
        feedgain,
        feedoffset,
        upward,
        upbias,
        downward,
        downbias,
        endgain,
        endoffset,
        project,
    )
    shards = tuple(
        lax.psum_scatter(term, "fsdp", scatter_dimension=0, tiled=True) for term in ordered
    )
    return lax.psum(shards, "dp")


def on_device_plain(*arrays):
    (
        text_tokens,
        image_tokens,
        pair_counts,
        log_scale,
        text_gain,
        text_offset,
        text_joint,
        text_mixer,
        text_mixbias,
        text_feedgain,
        text_feedoffset,
        text_upward,
        text_upbias,
        text_downward,
        text_downbias,
        text_endgain,
        text_endoffset,
        text_project,
        image_gain,
        image_offset,
        image_joint,
        image_mixer,
        image_mixbias,
        image_feedgain,
        image_feedoffset,
        image_upward,
        image_upbias,
        image_downward,
        image_downbias,
        image_endgain,
        image_endoffset,
        image_project,
    ) = arrays
    image_weights = (
        image_gain,
        image_offset,
        image_joint,
        image_mixer,
        image_mixbias,
        image_feedgain,
        image_feedoffset,
        image_upward,
        image_upbias,
        image_downward,
        image_downbias,
        image_endgain,
        image_endoffset,
        image_project,
    )
    group_count = lax.axis_size("dp") * lax.axis_size("fsdp")
    device = lax.axis_index("dp") * lax.axis_size("fsdp") + lax.axis_index("fsdp")
    pair_total = group_count * SLOTS
    live_all = (
        (jnp.arange(SLOTS)[None, :] < pair_counts[:, None]).astype(jnp.float32).reshape(pair_total)
    )
    live_total = jnp.sum(live_all)
    text_live = lax.dynamic_slice_in_dim(live_all, device * SLOTS, SLOTS)
    temper = jnp.exp(log_scale[0])
    half_inverse = 1.0 / (2.0 * live_total)
    image_unit = forward_block(image_tokens, image_weights, IMAGE_LEN)[0]
    image_low = image_unit.astype(jnp.bfloat16)
    shard_piece = lax.all_gather(image_low, ("dp", "fsdp"), axis=0, tiled=True)
    text_weights = tuple(
        lax.all_gather(shard, "fsdp", axis=0, tiled=True)
        for shard in (
            text_gain,
            text_offset,
            text_joint,
            text_mixer,
            text_mixbias,
            text_feedgain,
            text_feedoffset,
            text_upward,
            text_upbias,
            text_downward,
            text_downbias,
            text_endgain,
            text_endoffset,
            text_project,
        )
    )
    text_unit, kept_values = forward_block(text_tokens, text_weights, TEXT_LEN)
    text_low = text_unit.astype(jnp.bfloat16)
    cosine = contract_last(text_low, shard_piece)
    scaled = jnp.exp(temper * cosine - temper)
    image_live = live_all
    forward_row_sum = jnp.sum(scaled * image_live[None, :], axis=1)
    forward_column_sum = jnp.sum(scaled * text_live[:, None], axis=0)
    column_sum = forward_column_sum
    column_sum = lax.psum(column_sum, ("dp", "fsdp"))
    diagonal_cos = jnp.sum(text_low.astype(jnp.float32) * image_low.astype(jnp.float32), axis=1)
    row_log = temper + jnp.log(forward_row_sum)
    column_log = temper + jnp.log(lax.dynamic_slice_in_dim(column_sum, device * SLOTS, SLOTS))
    diagonal = temper * diagonal_cos
    loss_part = jnp.sum(text_live * (row_log - diagonal) + text_live * (column_log - diagonal)) / (
        2.0 * live_total
    )
    coupling = (
        scaled * (text_live / forward_row_sum)[:, None] * image_live[None, :]
        + scaled * text_live[:, None] * (image_live / column_sum)[None, :]
    ) * half_inverse
    temper_grad = jnp.sum(coupling * cosine)
    unit_grad = product((temper * coupling).astype(jnp.bfloat16), shard_piece)
    unit_grad, temper_grad = (unit_grad, temper_grad)
    unit_grad = unit_grad - temper / live_total * text_live[:, None] * image_low.astype(jnp.float32)
    temper_grad = temper_grad - jnp.sum(text_live * diagonal_cos) / live_total
    loss_total, scale_total = lax.psum((loss_part, temper * temper_grad), ("dp", "fsdp"))
    factors, vectors, token_grad = backward_block(
        kept_values, text_weights, unit_grad, TEXT_LEN
    )
    final_grads = reduce_plain(factors, vectors)
    return (
        *final_grads,
        jnp.reshape(scale_total, (1,)),
        token_grad,
        jnp.reshape(loss_total, (1,)),
    )


def on_device(*arrays):
    if (lax.axis_size("dp"), lax.axis_size("fsdp")) != (16, 2):
        return on_device_plain(*arrays)
    text_tokens, image_tokens, pair_counts, log_scale = arrays[:4]
    text_weights, image_weights = arrays[4:18], arrays[18:32]
    matrix_places = (2, 3, 7, 9, 13)
    vector_places = (0, 1, 4, 5, 6, 10, 11, 12)
    shard_vector = pack_rows(
        [text_weights[place] for place in vector_places]
        + [text_weights[8][start : start + HALF] for start in range(0, 4 * HALF, HALF)]
    )
    shards = tuple(text_weights[place] for place in matrix_places)
    image_low, vectors, others = image_kernel(image_tokens, image_weights, shard_vector, shards)
    grads, packed, token_grad = text_kernel(
        text_tokens, vectors, image_low, pair_counts, log_scale, shards, others
    )
    *final_grads, scale_total, loss_total = finish_kernel(grads, packed)
    return (*final_grads, scale_total.reshape(1), token_grad, loss_total.reshape(1))


def solution(mesh):
    return jax.shard_map(
        on_device,
        mesh=mesh,
        in_specs=(
            P(("dp", "fsdp"), None),
            P(("dp", "fsdp"), None),
            P(),
            P(),
            P("fsdp"),
            P("fsdp"),
            P("fsdp", None),
            P("fsdp", None),
            P("fsdp"),
            P("fsdp"),
            P("fsdp"),
            P("fsdp", None),
            P("fsdp"),
            P("fsdp", None),
            P("fsdp"),
            P("fsdp"),
            P("fsdp"),
            P("fsdp", None),
            P(),
            P(),
            P(),
            P(),
            P(),
            P(),
            P(),
            P(),
            P(),
            P(),
            P(),
            P(),
            P(),
            P(),
        ),
        out_specs=(
            P("fsdp"),
            P("fsdp"),
            P("fsdp", None),
            P("fsdp", None),
            P("fsdp"),
            P("fsdp"),
            P("fsdp"),
            P("fsdp", None),
            P("fsdp"),
            P("fsdp", None),
            P("fsdp"),
            P("fsdp"),
            P("fsdp"),
            P("fsdp", None),
            P(),
            P(("dp", "fsdp"), None),
            P(),
        ),
        check_vma=False,
    )
```

```python
import jax
import jax.numpy as jnp
from jax import lax
from jax.experimental import pallas as pl
from jax.experimental.pallas import tpu as pltpu
from jax.sharding import PartitionSpec as P

HEADS = 12
HEAD_DIM = 64
TEXT_LEN = 16
IMAGE_LEN = 50
SLOTS = 36


EPSILON = 1e-06


def product(left_side, right_side):
    return jnp.dot(left_side, right_side, preferred_element_type=jnp.float32)


def contract_last(left_side, right_side):
    return lax.dot_general(
        left_side, right_side, (((1,), (1,)), ((), ())), preferred_element_type=jnp.float32
    )


def contract_first(left_side, right_side):
    return lax.dot_general(
        left_side, right_side, (((0,), (0,)), ((), ())), preferred_element_type=jnp.float32
    )


def layer_norm(values, gain_vector, offset):
    centred = values - jnp.mean(values, axis=-1, keepdims=True)
    variance = jnp.mean(centred * centred, axis=-1, keepdims=True)
    return centred * lax.rsqrt(variance + EPSILON) * gain_vector.astype(
        jnp.float32
    ) + offset.astype(jnp.float32)


def normalize(embedding):
    return embedding * lax.rsqrt(jnp.sum(embedding * embedding, axis=-1, keepdims=True) + EPSILON)


def forward_block(tokens, weights, length):
    (
        norm_gain,
        norm_offset,
        joint_weight,
        mixer_weight,
        mixer_bias,
        feed_gain,
        feed_offset,
        up_weight,
        up_bias,
        down_weight,
        down_bias,
        end_gain,
        end_offset,
        projection,
    ) = weights
    inputs = tokens.astype(jnp.float32)
    total_rows, model_width = inputs.shape
    seq_count = total_rows // length
    factor = HEAD_DIM ** (-0.5)
    normed = layer_norm(inputs, norm_gain, norm_offset).astype(jnp.bfloat16)
    triple = (
        product(normed, joint_weight)
        .astype(jnp.bfloat16)
        .reshape(seq_count, length, 3, HEADS, HEAD_DIM)
    )
    queries = triple[:, :, 0]
    keyset = triple[:, :, 1]
    valueset = triple[:, :, 2]
    scores = (
        jnp.einsum("sqhd,skhd->shqk", queries, keyset, preferred_element_type=jnp.float32) * factor
    )
    soft_weights = jax.nn.softmax(scores, axis=-1)
    soft_low = soft_weights.astype(jnp.bfloat16)
    attended = jnp.einsum("shqk,skhd->sqhd", soft_low, valueset, preferred_element_type=jnp.float32)
    attended = attended.reshape(total_rows, model_width).astype(jnp.bfloat16)
    residual = inputs + product(attended, mixer_weight) + mixer_bias.astype(jnp.float32)
    normed_two = layer_norm(residual, feed_gain, feed_offset).astype(jnp.bfloat16)
    pre_active = product(normed_two, up_weight) + up_bias.astype(jnp.float32)
    active = jax.nn.gelu(pre_active).astype(jnp.bfloat16)
    output = residual + product(active, down_weight) + down_bias.astype(jnp.float32)
    final_norm = layer_norm(output, end_gain, end_offset)
    pooled = jnp.mean(final_norm.reshape(seq_count, length, model_width), axis=1)
    embedding = product(pooled.astype(jnp.bfloat16), projection)
    unit_vector = normalize(embedding)
    kept_values = (
        inputs,
        normed,
        triple,
        soft_weights,
        soft_low,
        attended,
        residual,
        normed_two,
        pre_active,
        active,
        output,
        pooled,
        embedding,
    )
    return (unit_vector, kept_values)


def backward_block(kept_values, weights, unit_grad, length):
    (
        norm_gain,
        norm_offset,
        joint_weight,
        mixer_weight,
        mixer_bias,
        feed_gain,
        feed_offset,
        up_weight,
        up_bias,
        down_weight,
        down_bias,
        end_gain,
        end_offset,
        projection,
    ) = weights
    (
        inputs,
        normed,
        triple,
        soft_weights,
        soft_low,
        attended,
        residual,
        normed_two,
        pre_active,
        active,
        output,
        pooled,
        embedding,
    ) = kept_values
    total_rows, model_width = inputs.shape
    seq_count = total_rows // length
    factor = HEAD_DIM ** (-0.5)
    unused_unit, norm_back = jax.vjp(normalize, embedding)
    embed_grad = norm_back(unit_grad)[0].astype(jnp.bfloat16)
    pooled_grad = contract_last(embed_grad, projection)
    final_grad = jnp.broadcast_to(
        pooled_grad[:, None, :] / length, (seq_count, length, model_width)
    ).reshape(total_rows, model_width)
    unused_final, end_back = jax.vjp(
        layer_norm, output, end_gain.astype(jnp.float32), end_offset.astype(jnp.float32)
    )
    output_grad, endgain_grad, endoffset_grad = end_back(final_grad)
    down_low = output_grad.astype(jnp.bfloat16)
    downbias_grad = jnp.sum(output_grad, axis=0)
    active_grad = contract_last(down_low, down_weight)
    unused_active, gelu_back = jax.vjp(jax.nn.gelu, pre_active)
    pre_grad = gelu_back(active_grad)[0]
    upbias_grad = jnp.sum(pre_grad, axis=0)
    pre_low = pre_grad.astype(jnp.bfloat16)
    normed_grad = contract_last(pre_low, up_weight)
    unused_feed, feed_back = jax.vjp(
        layer_norm, residual, feed_gain.astype(jnp.float32), feed_offset.astype(jnp.float32)
    )
    residual_part, feedgain_grad, feedoffset_grad = feed_back(normed_grad)
    residual_grad = output_grad + residual_part
    mixbias_grad = jnp.sum(residual_grad, axis=0)
    mix_low = residual_grad.astype(jnp.bfloat16)
    attended_grad = contract_last(mix_low, mixer_weight).astype(jnp.bfloat16)
    attended_grad = attended_grad.reshape(seq_count, length, HEADS, HEAD_DIM)
    queries = triple[:, :, 0]
    keyset = triple[:, :, 1]
    valueset = triple[:, :, 2]
    soft_grad = jnp.einsum(
        "sqhd,skhd->shqk", attended_grad, valueset, preferred_element_type=jnp.float32
    )
    value_grad = jnp.einsum(
        "shqk,sqhd->skhd", soft_low, attended_grad, preferred_element_type=jnp.float32
    )
    score_grad = soft_weights * (
        soft_grad - jnp.sum(soft_weights * soft_grad, axis=-1, keepdims=True)
    )
    score_grad = score_grad.astype(jnp.bfloat16)
    query_grad = (
        jnp.einsum("shqk,skhd->sqhd", score_grad, keyset, preferred_element_type=jnp.float32)
        * factor
    )
    key_grad = (
        jnp.einsum("shqk,sqhd->skhd", score_grad, queries, preferred_element_type=jnp.float32)
        * factor
    )
    triple_grad = jnp.stack([query_grad, key_grad, value_grad], axis=2)
    triple_grad = triple_grad.reshape(total_rows, 3 * model_width).astype(jnp.bfloat16)
    first_grad = contract_last(triple_grad, joint_weight)
    unused_first, first_back = jax.vjp(
        layer_norm, inputs, norm_gain.astype(jnp.float32), norm_offset.astype(jnp.float32)
    )
    input_part, gain_grad, offset_grad = first_back(first_grad)
    input_grad = residual_grad + input_part
    factors = (
        (normed, triple_grad),
        (attended, mix_low),
        (normed_two, pre_low),
        (active, down_low),
        (pooled.astype(jnp.bfloat16), embed_grad),
    )
    vectors = (
        gain_grad,
        offset_grad,
        mixbias_grad,
        feedgain_grad,
        feedoffset_grad,
        upbias_grad,
        downbias_grad,
        endgain_grad,
        endoffset_grad,
    )
    return (factors, vectors, input_grad)


WIDTH = 768
HALF = 384
QUARTER = 192
SUB = 2
ROWS = QUARTER // SUB
PART = ROWS // 2
UNITS = 13
STEPS = UNITS * SUB
TILE = 256
POOL_ROWS = 128
VECTOR_ROWS = 16
PART_RING = 8
CORE_RING = 4
RING = 8
TOTAL_RING = 6
VECTOR_START = 20
TAIL = 9
MESH = pl.DeviceIdType.MESH


ROOT_SCALE = 0.125
PAIR = 128
CUT = -1e30
TEXT_GROUP = 128
CHUNK = 96
SLOT_ROWS = 40
NEAR = 8
GELU_ROOT = 0.7978845608028654
GELU_CUBE = 0.044715


def wide(values):
    return values.astype(jnp.float32)


def low(values):
    return values.astype(jnp.bfloat16)


def centred_scale(values):
    centred = values - jnp.mean(values, axis=-1, keepdims=True)
    variance = jnp.mean(centred * centred, axis=-1, keepdims=True)
    rate = lax.rsqrt(variance + EPSILON)
    return centred * rate, rate


def gelu_value(values):
    inner = GELU_ROOT * (values + GELU_CUBE * (values * values * values))
    half = 0.5 * values
    return half + half * jnp.tanh(inner)


def gelu_slope(values):
    square = values * values
    bend = jnp.tanh(GELU_ROOT * values * (1.0 + GELU_CUBE * square))
    inner_slope = GELU_ROOT * (1.0 + (3.0 * GELU_CUBE) * square)
    return 0.5 * (1.0 + bend) + 0.5 * values * (1.0 - bend * bend) * inner_slope


def norm_back(values, grad, gain):
    unit, rate = centred_scale(values)
    scaled = grad * gain
    mean = jnp.mean(scaled, axis=-1, keepdims=True)
    slope = jnp.mean(scaled * unit, axis=-1, keepdims=True)
    return rate * (scaled - mean - unit * slope), grad * unit


def column_sum(values):
    return jnp.sum(values, axis=0, keepdims=True)


def peers_of(dp, x):
    z, y, core = dp // 4, (dp // 2) % 2, dp % 2
    near = []
    for step in range(1, NEAR):
        flip_x, flip_y, flip_core = step % 2, (step // 2) % 2, step // 4
        other_y = y + flip_y - 2 * flip_y * y
        other_core = core + flip_core - 2 * flip_core * core
        other_x = x + flip_x - 2 * flip_x * x
        near.append((z * 4 + other_y * 2 + other_core, other_x))
    far = [(((z + step) % 4) * 4 + y * 2 + core, x) for step in range(1, 4)]
    return near, far


def text_body(
    token_ref,
    vector_ref,
    image_ref,
    count_ref,
    scale_ref,
    joint_own,
    mixer_own,
    up_own,
    down_own,
    project_own,
    joint_other,
    mixer_other,
    up_other,
    down_other,
    project_other,
    grad_hbm,
    vector_out,
    token_out,
    joint,
    mixer,
    up,
    down,
    project,
    normed,
    normed_two,
    attended,
    hidden,
    pooled_rows,
    embed_rows,
    down_rows,
    mix_rows,
    pre_rows,
    triple,
    residual,
    active_in,
    output,
    work,
    bias_rows,
    images,
    near_sums,
    far_sums,
    weight_sem,
    image_sem,
    near_sem,
    far_sem,
    a_vmem,
    b_vmem,
    vector_acc,
    core_out,
    part,
    core_in,
    x_in,
    y_in,
    end_in,
    mid_in,
    total,
    vector_core,
    vector_x,
    vector_y,
    vector_z,
    vector_sum,
    core_sems,
    x_sems,
    y_sems,
    end_sems,
    mid_sems,
    back_sems,
    wide_sems,
    twin_sems,
    own_sems,
    vector_sems,
):
    dp = lax.axis_index("dp")
    x = lax.axis_index("fsdp")
    z, y, core = dp // 4, (dp // 2) % 2, dp % 2
    near, far = peers_of(dp, x)
    x_peer, y_peer, core_peer = near[0], near[1], near[3]
    loads = []
    for index, (own_half, other_half, target) in enumerate(
        (
            (joint_own, joint_other, joint),
            (mixer_own, mixer_other, mixer),
            (up_own, up_other, up),
            (down_own, down_other, down),
            (project_own, project_other, project),
        )
    ):
        half = own_half.shape[0]
        pair = []
        for side, (source, place) in enumerate(((own_half, x), (other_half, 1 - x))):
            piece = target.at[pl.ds(pl.multiple_of(place * half, half), half)]
            pair.append(pltpu.make_async_copy(source, piece, weight_sem.at[index, side]))
        loads.append(pair)
    for pair in loads:
        for load in pair:
            load.start()

    def loaded(index):
        for load in loads[index]:
            load.wait()

    barrier = pltpu.get_barrier_semaphore()
    for peer in near + far:
        pl.semaphore_signal(barrier, inc=1, device_id=peer, device_id_type=MESH)

    def send(source, target, sems, index, peer):
        return pltpu.make_async_remote_copy(
            src_ref=source,
            dst_ref=target,
            send_sem=sems.at[0, index],
            recv_sem=sems.at[1, index],
            device_id=peer,
            device_id_type=MESH,
        )

    own_slot = images.at[core, y, x, z]
    z_sends = [send(own_slot, own_slot, image_sem, k, far[k]) for k in range(3)]
    line = images.at[core, y, x]
    y_send = send(line, line, image_sem, 3, y_peer)
    x_send = send(line, line, image_sem, 4, x_peer)
    other_line = images.at[core, 1 - y, x, pl.ds(0, 2)]
    x_again = send(other_line, other_line, image_sem, 5, x_peer)
    cross_line = images.at[core, y, 1 - x, pl.ds(2, 2)]
    y_again = send(cross_line, cross_line, image_sem, 7, y_peer)
    plane = images.at[core]
    core_send = send(plane, plane, image_sem, 6, core_peer)

    rows, width = token_ref.shape
    feed = up.shape[1]
    seqs = rows // TEXT_LEN

    def vector(index):
        return wide(
            jnp.concatenate(
                [vector_ref[0, index : index + 1], vector_ref[1, index : index + 1]], axis=1
            )
        )

    def span(index, size):
        return pl.ds(pl.multiple_of(index * size, size), size)

    gain, offset, mix_bias, feed_gain, feed_offset, down_bias, end_gain, end_offset = (
        vector(index) for index in range(8)
    )
    images[core, y, x, z] = image_ref[...]
    column = lax.broadcasted_iota(jnp.int32, (1, 32 * SLOT_ROWS), 1)
    limit = jnp.zeros(column.shape, jnp.int32)
    for slot in range(32):
        slot_core, slot_y, slot_x, slot_z = slot // 16, (slot // 8) % 2, (slot // 4) % 2, slot % 4
        owner = (slot_z * 4 + slot_y * 2 + slot_core) * 2 + slot_x
        limit = jnp.where(
            (column >= slot * SLOT_ROWS) & (column < (slot + 1) * SLOT_ROWS),
            slot * SLOT_ROWS + count_ref[owner],
            limit,
        )
    live = jnp.where(column < limit, 1.0, 0.0)
    own_limit = count_ref[dp * 2 + x]
    own_live = jnp.where(
        lax.broadcasted_iota(jnp.int32, (rows // TEXT_LEN, 1), 0) < own_limit, 1.0, 0.0
    )

    normed[...] = low(centred_scale(wide(token_ref[...]))[0] * gain + offset)
    loaded(0)
    pl.semaphore_wait(barrier, 10)
    for copy in z_sends:
        copy.start()

    def tiles(base):
        for index in range(width // TILE):
            yield pl.ds(base + index * TILE, TILE)

    for index in range(3):
        for cols in tiles(index * width):
            values = product(normed[...], joint[:, cols])
            triple[:, cols] = low(values * ROOT_SCALE if index == 0 else values)

    lane = lax.broadcasted_iota(jnp.int32, (1, PAIR), 1)
    sides = (
        low(jnp.where(lane < HEAD_DIM, 1.0, 0.0)),
        low(jnp.where(lane < HEAD_DIM, 0.0, 1.0)),
    )
    counters = [jnp.broadcast_to(side, (TEXT_GROUP, PAIR)) for side in sides]
    pairs = width // PAIR
    tail_rows = rows % TEXT_GROUP
    tail_start = rows - tail_rows

    def same_of(count):
        row = lax.broadcasted_iota(jnp.int32, (count, TEXT_GROUP), 0) + (TEXT_GROUP - count)
        col = lax.broadcasted_iota(jnp.int32, (count, TEXT_GROUP), 1)
        return jnp.where(row // TEXT_LEN == col // TEXT_LEN, 0.0, CUT)

    def head_parts(values):
        return [values[:, head * TEXT_GROUP : (head + 1) * TEXT_GROUP] for head in range(2)]

    def scores_of(query, keys, same):
        both = jnp.concatenate([keys * side for side in sides], axis=0)
        softs = []
        for score in head_parts(contract_last(query, both)):
            score = score + same
            softs.append(jnp.exp(score - jnp.max(score, axis=-1, keepdims=True)))
        return both, softs

    def attend(group, key_group, same, pair):
        cols = pl.ds(pair * PAIR, PAIR)
        keys = triple[key_group, pl.ds(width + pair * PAIR, PAIR)]
        values = triple[key_group, pl.ds(2 * width + pair * PAIR, PAIR)]
        both, softs = scores_of(triple[group, cols], keys, same)
        spread = jnp.concatenate(
            [
                jnp.concatenate([values * side, counter], axis=1)
                for side, counter in zip(sides, counters)
            ],
            axis=0,
        )
        mixed = product(low(jnp.concatenate(softs, axis=1)), spread)
        attended[group, cols] = low(mixed[:, :PAIR] / mixed[:, PAIR:])

    tail_group = pl.ds(tail_start, tail_rows)
    tail_keys = pl.ds(rows - TEXT_GROUP, TEXT_GROUP)
    same_full = same_of(TEXT_GROUP)
    same_tail = same_of(tail_rows) if tail_rows else None
    for index in range(rows // TEXT_GROUP):
        group = pl.ds(index * TEXT_GROUP, TEXT_GROUP)
        for pair in range(pairs):
            attend(group, group, same_full, pair)
    if tail_rows:
        for pair in range(pairs):
            attend(tail_group, tail_keys, same_tail, pair)

    loaded(1)
    for cols in tiles(0):
        residual[:, cols] = product(attended[...], mixer[:, cols])
    values = wide(token_ref[...]) + residual[...] + mix_bias
    residual[...] = values
    normed_two[...] = low(centred_scale(values)[0] * feed_gain + feed_offset)
    for copy in z_sends:
        copy.wait()
    x_send.start()
    y_send.start()
    loaded(2)
    for index in range(8):
        bias_rows[0:1, index * HALF : (index + 1) * HALF] = wide(
            vector_ref[index // 4, 8 + index % 4 : 9 + index % 4]
        )

    for index in range(feed // width):
        for cols in tiles(index * width):
            values = product(normed_two[...], up[:, cols])
            values = values + bias_rows[0:1, cols]
            active_in[:, cols] = values
            hidden[:, cols] = low(gelu_value(values))

    x_send.wait()
    y_send.wait()
    x_again.start()
    y_again.start()
    loaded(3)
    for cols in tiles(0):
        output[:, cols] = product(hidden[...], down[:, cols])

    x_again.wait()
    y_again.wait()
    core_send.start()
    values = residual[...] + output[...] + down_bias
    output[...] = values
    pooled = jnp.sum(centred_scale(values)[0].reshape(seqs, TEXT_LEN, width), axis=1)
    pooled = low(pooled * (1.0 / TEXT_LEN) * end_gain + end_offset)
    loaded(4)
    embedding = product(pooled, project[...])
    length_rate = lax.rsqrt(jnp.sum(embedding * embedding, axis=-1, keepdims=True) + EPSILON)
    text_unit = embedding * length_rate
    text_low = low(text_unit)
    core_send.wait()

    every = images[...].reshape(2 * 2 * 2 * 4 * SLOT_ROWS, width)
    temper = jnp.exp(jnp.full((1, 1), scale_ref[0], jnp.float32))
    live_total = jnp.sum(live, axis=1, keepdims=True)
    half_inverse = 0.5 / live_total
    cosine = contract_last(text_low, every)
    scaled = jnp.exp(temper * cosine - temper)
    row_sum = jnp.sum(scaled * live, axis=1, keepdims=True)
    near_place = x + 2 * y + 4 * core
    near_sums[near_place] = column_sum(scaled * own_live)
    near_sends = [
        send(near_sums.at[near_place], near_sums.at[near_place], near_sem, k, near[k])
        for k in range(NEAR - 1)
    ]
    for copy in near_sends:
        copy.start()
    image_own = wide(image_ref[:seqs])
    diagonal_cos = jnp.sum(wide(text_low) * image_own, axis=1, keepdims=True)
    row_part = scaled * (own_live / row_sum) * live
    for copy in near_sends:
        copy.wait()
    far_sums[z] = (
        ((near_sums[0] + near_sums[1]) + (near_sums[2] + near_sums[3]))
        + ((near_sums[4] + near_sums[5]) + (near_sums[6] + near_sums[7]))
    )
    far_sends = [
        send(far_sums.at[z], far_sums.at[z], far_sem, k, far[k]) for k in range(3)
    ]
    for copy in far_sends:
        copy.start()
    for copy in far_sends:
        copy.wait()
    columns = (far_sums[0] + far_sums[1]) + (far_sums[2] + far_sums[3])
    coupling = (row_part + scaled * own_live * (live / columns)) * half_inverse
    column_log = jnp.where(live > 0.0, temper + jnp.log(columns), 0.0)
    row_log = temper + jnp.log(row_sum)
    loss_own = column_sum(own_live * (row_log - 2.0 * temper * diagonal_cos))
    loss_shared = jnp.sum(live * column_log, axis=1, keepdims=True)
    devices = lax.axis_size("dp") * lax.axis_size("fsdp")
    loss_part = (loss_own + loss_shared * (1.0 / devices)) * half_inverse
    temper_grad = (
        jnp.sum(column_sum(coupling * cosine), axis=1, keepdims=True)
        - column_sum(own_live * diagonal_cos) / live_total
    )
    unit_grad = product(low(temper * coupling), every)
    unit_grad = unit_grad - (temper / live_total) * own_live * image_own
    embed_grad = low(
        (unit_grad - text_unit * jnp.sum(text_unit * unit_grad, axis=-1, keepdims=True))
        * length_rate
    )
    at_end = (z == 0) | (z == 3)
    at_mid = (z == 1) | (z == 2)
    pair_peer = ((z + 1 - 2 * (z % 2)) * 4 + y * 2 + core, x)
    mid_peer = ((3 - z) * 4 + y * 2 + core, x)

    def remote(source, target, sems, index, peer):
        return pltpu.make_async_remote_copy(
            src_ref=source,
            dst_ref=target,
            send_sem=sems.at[0, index],
            recv_sem=sems.at[1, index],
            device_id=peer,
            device_id_type=MESH,
        )

    def core_copy(step):
        return remote(core_out.at[step % 2], core_in.at[step % CORE_RING], core_sems, step, core_peer)

    def x_copy(step):
        return remote(part.at[step % PART_RING, 1 - x], x_in.at[step % RING], x_sems, step, x_peer)

    def y_copy(step):
        rows = pl.ds(pl.multiple_of((1 - y) * PART, PART), PART)
        return remote(part.at[step % PART_RING, x, rows], y_in.at[step % RING], y_sems, step, y_peer)

    def own_rows():
        return pl.ds(pl.multiple_of(y * PART, PART), PART)

    def end_copy(step):
        return remote(part.at[step % PART_RING, x, own_rows()], end_in.at[step % RING], end_sems, step, pair_peer)

    def mid_copy(step):
        return remote(part.at[step % PART_RING, x, own_rows()], mid_in.at[step % RING], mid_sems, step, mid_peer)

    def own_piece(step):
        return grad_hbm.at[step, core, own_rows()]

    def back_copy(step):
        return remote(total.at[step % TOTAL_RING], own_piece(step), back_sems, step, pair_peer)

    def wide_copy(step, source):
        return remote(source, own_piece(step), wide_sems, step, y_peer)

    def own_copy(step):
        return pltpu.make_async_copy(total.at[step % TOTAL_RING], own_piece(step), own_sems.at[step])

    def twin_copy(step):
        piece = grad_hbm.at[step, core]
        return remote(piece, piece, twin_sems, step, core_peer)

    vector_first = remote(vector_acc, vector_core, vector_sems, 0, core_peer)
    vector_second = remote(vector_sum.at[0], vector_x, vector_sems, 1, x_peer)
    vector_third = remote(vector_sum.at[1], vector_y, vector_sems, 2, y_peer)
    vector_last = []
    for step in range(1, 4):
        other = ((z + step) % 4) * 4 + y * 2 + core
        vector_last.append(
            remote(vector_sum.at[2], vector_z.at[step - 1], vector_sems, 2 + step, (other, x))
        )

    def tick(time):
        @pl.when((time >= 1) & (time - 1 < STEPS))
        def _():
            step = time - 1
            core_copy(step).wait()
            part[step % PART_RING, 1 - x] = low(wide(part[step % PART_RING, 1 - x]) + wide(core_in[step % CORE_RING, 1 - x]))
            x_copy(step).start()
            part[step % PART_RING, x] = low(wide(part[step % PART_RING, x]) + wide(core_in[step % CORE_RING, x]))

        @pl.when(time < STEPS)
        def _():
            step = time
            unit = step // SUB
            half = step % SUB
            fresh = half == 0

            @pl.when(fresh & (unit == 0))
            def _():
                a_vmem[...] = jnp.zeros(a_vmem.shape, jnp.bfloat16)
                a_vmem[:, :POOL_ROWS] = pooled_rows[...].T
                b_vmem[...] = jnp.zeros(b_vmem.shape, jnp.bfloat16)
                b_vmem[:POOL_ROWS] = embed_rows[...]

            @pl.when(fresh & (unit >= 1) & (unit <= 4))
            def _():
                block = unit - 1
                for side in range(2):
                    cols = pl.ds(pl.multiple_of(side * 2 * width + block * HALF, HALF), HALF)
                    a_vmem[pl.ds(side * HALF, HALF)] = hidden[:, cols].T

            @pl.when(fresh & (unit == 1))
            def _():
                b_vmem[...] = down_rows[...]

            @pl.when(fresh & (unit == 5))
            def _():
                a_vmem[...] = normed_two[...].T

            @pl.when(fresh & (unit >= 5) & (unit <= 8))
            def _():
                b_vmem[...] = pre_rows[:, span(unit - 5, width)]

            @pl.when(fresh & (unit == 9))
            def _():
                a_vmem[...] = attended[...].T
                b_vmem[...] = mix_rows[...]

            @pl.when(fresh & (unit == 10))
            def _():
                a_vmem[...] = normed[...].T

            @pl.when(fresh & (unit >= 10))
            def _():
                b_vmem[...] = triple[:, span(unit - 10, width)]

            term = b_vmem[...]
            for which in range(2):
                rows = pl.ds(
                    pl.multiple_of(which * HALF + (1 - core) * QUARTER + half * ROWS, ROWS), ROWS
                )
                core_out[step % 2, which] = low(product(a_vmem[rows], term))
            core_copy(step).start()
            for which in range(2):
                rows = pl.ds(
                    pl.multiple_of(which * HALF + core * QUARTER + half * ROWS, ROWS), ROWS
                )
                part[step % PART_RING, which] = low(product(a_vmem[rows], term))

        @pl.when((time >= 3) & (time - 3 < STEPS))
        def _():
            step = time - 3
            x_copy(step).wait()
            rows = pl.ds(pl.multiple_of((1 - y) * PART, PART), PART)
            part[step % PART_RING, x, rows] = low(wide(part[step % PART_RING, x, rows]) + wide(x_in[step % RING, rows]))
            y_copy(step).start()
            part[step % PART_RING, x, own_rows()] = low(
                wide(part[step % PART_RING, x, own_rows()]) + wide(x_in[step % RING, own_rows()])
            )

        @pl.when((time >= 4) & (time - 4 < STEPS))
        def _():
            step = time - 4
            y_copy(step).wait()
            part[step % PART_RING, x, own_rows()] = low(
                wide(part[step % PART_RING, x, own_rows()]) + wide(y_in[step % RING])
            )

            @pl.when(at_end)
            def _():
                end_copy(step).start()

        @pl.when((time >= 5) & (time - 5 < STEPS))
        def _():
            step = time - 5

            @pl.when(at_end)
            def _():
                end_copy(step).wait_send()

            @pl.when(at_mid)
            def _():
                end_copy(step).wait_recv()
                part[step % PART_RING, x, own_rows()] = low(
                    wide(part[step % PART_RING, x, own_rows()]) + wide(end_in[step % RING])
                )
                mid_copy(step).start()

        @pl.when((time >= 6) & (time - 6 < STEPS) & at_mid)
        def _():
            step = time - 6
            mid_copy(step).wait()
            total[step % TOTAL_RING] = low(
                wide(part[step % PART_RING, x, own_rows()]) + wide(mid_in[step % RING])
            )
            back_copy(step).start()
            wide_copy(step, total.at[step % TOTAL_RING]).start()
            own_copy(step).start()

        @pl.when((time >= 7) & (time - 7 < STEPS))
        def _():
            step = time - 7

            @pl.when(at_end)
            def _():
                back_copy(step).wait_recv()
                wide_copy(step, own_piece(step)).start()

            @pl.when(at_mid)
            def _():
                back_copy(step).wait_send()

        @pl.when((time >= 8) & (time - 8 < STEPS))
        def _():
            step = time - 8
            wide_copy(step, total.at[step % TOTAL_RING]).wait()

            @pl.when(at_mid)
            def _():
                own_copy(step).wait()

            twin_copy(step).start()

        @pl.when((time >= 9) & (time - 9 < STEPS))
        def _():
            step = time - 9
            twin_copy(step).wait()

        @pl.when(time == VECTOR_START + 0)
        def _():
            vector_first.start()

        @pl.when(time == VECTOR_START + 1)
        def _():
            vector_first.wait()
            vector_sum[0] = vector_acc[...] + vector_core[...]
            vector_second.start()

        @pl.when(time == VECTOR_START + 3)
        def _():
            vector_second.wait()
            vector_sum[1] = vector_sum[0] + vector_x[...]
            vector_third.start()

        @pl.when(time == VECTOR_START + 5)
        def _():
            vector_third.wait()
            vector_sum[2] = vector_sum[1] + vector_y[...]
            for copy in vector_last:
                copy.start()

        @pl.when(time == VECTOR_START + 7)
        def _():
            for copy in vector_last:
                copy.wait()
            order = lax.broadcasted_iota(jnp.int32, (VECTOR_ROWS, WIDTH), 0) * 0 + z
            own = vector_sum[2]
            before_one = vector_z[0]
            before_two = vector_z[1]
            before_three = vector_z[2]

            def pick(where):
                shift = (order - where + 4) % 4
                return jnp.where(
                    shift == 0,
                    own,
                    jnp.where(
                        shift == 1,
                        before_one,
                        jnp.where(shift == 2, before_two, before_three),
                    ),
                )

            vector_out[...] = (pick(0) + pick(1)) + (pick(2) + pick(3))

    pooled_rows[...] = jnp.zeros(pooled_rows.shape, jnp.bfloat16)
    pooled_rows[:SLOT_ROWS] = jnp.pad(pooled, ((0, SLOT_ROWS - seqs), (0, 0)))
    embed_rows[...] = jnp.zeros(embed_rows.shape, jnp.bfloat16)
    embed_rows[:SLOT_ROWS] = jnp.pad(embed_grad, ((0, SLOT_ROWS - seqs), (0, 0)))
    pooled_grad = contract_last(embed_grad, project[...]) * (1.0 / TEXT_LEN)
    pl.loop(0, 2)(tick)
    for index in range(rows // CHUNK):
        work[index * 8 : index * 8 + CHUNK // TEXT_LEN] = pooled_grad[
            index * (CHUNK // TEXT_LEN) : (index + 1) * (CHUNK // TEXT_LEN)
        ]

    vector_acc[...] = jnp.zeros(vector_acc.shape, jnp.float32)
    column = lax.broadcasted_iota(jnp.int32, (1, width), 1)
    vector_acc[12:13] = jnp.where(
        column == 0, loss_part, jnp.where(column == 1, temper * temper_grad, 0.0)
    )
    vector_acc[11:12] = column_sum(pooled_grad) * float(TEXT_LEN)

    def gather(index, value):
        vector_acc[index : index + 1] = vector_acc[index : index + 1] + value

    @pl.loop(0, rows // CHUNK)
    def _(index):
        chunk = span(index, CHUNK)
        grad = work[span(index, 8)][: CHUNK // TEXT_LEN]
        grad = jnp.broadcast_to(
            grad[:, None, :], (CHUNK // TEXT_LEN, TEXT_LEN, width)
        ).reshape(CHUNK, width)
        value, gain_part = norm_back(output[chunk], grad, end_gain)
        output[chunk] = value
        down_rows[chunk] = low(value)
        gather(10, column_sum(gain_part))
        gather(9, column_sum(value))

    @pl.loop(0, feed // width)
    def _(index):
        tick(2 + index)
        for cols in tiles(pl.multiple_of(index * width, width)):
            values = contract_last(down_rows[...], down[cols]) * gelu_slope(active_in[:, cols])
            pre_rows[:, cols] = low(values)
            bias_rows[:, cols] = jnp.sum(values.reshape(rows // 8, 8, TILE), axis=0)

    for index, cols in enumerate(tiles(0)):
        active_in[:, cols] = contract_last(pre_rows[...], up[cols])
        if index < 2:
            tick(6 + index)

    @pl.loop(0, rows // CHUNK)
    def _(index):
        chunk = span(index, CHUNK)
        grad = active_in[chunk, :width]
        value, gain_part = norm_back(residual[chunk], grad, feed_gain)
        value = value + output[chunk]
        output[chunk] = value
        mix_rows[chunk] = low(value)
        gather(3, column_sum(gain_part))
        gather(4, column_sum(grad))
        gather(2, column_sum(value))

    tick(8)
    for index in range(width // TILE):
        active_in[:, pl.ds(width + index * TILE, TILE)] = contract_last(
            mix_rows[...], mixer[pl.ds(index * TILE, TILE)]
        )
    tick(9)

    def attend_back(group, key_group, same, pair, count):
        cols = pl.ds(pair * PAIR, PAIR)
        key_cols = pl.ds(width + pair * PAIR, PAIR)
        value_cols = pl.ds(2 * width + pair * PAIR, PAIR)
        query = triple[group, cols]
        values = triple[key_group, value_cols]
        both, softs = scores_of(query, triple[key_group, key_cols], same)
        outer = low(active_in[group, pl.ds(width + pair * PAIR, PAIR)])
        grads = head_parts(
            contract_last(outer, jnp.concatenate([values * side for side in sides], axis=0))
        )
        lows, score_grads = [], []
        for soft, grad in zip(softs, grads):
            soft = soft / jnp.sum(soft, axis=-1, keepdims=True)
            lows.append(low(soft))
            score_grads.append(
                low(soft * (grad - jnp.sum(soft * grad, axis=-1, keepdims=True)))
            )
        score_grad = jnp.concatenate(score_grads, axis=1)
        left_lane = lax.broadcasted_iota(jnp.int32, (count, PAIR), 1) < HEAD_DIM

        def joined(stacked):
            top = stacked[TEXT_GROUP - count : TEXT_GROUP]
            bottom = stacked[2 * TEXT_GROUP - count :]
            return low(jnp.where(left_lane, top, bottom))

        triple[group, key_cols] = joined(contract_first(score_grad, query))
        triple[group, cols] = low(product(score_grad, both) * ROOT_SCALE)
        triple[group, value_cols] = joined(
            contract_first(jnp.concatenate(lows, axis=1), outer)
        )

    @pl.loop(0, rows // TEXT_GROUP)
    def _(index):
        tick(10 + index)
        group = span(index, TEXT_GROUP)
        for pair in range(pairs):
            attend_back(group, group, same_full, pair, TEXT_GROUP)

    tick(14)
    if tail_rows:
        for pair in range(pairs):
            attend_back(tail_group, tail_keys, same_tail, pair, tail_rows)
    for index, cols in enumerate(tiles(0)):
        active_in[:, cols] = contract_last(triple[...], joint[cols])
        if index < 2:
            tick(15 + index)

    @pl.loop(0, rows // CHUNK)
    def _(index):
        chunk = span(index, CHUNK)
        grad = active_in[chunk, :width]
        value, gain_part = norm_back(wide(token_ref[chunk]), grad, gain)
        token_out[chunk] = value + output[chunk]
        gather(0, column_sum(gain_part))
        gather(1, column_sum(grad))

    for index in range(feed // width):
        vector_acc[5 + index : 6 + index] = column_sum(
            bias_rows[:, index * width : (index + 1) * width]
        )
    pl.loop(17, STEPS + TAIL + 1)(tick)


def text_kernel(tokens, vectors, image_low, pair_counts, log_scale, shards, others):
    rows, width = tokens.shape
    feed = shards[2].shape[1]
    any_spec = pl.BlockSpec(memory_space=pl.ANY)
    vmem_spec = pl.BlockSpec(memory_space=pltpu.VMEM)
    dma = pltpu.SemaphoreType.DMA
    low_type = jnp.bfloat16
    smem_spec = pl.BlockSpec(memory_space=pltpu.SMEM)
    slots = 2 * 2 * 2 * 4 * SLOT_ROWS
    return pl.pallas_call(
        text_body,
        out_shape=(
            jax.ShapeDtypeStruct((STEPS, 2, ROWS, width), low_type),
            jax.ShapeDtypeStruct((VECTOR_ROWS, width), jnp.float32),
            jax.ShapeDtypeStruct((rows, width), jnp.float32),
        ),
        in_specs=[vmem_spec] * 3 + [smem_spec] * 2 + [any_spec] * 10,
        out_specs=(any_spec, vmem_spec, vmem_spec),
        scratch_shapes=[
            pltpu.VMEM((2 * shard.shape[0], shard.shape[1]), low_type) for shard in shards
        ]
        + [
            pltpu.VMEM((rows, width), low_type),
            pltpu.VMEM((rows, width), low_type),
            pltpu.VMEM((rows, width), low_type),
            pltpu.VMEM((rows, feed), low_type),
            pltpu.VMEM((POOL_ROWS, width), low_type),
            pltpu.VMEM((POOL_ROWS, width), low_type),
            pltpu.VMEM((rows, width), low_type),
            pltpu.VMEM((rows, width), low_type),
            pltpu.VMEM((rows, feed), low_type),
            pltpu.VMEM((rows, 3 * width), low_type),
            pltpu.VMEM((rows, width), jnp.float32),
            pltpu.VMEM((rows, feed), jnp.float32),
            pltpu.VMEM((rows, width), jnp.float32),
            pltpu.VMEM((rows // CHUNK * 8, width), jnp.float32),
            pltpu.VMEM((8, feed), jnp.float32),
            pltpu.VMEM((2, 2, 2, 4, SLOT_ROWS, width), low_type),
            pltpu.VMEM((NEAR, 1, slots), jnp.float32),
            pltpu.VMEM((4, 1, slots), jnp.float32),
            dma((5, 2)),
            dma((2, 8)),
            dma((2, NEAR - 1)),
            dma((2, 3)),
            pltpu.VMEM((width, rows), low_type),
            pltpu.VMEM((rows, width), low_type),
            pltpu.VMEM((VECTOR_ROWS, width), jnp.float32),
            pltpu.VMEM((2, 2, ROWS, width), low_type),
            pltpu.VMEM((PART_RING, 2, ROWS, width), low_type),
            pltpu.VMEM((CORE_RING, 2, ROWS, width), low_type),
            pltpu.VMEM((RING, ROWS, width), low_type),
            pltpu.VMEM((RING, PART, width), low_type),
            pltpu.VMEM((RING, PART, width), low_type),
            pltpu.VMEM((RING, PART, width), low_type),
            pltpu.VMEM((TOTAL_RING, PART, width), low_type),
            pltpu.VMEM((VECTOR_ROWS, width), jnp.float32),
            pltpu.VMEM((VECTOR_ROWS, width), jnp.float32),
            pltpu.VMEM((VECTOR_ROWS, width), jnp.float32),
            pltpu.VMEM((3, VECTOR_ROWS, width), jnp.float32),
            pltpu.VMEM((3, VECTOR_ROWS, width), jnp.float32),
        ]
        + [dma((2, STEPS)) for _ in range(8)]
        + [
            dma((STEPS,)),
            dma((2, 6)),
        ],
        compiler_params=pltpu.CompilerParams(
            collective_id=1, has_side_effects=True, vmem_limit_bytes=62 * 1024 * 1024
        ),
    )(tokens, vectors, image_low, pair_counts, log_scale, *shards, *others)


def pack_rows(vectors):
    index = lax.broadcasted_iota(jnp.int32, (VECTOR_ROWS, vectors[0].shape[0]), 0)
    packed = jnp.zeros(index.shape, vectors[0].dtype)
    for row, vector in enumerate(vectors):
        packed = jnp.where(index == row, vector[None, :], packed)
    return packed


IMAGE_GROUP = 4
IMAGE_BLOCK = 12
IMAGE_ROWS = 104
IMAGE_KEYS = 128


def image_body(
    token_ref,
    vector_ref,
    shard_vector,
    joint_hbm,
    mixer_hbm,
    up_hbm,
    down_hbm,
    project_hbm,
    joint_shard,
    mixer_shard,
    up_shard,
    down_shard,
    project_shard,
    image_out,
    vector_out,
    joint_other,
    mixer_other,
    up_other,
    down_other,
    project_other,
    joint,
    mixer,
    up,
    down,
    project,
    normed,
    normed_two,
    triple,
    attended,
    residual,
    final,
    hidden,
    pooled,
    load_sem,
    x_sem,
    y_sem,
    z_sem,
    core_sem,
):
    dp = lax.axis_index("dp")
    x = lax.axis_index("fsdp")
    zb, y, core = (dp // 4) % 2, (dp // 2) % 2, dp % 2
    x_peer, y_peer, core_peer = (dp, 1 - x), (dp + 2 - 4 * y, x), (dp + 1 - 2 * core, x)
    z_peer = (dp + 4 - 8 * zb, x)
    loads = [
        pltpu.make_async_copy(source, target, load_sem.at[index])
        for index, (source, target) in enumerate(
            (
                (joint_hbm, joint),
                (mixer_hbm, mixer),
                (up_hbm, up),
                (down_hbm, down),
                (project_hbm, project),
            )
        )
    ]
    for load in loads:
        load.start()
    barrier = pltpu.get_barrier_semaphore()
    for peer in (x_peer, y_peer, z_peer, core_peer):
        pl.semaphore_signal(barrier, inc=1, device_id=peer, device_id_type=MESH)
    vector_out[x] = shard_vector[...]
    pl.semaphore_wait(barrier, 4)

    def send(source, target, sems, index, peer):
        return pltpu.make_async_remote_copy(
            src_ref=source,
            dst_ref=target,
            send_sem=sems.at[0, index],
            recv_sem=sems.at[1, index],
            device_id=peer,
            device_id_type=MESH,
        )

    shards = (joint_shard, mixer_shard, up_shard, down_shard, project_shard)
    others = (joint_other, mixer_other, up_other, down_other, project_other)
    x_sends, x_cross, y_sends, z_sends, core_sends, core_cross = [], [], [], [], [], []
    for index, (shard, other) in enumerate(zip(shards, others)):
        size = shard.shape[0] // 8

        def rows_of(piece):
            return pl.ds(pl.multiple_of(piece * size, size), size)

        own = rows_of(core * 4 + y * 2 + zb)
        beside_y = rows_of(core * 4 + (1 - y) * 2 + zb)
        beside_z = rows_of(core * 4 + y * 2 + 1 - zb)
        cross = rows_of(core * 4 + (1 - y) * 2 + 1 - zb)
        x_sends.append(send(shard.at[own], other.at[own], x_sem, index, x_peer))
        x_cross.append(send(shard.at[cross], other.at[cross], x_sem, 6 + index, x_peer))
        y_sends.append(send(other.at[own], other.at[own], y_sem, index, y_peer))
        z_sends.append(send(other.at[own], other.at[own], z_sem, index, z_peer))
        core_sends.append(
            [
                send(other.at[piece], other.at[piece], core_sem, 4 * index + place, core_peer)
                for place, piece in enumerate((own, beside_y, beside_z))
            ]
        )
        core_cross.append(
            send(other.at[cross], other.at[cross], core_sem, 4 * index + 3, core_peer)
        )
    vector_send = send(vector_out.at[x], vector_out.at[x], x_sem, 5, x_peer)
    vector_send.start()
    for index in (2, 3, 0, 1, 4):
        x_sends[index].start()
    for index in (2, 3, 0, 1, 4):
        x_cross[index].start()

    def pass_near(index):
        x_sends[index].wait()
        y_sends[index].start()
        z_sends[index].start()

    def pass_core(index):
        y_sends[index].wait()
        z_sends[index].wait()
        for copy in core_sends[index]:
            copy.start()

    def pass_cross(index):
        x_cross[index].wait()
        core_cross[index].start()

    blocks, rows, width = token_ref.shape
    feed = up.shape[1]
    gain, offset, mix_bias, feed_gain, feed_offset, down_bias, end_gain, end_offset = (
        wide(vector_ref[index : index + 1]) for index in range(8)
    )

    def span(index, size):
        return pl.ds(pl.multiple_of(index * size, 8), size)

    seqs = rows // IMAGE_LEN
    pool_row = lax.broadcasted_iota(jnp.int32, (seqs, rows), 0)
    pool_col = lax.broadcasted_iota(jnp.int32, (seqs, rows), 1) // IMAGE_LEN
    pool = low(jnp.where(pool_row == pool_col, 1.0, 0.0))
    group_rows = IMAGE_GROUP * IMAGE_LEN
    lane = lax.broadcasted_iota(jnp.int32, (1, PAIR), 1)
    sides = (
        low(jnp.where(lane < HEAD_DIM, 1.0, 0.0)),
        low(jnp.where(lane < HEAD_DIM, 0.0, 1.0)),
    )
    seam = lax.broadcasted_iota(jnp.int32, (8, PAIR), 0) < 4
    windows = []
    for row_start, key_start in (
        (0, 0),
        (group_rows - IMAGE_ROWS, group_rows - IMAGE_KEYS),
    ):
        row = lax.broadcasted_iota(jnp.int32, (IMAGE_ROWS, IMAGE_KEYS), 0) + row_start
        col = lax.broadcasted_iota(jnp.int32, (IMAGE_ROWS, IMAGE_KEYS), 1) + key_start
        same = jnp.where(row // IMAGE_LEN == col // IMAGE_LEN, 0.0, CUT)
        windows.append((row_start, key_start, same))
    counters = [jnp.broadcast_to(side, (IMAGE_KEYS, PAIR)) for side in sides]

    def attend(start, pair):
        cols = pair * PAIR
        parts = []
        for row_start, key_start, same in windows:
            query = triple[pl.ds(start + row_start, IMAGE_ROWS), pl.ds(cols, PAIR)]
            keys = triple[pl.ds(start + key_start, IMAGE_KEYS), pl.ds(width + cols, PAIR)]
            values = triple[pl.ds(start + key_start, IMAGE_KEYS), pl.ds(2 * width + cols, PAIR)]
            scores = contract_last(
                query, jnp.concatenate([keys * side for side in sides], axis=0)
            )
            softs = []
            for head in range(2):
                score = scores[:, head * IMAGE_KEYS : (head + 1) * IMAGE_KEYS] + same
                softs.append(low(jnp.exp(score - jnp.max(score, axis=-1, keepdims=True))))
            spread = jnp.concatenate(
                [
                    jnp.concatenate([values * side, counter], axis=1)
                    for side, counter in zip(sides, counters)
                ],
                axis=0,
            )
            mixed = product(jnp.concatenate(softs, axis=1), spread)
            parts.append(mixed[:, :PAIR] / mixed[:, PAIR:])
        first, second = parts
        edge = IMAGE_ROWS - 8
        attended[pl.ds(start, edge), pl.ds(cols, PAIR)] = low(first[:edge])
        attended[pl.ds(start + edge, 8), pl.ds(cols, PAIR)] = low(
            jnp.where(seam, first[edge:], second[:8])
        )
        attended[pl.ds(start + IMAGE_ROWS, edge), pl.ds(cols, PAIR)] = low(second[8:])

    pairs = width // PAIR
    groups = rows // group_rows

    def cols_of(index):
        return pl.ds(index * TILE, TILE)

    def first_norm(block):
        normed[...] = low(centred_scale(wide(token_ref[block]))[0] * gain + offset)

    def make_triple(index):
        cols = cols_of(index)
        values = product(normed[...], joint[:, cols])
        triple[:, cols] = low(values * ROOT_SCALE if index < 3 else values)

    def mix(block, index):
        cols = cols_of(index)
        residual[:, cols] = (
            wide(token_ref[block, :, cols])
            + product(attended[...], mixer[:, cols])
            + mix_bias[:, index * TILE : (index + 1) * TILE]
        )

    def second_norm():
        normed_two[...] = low(centred_scale(residual[...])[0] * feed_gain + feed_offset)

    def feed_up(index):
        cols = cols_of(index)
        row, start = 8 + index // 3, (index % 3) * TILE
        bias = wide(vector_ref[row : row + 1, start : start + TILE])
        hidden[:, cols] = low(gelu_value(product(normed_two[...], up[:, cols]) + bias))

    def feed_down(index):
        cols = cols_of(index)
        final[:, cols] = (
            residual[:, cols]
            + product(hidden[...], down[:, cols])
            + down_bias[:, index * TILE : (index + 1) * TILE]
        )

    def pool_rows(block):
        mean = product(pool, low(centred_scale(final[...])[0])) * (1.0 / IMAGE_LEN)
        pooled[block] = mean * end_gain + end_offset

    def attend_unit(unit):
        attend((unit // pairs) * group_rows, unit % pairs)

    units = groups * pairs

    first_norm(0)
    loads[0].wait()
    for index in range(9):
        make_triple(index)
    for unit in range(units):
        attend_unit(unit)
    loads[1].wait()
    loads[2].wait()
    loads[3].wait()
    pass_near(2)
    for index in range(3):
        mix(0, index)
    second_norm()
    for block in range(1, blocks):
        first_norm(block)
        for index in range(9):
            make_triple(index)
        if block == 1:
            pass_near(3)
        for unit in range(units):
            attend_unit(unit)
            if unit < 12:
                feed_up(unit)
            elif unit % 2 == 1:
                feed_down((unit - 12) // 2)
        if block == 1:
            pass_near(0)
            pass_near(1)
            pass_near(4)
            pass_core(2)
            pass_core(3)
        if block == 2:
            pass_core(0)
            pass_core(1)
            pass_core(4)
        for index in range(3):
            mix(block, index)
        pool_rows(block - 1)
        second_norm()

    for index in range(12):
        feed_up(index)
    for index in range(3):
        feed_down(index)
    for index in range(5):
        pass_cross(index)
    pool_rows(blocks - 1)
    loads[4].wait()
    rest = jnp.zeros((SLOT_ROWS - blocks * IMAGE_BLOCK, width), jnp.float32)
    means = jnp.concatenate([pooled[block] for block in range(blocks)] + [rest], axis=0)
    embedding = product(low(means), project[...])
    image_out[...] = low(
        embedding * lax.rsqrt(jnp.sum(embedding * embedding, axis=-1, keepdims=True) + EPSILON)
    )
    for copies, copy in zip(core_sends, core_cross):
        for near in copies:
            near.wait()
        copy.wait()
    vector_send.wait()


def image_kernel(tokens, weights, shard_vector, shards):
    (
        norm_gain,
        norm_offset,
        joint,
        mixer,
        mixer_bias,
        feed_gain,
        feed_offset,
        up,
        up_bias,
        down,
        down_bias,
        end_gain,
        end_offset,
        project,
    ) = weights
    total, width = tokens.shape
    rows = IMAGE_BLOCK * IMAGE_LEN
    blocks = total // rows
    feed = up.shape[1]
    vectors = pack_rows(
        [
            norm_gain,
            norm_offset,
            mixer_bias,
            feed_gain,
            feed_offset,
            down_bias,
            end_gain,
            end_offset,
        ]
        + [up_bias[start : start + width] for start in range(0, feed, width)],
    )
    any_spec = pl.BlockSpec(memory_space=pl.ANY)
    vmem_spec = pl.BlockSpec(memory_space=pltpu.VMEM)
    dma = pltpu.SemaphoreType.DMA
    low_type = jnp.bfloat16
    matrices = (joint, mixer, up, down, project)
    image_out, vector_out, *others = pl.pallas_call(
        image_body,
        out_shape=(
            jax.ShapeDtypeStruct((SLOT_ROWS, width), low_type),
            jax.ShapeDtypeStruct((2, *shard_vector.shape), low_type),
            *(
                jax.ShapeDtypeStruct(shard.shape, low_type)
                for shard in shards
            ),
        ),
        in_specs=[vmem_spec] * 3 + [any_spec] * 10,
        out_specs=(vmem_spec, vmem_spec, *([any_spec] * 5)),
        scratch_shapes=[pltpu.VMEM(matrix.shape, low_type) for matrix in matrices]
        + [
            pltpu.VMEM((rows, width), low_type),
            pltpu.VMEM((rows, width), low_type),
            pltpu.VMEM((rows, 3 * width), low_type),
            pltpu.VMEM((rows, width), low_type),
            pltpu.VMEM((rows, width), jnp.float32),
            pltpu.VMEM((rows, width), jnp.float32),
            pltpu.VMEM((rows, feed), low_type),
            pltpu.VMEM((blocks, IMAGE_BLOCK, width), jnp.float32),
            dma((5,)),
            dma((2, 11)),
            dma((2, 5)),
            dma((2, 5)),
            dma((2, 20)),
        ],
        compiler_params=pltpu.CompilerParams(
            collective_id=2, has_side_effects=True, vmem_limit_bytes=60 * 1024 * 1024
        ),
    )(
        tokens.reshape(blocks, rows, width),
        vectors,
        shard_vector,
        *matrices,
        *shards,
    )
    return image_out, vector_out, others


def finish_body(grad_hbm, packed_ref, *refs):
    (
        gain,
        offset,
        joint,
        mixer,
        mix_bias,
        feed_gain,
        feed_offset,
        up,
        up_bias,
        down,
        down_bias,
        end_gain,
        end_offset,
        project,
        scale_out,
        loss_out,
        low_values,
        wide_values,
        load_sem,
        store_sem,
    ) = refs
    shard = lax.axis_index("fsdp")
    loads = [
        pltpu.make_async_copy(
            grad_hbm.at[pl.ds(unit * SUB, SUB)],
            low_values.at[pl.ds(unit * SUB, SUB)],
            load_sem.at[unit],
        )
        for unit in range(UNITS)
    ]
    for load in loads:
        load.start()
    for row, target in (
        (0, gain),
        (1, offset),
        (2, mix_bias),
        (3, feed_gain),
        (4, feed_offset),
        (9, down_bias),
        (10, end_gain),
        (11, end_offset),
    ):
        cols = pl.ds(pl.multiple_of(shard * HALF, HALF), HALF)
        target[...] = packed_ref[pl.ds(row, 1), cols].reshape(HALF)
    for part in range(2):
        up_bias[pl.ds(part * WIDTH, WIDTH)] = packed_ref[
            pl.ds(5 + 2 * shard + part, 1), :
        ].reshape(WIDTH)
    loss_out[...] = packed_ref[12:13, 0:1]
    scale_out[...] = packed_ref[12:13, 1:2]
    places = (
        [(project, pl.ds(0, HALF), pl.ds(0, WIDTH))]
        + [(down, pl.ds(unit * HALF, HALF), pl.ds(0, WIDTH)) for unit in range(4)]
        + [(up, pl.ds(0, HALF), pl.ds(unit * WIDTH, WIDTH)) for unit in range(4)]
        + [(mixer, pl.ds(0, HALF), pl.ds(0, WIDTH))]
        + [(joint, pl.ds(0, HALF), pl.ds(unit * WIDTH, WIDTH)) for unit in range(3)]
    )
    stores = []
    for unit, (target, rows, cols) in enumerate(places):
        loads[unit].wait()
        for core in range(2):
            for half in range(SUB):
                rows_here = pl.ds(core * QUARTER + half * ROWS, ROWS)
                wide_values[unit, rows_here] = wide(low_values[unit * SUB + half, core])
        copy = pltpu.make_async_copy(wide_values.at[unit], target.at[rows, cols], store_sem.at[unit])
        copy.start()
        stores.append(copy)
    for copy in stores:
        copy.wait()


def finish_kernel(grads, packed):
    single = jnp.float32
    any_spec = pl.BlockSpec(memory_space=pl.ANY)
    vmem_spec = pl.BlockSpec(memory_space=pltpu.VMEM)
    vector = (jax.ShapeDtypeStruct((HALF,), single), vmem_spec)
    scalar = (jax.ShapeDtypeStruct((1, 1), single), vmem_spec)

    def matrix(rows, cols):
        return (jax.ShapeDtypeStruct((rows, cols), single), any_spec)

    outs = (
        vector,
        vector,
        matrix(HALF, 3 * WIDTH),
        matrix(HALF, WIDTH),
        vector,
        vector,
        vector,
        matrix(HALF, 4 * WIDTH),
        (jax.ShapeDtypeStruct((4 * HALF,), single), vmem_spec),
        matrix(4 * HALF, WIDTH),
        vector,
        vector,
        vector,
        matrix(HALF, WIDTH),
        scalar,
        scalar,
    )
    return pl.pallas_call(
        finish_body,
        out_shape=tuple(shape for shape, spec in outs),
        in_specs=[any_spec, vmem_spec],
        out_specs=tuple(spec for shape, spec in outs),
        scratch_shapes=[
            pltpu.VMEM((STEPS, 2, ROWS, WIDTH), jnp.bfloat16),
            pltpu.VMEM((UNITS, HALF, WIDTH), single),
            pltpu.SemaphoreType.DMA((UNITS,)),
            pltpu.SemaphoreType.DMA((UNITS,)),
        ],
        compiler_params=pltpu.CompilerParams(vmem_limit_bytes=48 * 1024 * 1024),
    )(grads, packed)


def reduce_plain(factors, vectors):
    terms = [contract_first(left, right) for left, right in factors]
    joint, mixer, upward, downward, project = terms
    gain, offset, mixbias, feedgain, feedoffset, upbias, downbias, endgain, endoffset = vectors
    ordered = (
        gain,
        offset,
        joint,
        mixer,
        mixbias,
        feedgain,
        feedoffset,
        upward,
        upbias,
        downward,
        downbias,
        endgain,
        endoffset,
        project,
    )
    shards = tuple(
        lax.psum_scatter(term, "fsdp", scatter_dimension=0, tiled=True) for term in ordered
    )
    return lax.psum(shards, "dp")


def on_device_plain(*arrays):
    (
        text_tokens,
        image_tokens,
        pair_counts,
        log_scale,
        text_gain,
        text_offset,
        text_joint,
        text_mixer,
        text_mixbias,
        text_feedgain,
        text_feedoffset,
        text_upward,
        text_upbias,
        text_downward,
        text_downbias,
        text_endgain,
        text_endoffset,
        text_project,
        image_gain,
        image_offset,
        image_joint,
        image_mixer,
        image_mixbias,
        image_feedgain,
        image_feedoffset,
        image_upward,
        image_upbias,
        image_downward,
        image_downbias,
        image_endgain,
        image_endoffset,
        image_project,
    ) = arrays
    image_weights = (
        image_gain,
        image_offset,
        image_joint,
        image_mixer,
        image_mixbias,
        image_feedgain,
        image_feedoffset,
        image_upward,
        image_upbias,
        image_downward,
        image_downbias,
        image_endgain,
        image_endoffset,
        image_project,
    )
    group_count = lax.axis_size("dp") * lax.axis_size("fsdp")
    device = lax.axis_index("dp") * lax.axis_size("fsdp") + lax.axis_index("fsdp")
    pair_total = group_count * SLOTS
    live_all = (
        (jnp.arange(SLOTS)[None, :] < pair_counts[:, None]).astype(jnp.float32).reshape(pair_total)
    )
    live_total = jnp.sum(live_all)
    text_live = lax.dynamic_slice_in_dim(live_all, device * SLOTS, SLOTS)
    temper = jnp.exp(log_scale[0])
    half_inverse = 1.0 / (2.0 * live_total)
    image_unit = forward_block(image_tokens, image_weights, IMAGE_LEN)[0]
    image_low = image_unit.astype(jnp.bfloat16)
    shard_piece = lax.all_gather(image_low, ("dp", "fsdp"), axis=0, tiled=True)
    text_weights = tuple(
        lax.all_gather(shard, "fsdp", axis=0, tiled=True)
        for shard in (
            text_gain,
            text_offset,
            text_joint,
            text_mixer,
            text_mixbias,
            text_feedgain,
            text_feedoffset,
            text_upward,
            text_upbias,
            text_downward,
            text_downbias,
            text_endgain,
            text_endoffset,
            text_project,
        )
    )
    text_unit, kept_values = forward_block(text_tokens, text_weights, TEXT_LEN)
    text_low = text_unit.astype(jnp.bfloat16)
    cosine = contract_last(text_low, shard_piece)
    scaled = jnp.exp(temper * cosine - temper)
    image_live = live_all
    forward_row_sum = jnp.sum(scaled * image_live[None, :], axis=1)
    forward_column_sum = jnp.sum(scaled * text_live[:, None], axis=0)
    column_sum = forward_column_sum
    column_sum = lax.psum(column_sum, ("dp", "fsdp"))
    diagonal_cos = jnp.sum(text_low.astype(jnp.float32) * image_low.astype(jnp.float32), axis=1)
    row_log = temper + jnp.log(forward_row_sum)
    column_log = temper + jnp.log(lax.dynamic_slice_in_dim(column_sum, device * SLOTS, SLOTS))
    diagonal = temper * diagonal_cos
    loss_part = jnp.sum(text_live * (row_log - diagonal) + text_live * (column_log - diagonal)) / (
        2.0 * live_total
    )
    coupling = (
        scaled * (text_live / forward_row_sum)[:, None] * image_live[None, :]
        + scaled * text_live[:, None] * (image_live / column_sum)[None, :]
    ) * half_inverse
    temper_grad = jnp.sum(coupling * cosine)
    unit_grad = product((temper * coupling).astype(jnp.bfloat16), shard_piece)
    unit_grad, temper_grad = (unit_grad, temper_grad)
    unit_grad = unit_grad - temper / live_total * text_live[:, None] * image_low.astype(jnp.float32)
    temper_grad = temper_grad - jnp.sum(text_live * diagonal_cos) / live_total
    loss_total, scale_total = lax.psum((loss_part, temper * temper_grad), ("dp", "fsdp"))
    factors, vectors, token_grad = backward_block(
        kept_values, text_weights, unit_grad, TEXT_LEN
    )
    final_grads = reduce_plain(factors, vectors)
    return (
        *final_grads,
        jnp.reshape(scale_total, (1,)),
        token_grad,
        jnp.reshape(loss_total, (1,)),
    )


def on_device(*arrays):
    if (lax.axis_size("dp"), lax.axis_size("fsdp")) != (16, 2):
        return on_device_plain(*arrays)
    text_tokens, image_tokens, pair_counts, log_scale = arrays[:4]
    text_weights, image_weights = arrays[4:18], arrays[18:32]
    matrix_places = (2, 3, 7, 9, 13)
    vector_places = (0, 1, 4, 5, 6, 10, 11, 12)
    shard_vector = pack_rows(
        [text_weights[place] for place in vector_places]
        + [text_weights[8][start : start + HALF] for start in range(0, 4 * HALF, HALF)]
    )
    shards = tuple(text_weights[place] for place in matrix_places)
    image_low, vectors, others = image_kernel(image_tokens, image_weights, shard_vector, shards)
    grads, packed, token_grad = text_kernel(
        text_tokens, vectors, image_low, pair_counts, log_scale, shards, others
    )
    *final_grads, scale_total, loss_total = finish_kernel(grads, packed)
    return (*final_grads, scale_total.reshape(1), token_grad, loss_total.reshape(1))


def solution(mesh):
    return jax.shard_map(
        on_device,
        mesh=mesh,
        in_specs=(
            P(("dp", "fsdp"), None),
            P(("dp", "fsdp"), None),
            P(),
            P(),
            P("fsdp"),
            P("fsdp"),
            P("fsdp", None),
            P("fsdp", None),
            P("fsdp"),
            P("fsdp"),
            P("fsdp"),
            P("fsdp", None),
            P("fsdp"),
            P("fsdp", None),
            P("fsdp"),
            P("fsdp"),
            P("fsdp"),
            P("fsdp", None),
            P(),
            P(),
            P(),
            P(),
            P(),
            P(),
            P(),
            P(),
            P(),
            P(),
            P(),
            P(),
            P(),
            P(),
        ),
        out_specs=(
            P("fsdp"),
            P("fsdp"),
            P("fsdp", None),
            P("fsdp", None),
            P("fsdp"),
            P("fsdp"),
            P("fsdp"),
            P("fsdp", None),
            P("fsdp"),
            P("fsdp", None),
            P("fsdp"),
            P("fsdp"),
            P("fsdp"),
            P("fsdp", None),
            P(),
            P(("dp", "fsdp"), None),
            P(),
        ),
        check_vma=False,
    )
```

```python
import jax
import jax.numpy as jnp
from jax import lax
from jax.experimental import pallas as pl
from jax.experimental.pallas import tpu as pltpu
from jax.sharding import PartitionSpec as P

HEADS = 12
HEAD_DIM = 64
TEXT_LEN = 16
IMAGE_LEN = 50
SLOTS = 36


EPSILON = 1e-06


def product(left_side, right_side):
    return jnp.dot(left_side, right_side, preferred_element_type=jnp.float32)


def contract_last(left_side, right_side):
    return lax.dot_general(
        left_side, right_side, (((1,), (1,)), ((), ())), preferred_element_type=jnp.float32
    )


def contract_first(left_side, right_side):
    return lax.dot_general(
        left_side, right_side, (((0,), (0,)), ((), ())), preferred_element_type=jnp.float32
    )


def layer_norm(values, gain_vector, offset):
    centred = values - jnp.mean(values, axis=-1, keepdims=True)
    variance = jnp.mean(centred * centred, axis=-1, keepdims=True)
    return centred * lax.rsqrt(variance + EPSILON) * gain_vector.astype(
        jnp.float32
    ) + offset.astype(jnp.float32)


def normalize(embedding):
    return embedding * lax.rsqrt(jnp.sum(embedding * embedding, axis=-1, keepdims=True) + EPSILON)


def forward_block(tokens, weights, length):
    (
        norm_gain,
        norm_offset,
        joint_weight,
        mixer_weight,
        mixer_bias,
        feed_gain,
        feed_offset,
        up_weight,
        up_bias,
        down_weight,
        down_bias,
        end_gain,
        end_offset,
        projection,
    ) = weights
    inputs = tokens.astype(jnp.float32)
    total_rows, model_width = inputs.shape
    seq_count = total_rows // length
    factor = HEAD_DIM ** (-0.5)
    normed = layer_norm(inputs, norm_gain, norm_offset).astype(jnp.bfloat16)
    triple = (
        product(normed, joint_weight)
        .astype(jnp.bfloat16)
        .reshape(seq_count, length, 3, HEADS, HEAD_DIM)
    )
    queries = triple[:, :, 0]
    keyset = triple[:, :, 1]
    valueset = triple[:, :, 2]
    scores = (
        jnp.einsum("sqhd,skhd->shqk", queries, keyset, preferred_element_type=jnp.float32) * factor
    )
    soft_weights = jax.nn.softmax(scores, axis=-1)
    soft_low = soft_weights.astype(jnp.bfloat16)
    attended = jnp.einsum("shqk,skhd->sqhd", soft_low, valueset, preferred_element_type=jnp.float32)
    attended = attended.reshape(total_rows, model_width).astype(jnp.bfloat16)
    residual = inputs + product(attended, mixer_weight) + mixer_bias.astype(jnp.float32)
    normed_two = layer_norm(residual, feed_gain, feed_offset).astype(jnp.bfloat16)
    pre_active = product(normed_two, up_weight) + up_bias.astype(jnp.float32)
    active = jax.nn.gelu(pre_active).astype(jnp.bfloat16)
    output = residual + product(active, down_weight) + down_bias.astype(jnp.float32)
    final_norm = layer_norm(output, end_gain, end_offset)
    pooled = jnp.mean(final_norm.reshape(seq_count, length, model_width), axis=1)
    embedding = product(pooled.astype(jnp.bfloat16), projection)
    unit_vector = normalize(embedding)
    kept_values = (
        inputs,
        normed,
        triple,
        soft_weights,
        soft_low,
        attended,
        residual,
        normed_two,
        pre_active,
        active,
        output,
        pooled,
        embedding,
    )
    return (unit_vector, kept_values)


def backward_block(kept_values, weights, unit_grad, length):
    (
        norm_gain,
        norm_offset,
        joint_weight,
        mixer_weight,
        mixer_bias,
        feed_gain,
        feed_offset,
        up_weight,
        up_bias,
        down_weight,
        down_bias,
        end_gain,
        end_offset,
        projection,
    ) = weights
    (
        inputs,
        normed,
        triple,
        soft_weights,
        soft_low,
        attended,
        residual,
        normed_two,
        pre_active,
        active,
        output,
        pooled,
        embedding,
    ) = kept_values
    total_rows, model_width = inputs.shape
    seq_count = total_rows // length
    factor = HEAD_DIM ** (-0.5)
    unused_unit, norm_back = jax.vjp(normalize, embedding)
    embed_grad = norm_back(unit_grad)[0].astype(jnp.bfloat16)
    pooled_grad = contract_last(embed_grad, projection)
    final_grad = jnp.broadcast_to(
        pooled_grad[:, None, :] / length, (seq_count, length, model_width)
    ).reshape(total_rows, model_width)
    unused_final, end_back = jax.vjp(
        layer_norm, output, end_gain.astype(jnp.float32), end_offset.astype(jnp.float32)
    )
    output_grad, endgain_grad, endoffset_grad = end_back(final_grad)
    down_low = output_grad.astype(jnp.bfloat16)
    downbias_grad = jnp.sum(output_grad, axis=0)
    active_grad = contract_last(down_low, down_weight)
    unused_active, gelu_back = jax.vjp(jax.nn.gelu, pre_active)
    pre_grad = gelu_back(active_grad)[0]
    upbias_grad = jnp.sum(pre_grad, axis=0)
    pre_low = pre_grad.astype(jnp.bfloat16)
    normed_grad = contract_last(pre_low, up_weight)
    unused_feed, feed_back = jax.vjp(
        layer_norm, residual, feed_gain.astype(jnp.float32), feed_offset.astype(jnp.float32)
    )
    residual_part, feedgain_grad, feedoffset_grad = feed_back(normed_grad)
    residual_grad = output_grad + residual_part
    mixbias_grad = jnp.sum(residual_grad, axis=0)
    mix_low = residual_grad.astype(jnp.bfloat16)
    attended_grad = contract_last(mix_low, mixer_weight).astype(jnp.bfloat16)
    attended_grad = attended_grad.reshape(seq_count, length, HEADS, HEAD_DIM)
    queries = triple[:, :, 0]
    keyset = triple[:, :, 1]
    valueset = triple[:, :, 2]
    soft_grad = jnp.einsum(
        "sqhd,skhd->shqk", attended_grad, valueset, preferred_element_type=jnp.float32
    )
    value_grad = jnp.einsum(
        "shqk,sqhd->skhd", soft_low, attended_grad, preferred_element_type=jnp.float32
    )
    score_grad = soft_weights * (
        soft_grad - jnp.sum(soft_weights * soft_grad, axis=-1, keepdims=True)
    )
    score_grad = score_grad.astype(jnp.bfloat16)
    query_grad = (
        jnp.einsum("shqk,skhd->sqhd", score_grad, keyset, preferred_element_type=jnp.float32)
        * factor
    )
    key_grad = (
        jnp.einsum("shqk,sqhd->skhd", score_grad, queries, preferred_element_type=jnp.float32)
        * factor
    )
    triple_grad = jnp.stack([query_grad, key_grad, value_grad], axis=2)
    triple_grad = triple_grad.reshape(total_rows, 3 * model_width).astype(jnp.bfloat16)
    first_grad = contract_last(triple_grad, joint_weight)
    unused_first, first_back = jax.vjp(
        layer_norm, inputs, norm_gain.astype(jnp.float32), norm_offset.astype(jnp.float32)
    )
    input_part, gain_grad, offset_grad = first_back(first_grad)
    input_grad = residual_grad + input_part
    factors = (
        (normed, triple_grad),
        (attended, mix_low),
        (normed_two, pre_low),
        (active, down_low),
        (pooled.astype(jnp.bfloat16), embed_grad),
    )
    vectors = (
        gain_grad,
        offset_grad,
        mixbias_grad,
        feedgain_grad,
        feedoffset_grad,
        upbias_grad,
        downbias_grad,
        endgain_grad,
        endoffset_grad,
    )
    return (factors, vectors, input_grad)


WIDTH = 768
HALF = 384
QUARTER = 192
SUB = 2
ROWS = QUARTER // SUB
PART = ROWS // 2
UNITS = 13
STEPS = UNITS * SUB
TILE = 256
POOL_ROWS = 128
VECTOR_ROWS = 16
PART_RING = 8
CORE_RING = 4
RING = 8
TOTAL_RING = 6
VECTOR_START = 24
TAIL = 9
MESH = pl.DeviceIdType.MESH


ROOT_SCALE = 0.125
PAIR = 128
CUT = -1e30
TEXT_GROUP = 128
CHUNK = 96
SLOT_ROWS = 40
NEAR = 8
GELU_ROOT = 0.7978845608028654
GELU_CUBE = 0.044715


def wide(values):
    return values.astype(jnp.float32)


def low(values):
    return values.astype(jnp.bfloat16)


def centred_scale(values):
    centred = values - jnp.mean(values, axis=-1, keepdims=True)
    variance = jnp.mean(centred * centred, axis=-1, keepdims=True)
    rate = lax.rsqrt(variance + EPSILON)
    return centred * rate, rate


def gelu_value(values):
    inner = GELU_ROOT * (values + GELU_CUBE * (values * values * values))
    half = 0.5 * values
    return half + half * jnp.tanh(inner)


def gelu_slope(values):
    square = values * values
    bend = jnp.tanh(GELU_ROOT * values * (1.0 + GELU_CUBE * square))
    inner_slope = GELU_ROOT * (1.0 + (3.0 * GELU_CUBE) * square)
    return 0.5 * (1.0 + bend) + 0.5 * values * (1.0 - bend * bend) * inner_slope


def norm_back(values, grad, gain):
    unit, rate = centred_scale(values)
    scaled = grad * gain
    mean = jnp.mean(scaled, axis=-1, keepdims=True)
    slope = jnp.mean(scaled * unit, axis=-1, keepdims=True)
    return rate * (scaled - mean - unit * slope), grad * unit


def column_sum(values):
    return jnp.sum(values, axis=0, keepdims=True)


def peers_of(dp, x):
    z, y, core = dp // 4, (dp // 2) % 2, dp % 2
    near = []
    for step in range(1, NEAR):
        flip_x, flip_y, flip_core = step % 2, (step // 2) % 2, step // 4
        other_y = y + flip_y - 2 * flip_y * y
        other_core = core + flip_core - 2 * flip_core * core
        other_x = x + flip_x - 2 * flip_x * x
        near.append((z * 4 + other_y * 2 + other_core, other_x))
    far = [(((z + step) % 4) * 4 + y * 2 + core, x) for step in range(1, 4)]
    return near, far


def text_body(
    token_ref,
    vector_ref,
    image_ref,
    count_ref,
    scale_ref,
    joint_own,
    mixer_own,
    up_own,
    down_own,
    project_own,
    joint_other,
    mixer_other,
    up_other,
    down_other,
    project_other,
    grad_hbm,
    vector_out,
    token_out,
    joint,
    mixer,
    up,
    down,
    project,
    normed,
    normed_two,
    attended,
    hidden,
    pooled_rows,
    embed_rows,
    down_rows,
    mix_rows,
    pre_rows,
    triple,
    residual,
    active_in,
    output,
    work,
    bias_rows,
    images,
    near_sums,
    far_sums,
    weight_sem,
    image_sem,
    near_sem,
    far_sem,
    a_vmem,
    b_vmem,
    vector_acc,
    core_out,
    part,
    core_in,
    x_in,
    y_in,
    end_in,
    mid_in,
    total,
    vector_core,
    vector_x,
    vector_y,
    vector_z,
    vector_sum,
    core_sems,
    x_sems,
    y_sems,
    end_sems,
    mid_sems,
    back_sems,
    wide_sems,
    twin_sems,
    own_sems,
    vector_sems,
):
    dp = lax.axis_index("dp")
    x = lax.axis_index("fsdp")
    z, y, core = dp // 4, (dp // 2) % 2, dp % 2
    near, far = peers_of(dp, x)
    x_peer, y_peer, core_peer = near[0], near[1], near[3]
    loads = []
    for index, (own_half, other_half, target) in enumerate(
        (
            (joint_own, joint_other, joint),
            (mixer_own, mixer_other, mixer),
            (up_own, up_other, up),
            (down_own, down_other, down),
            (project_own, project_other, project),
        )
    ):
        half = own_half.shape[0]
        pair = []
        for side, (source, place) in enumerate(((own_half, x), (other_half, 1 - x))):
            piece = target.at[pl.ds(pl.multiple_of(place * half, half), half)]
            pair.append(pltpu.make_async_copy(source, piece, weight_sem.at[index, side]))
        loads.append(pair)
    for pair in loads:
        for load in pair:
            load.start()

    def loaded(index):
        for load in loads[index]:
            load.wait()

    barrier = pltpu.get_barrier_semaphore()
    for peer in near + far:
        pl.semaphore_signal(barrier, inc=1, device_id=peer, device_id_type=MESH)

    def send(source, target, sems, index, peer):
        return pltpu.make_async_remote_copy(
            src_ref=source,
            dst_ref=target,
            send_sem=sems.at[0, index],
            recv_sem=sems.at[1, index],
            device_id=peer,
            device_id_type=MESH,
        )

    own_slot = images.at[core, y, x, z]
    z_sends = [send(own_slot, own_slot, image_sem, k, far[k]) for k in range(3)]
    line = images.at[core, y, x]
    y_send = send(line, line, image_sem, 3, y_peer)
    x_send = send(line, line, image_sem, 4, x_peer)
    other_line = images.at[core, 1 - y, x, pl.ds(0, 2)]
    x_again = send(other_line, other_line, image_sem, 5, x_peer)
    cross_line = images.at[core, y, 1 - x, pl.ds(2, 2)]
    y_again = send(cross_line, cross_line, image_sem, 7, y_peer)
    plane = images.at[core]
    core_send = send(plane, plane, image_sem, 6, core_peer)

    rows, width = token_ref.shape
    feed = up.shape[1]
    seqs = rows // TEXT_LEN

    def vector(index):
        return wide(
            jnp.concatenate(
                [vector_ref[0, index : index + 1], vector_ref[1, index : index + 1]], axis=1
            )
        )

    def span(index, size):
        return pl.ds(pl.multiple_of(index * size, size), size)

    gain, offset, mix_bias, feed_gain, feed_offset, down_bias, end_gain, end_offset = (
        vector(index) for index in range(8)
    )
    images[core, y, x, z] = image_ref[...]
    column = lax.broadcasted_iota(jnp.int32, (1, 32 * SLOT_ROWS), 1)
    limit = jnp.zeros(column.shape, jnp.int32)
    for slot in range(32):
        slot_core, slot_y, slot_x, slot_z = slot // 16, (slot // 8) % 2, (slot // 4) % 2, slot % 4
        owner = (slot_z * 4 + slot_y * 2 + slot_core) * 2 + slot_x
        limit = jnp.where(
            (column >= slot * SLOT_ROWS) & (column < (slot + 1) * SLOT_ROWS),
            slot * SLOT_ROWS + count_ref[owner],
            limit,
        )
    live = jnp.where(column < limit, 1.0, 0.0)
    own_limit = count_ref[dp * 2 + x]
    own_live = jnp.where(
        lax.broadcasted_iota(jnp.int32, (rows // TEXT_LEN, 1), 0) < own_limit, 1.0, 0.0
    )

    normed[...] = low(centred_scale(wide(token_ref[...]))[0] * gain + offset)
    loaded(0)
    pl.semaphore_wait(barrier, 10)
    for copy in z_sends:
        copy.start()

    def tiles(base):
        for index in range(width // TILE):
            yield pl.ds(base + index * TILE, TILE)

    for index in range(3):
        for cols in tiles(index * width):
            values = product(normed[...], joint[:, cols])
            triple[:, cols] = low(values * ROOT_SCALE if index == 0 else values)

    lane = lax.broadcasted_iota(jnp.int32, (1, PAIR), 1)
    sides = (
        low(jnp.where(lane < HEAD_DIM, 1.0, 0.0)),
        low(jnp.where(lane < HEAD_DIM, 0.0, 1.0)),
    )
    counters = [jnp.broadcast_to(side, (TEXT_GROUP, PAIR)) for side in sides]
    pairs = width // PAIR
    tail_rows = rows % TEXT_GROUP
    tail_start = rows - tail_rows

    def same_of(count):
        row = lax.broadcasted_iota(jnp.int32, (count, TEXT_GROUP), 0) + (TEXT_GROUP - count)
        col = lax.broadcasted_iota(jnp.int32, (count, TEXT_GROUP), 1)
        return jnp.where(row // TEXT_LEN == col // TEXT_LEN, 0.0, CUT)

    def head_parts(values):
        return [values[:, head * TEXT_GROUP : (head + 1) * TEXT_GROUP] for head in range(2)]

    def scores_of(query, keys, same):
        both = jnp.concatenate([keys * side for side in sides], axis=0)
        softs = []
        for score in head_parts(contract_last(query, both)):
            score = score + same
            softs.append(jnp.exp(score - jnp.max(score, axis=-1, keepdims=True)))
        return both, softs

    def attend(group, key_group, same, pair):
        cols = pl.ds(pair * PAIR, PAIR)
        keys = triple[key_group, pl.ds(width + pair * PAIR, PAIR)]
        values = triple[key_group, pl.ds(2 * width + pair * PAIR, PAIR)]
        both, softs = scores_of(triple[group, cols], keys, same)
        spread = jnp.concatenate(
            [
                jnp.concatenate([values * side, counter], axis=1)
                for side, counter in zip(sides, counters)
            ],
            axis=0,
        )
        mixed = product(low(jnp.concatenate(softs, axis=1)), spread)
        attended[group, cols] = low(mixed[:, :PAIR] / mixed[:, PAIR:])

    tail_group = pl.ds(tail_start, tail_rows)
    tail_keys = pl.ds(rows - TEXT_GROUP, TEXT_GROUP)
    same_full = same_of(TEXT_GROUP)
    same_tail = same_of(tail_rows) if tail_rows else None
    for index in range(rows // TEXT_GROUP):
        group = pl.ds(index * TEXT_GROUP, TEXT_GROUP)
        for pair in range(pairs):
            attend(group, group, same_full, pair)
    if tail_rows:
        for pair in range(pairs):
            attend(tail_group, tail_keys, same_tail, pair)

    loaded(1)
    for cols in tiles(0):
        residual[:, cols] = product(attended[...], mixer[:, cols])
    values = wide(token_ref[...]) + residual[...] + mix_bias
    residual[...] = values
    normed_two[...] = low(centred_scale(values)[0] * feed_gain + feed_offset)
    for copy in z_sends:
        copy.wait()
    x_send.start()
    y_send.start()
    loaded(2)
    for index in range(8):
        bias_rows[0:1, index * HALF : (index + 1) * HALF] = wide(
            vector_ref[index // 4, 8 + index % 4 : 9 + index % 4]
        )

    for index in range(feed // width):
        for cols in tiles(index * width):
            values = product(normed_two[...], up[:, cols])
            values = values + bias_rows[0:1, cols]
            active_in[:, cols] = values
            hidden[:, cols] = low(gelu_value(values))

    x_send.wait()
    y_send.wait()
    x_again.start()
    y_again.start()
    loaded(3)
    for cols in tiles(0):
        output[:, cols] = product(hidden[...], down[:, cols])

    x_again.wait()
    y_again.wait()
    core_send.start()
    values = residual[...] + output[...] + down_bias
    output[...] = values
    pooled = jnp.sum(centred_scale(values)[0].reshape(seqs, TEXT_LEN, width), axis=1)
    pooled = low(pooled * (1.0 / TEXT_LEN) * end_gain + end_offset)
    loaded(4)
    embedding = product(pooled, project[...])
    length_rate = lax.rsqrt(jnp.sum(embedding * embedding, axis=-1, keepdims=True) + EPSILON)
    text_unit = embedding * length_rate
    text_low = low(text_unit)
    core_send.wait()

    every = images[...].reshape(2 * 2 * 2 * 4 * SLOT_ROWS, width)
    temper = jnp.exp(jnp.full((1, 1), scale_ref[0], jnp.float32))
    live_total = jnp.sum(live, axis=1, keepdims=True)
    half_inverse = 0.5 / live_total
    cosine = contract_last(text_low, every)
    scaled = jnp.exp(temper * cosine - temper)
    row_sum = jnp.sum(scaled * live, axis=1, keepdims=True)
    near_place = x + 2 * y + 4 * core
    near_sums[near_place] = column_sum(scaled * own_live)
    near_sends = [
        send(near_sums.at[near_place], near_sums.at[near_place], near_sem, k, near[k])
        for k in range(NEAR - 1)
    ]
    for copy in near_sends:
        copy.start()
    image_own = wide(image_ref[:seqs])
    diagonal_cos = jnp.sum(wide(text_low) * image_own, axis=1, keepdims=True)
    row_part = scaled * (own_live / row_sum) * live
    for copy in near_sends:
        copy.wait()
    far_sums[z] = (
        ((near_sums[0] + near_sums[1]) + (near_sums[2] + near_sums[3]))
        + ((near_sums[4] + near_sums[5]) + (near_sums[6] + near_sums[7]))
    )
    far_sends = [
        send(far_sums.at[z], far_sums.at[z], far_sem, k, far[k]) for k in range(3)
    ]
    for copy in far_sends:
        copy.start()
    for copy in far_sends:
        copy.wait()
    columns = (far_sums[0] + far_sums[1]) + (far_sums[2] + far_sums[3])
    coupling = (row_part + scaled * own_live * (live / columns)) * half_inverse
    column_log = jnp.where(live > 0.0, temper + jnp.log(columns), 0.0)
    row_log = temper + jnp.log(row_sum)
    loss_own = column_sum(own_live * (row_log - 2.0 * temper * diagonal_cos))
    loss_shared = jnp.sum(live * column_log, axis=1, keepdims=True)
    devices = lax.axis_size("dp") * lax.axis_size("fsdp")
    loss_part = (loss_own + loss_shared * (1.0 / devices)) * half_inverse
    temper_grad = (
        jnp.sum(column_sum(coupling * cosine), axis=1, keepdims=True)
        - column_sum(own_live * diagonal_cos) / live_total
    )
    unit_grad = product(low(temper * coupling), every)
    unit_grad = unit_grad - (temper / live_total) * own_live * image_own
    embed_grad = low(
        (unit_grad - text_unit * jnp.sum(text_unit * unit_grad, axis=-1, keepdims=True))
        * length_rate
    )
    at_end = (z == 0) | (z == 3)
    at_mid = (z == 1) | (z == 2)
    pair_peer = ((z + 1 - 2 * (z % 2)) * 4 + y * 2 + core, x)
    mid_peer = ((3 - z) * 4 + y * 2 + core, x)

    def remote(source, target, sems, index, peer):
        return pltpu.make_async_remote_copy(
            src_ref=source,
            dst_ref=target,
            send_sem=sems.at[0, index],
            recv_sem=sems.at[1, index],
            device_id=peer,
            device_id_type=MESH,
        )

    def core_copy(step):
        return remote(core_out.at[step % 2], core_in.at[step % CORE_RING], core_sems, step, core_peer)

    def x_copy(step):
        return remote(part.at[step % PART_RING, 1 - x], x_in.at[step % RING], x_sems, step, x_peer)

    def y_copy(step):
        rows = pl.ds(pl.multiple_of((1 - y) * PART, PART), PART)
        return remote(part.at[step % PART_RING, x, rows], y_in.at[step % RING], y_sems, step, y_peer)

    def own_rows():
        return pl.ds(pl.multiple_of(y * PART, PART), PART)

    def end_copy(step):
        return remote(part.at[step % PART_RING, x, own_rows()], end_in.at[step % RING], end_sems, step, pair_peer)

    def mid_copy(step):
        return remote(part.at[step % PART_RING, x, own_rows()], mid_in.at[step % RING], mid_sems, step, mid_peer)

    def own_piece(step):
        return grad_hbm.at[step, core, own_rows()]

    def back_copy(step):
        return remote(total.at[step % TOTAL_RING], own_piece(step), back_sems, step, pair_peer)

    def wide_copy(step, source):
        return remote(source, own_piece(step), wide_sems, step, y_peer)

    def own_copy(step):
        return pltpu.make_async_copy(total.at[step % TOTAL_RING], own_piece(step), own_sems.at[step])

    def twin_copy(step):
        piece = grad_hbm.at[step, core]
        return remote(piece, piece, twin_sems, step, core_peer)

    vector_first = remote(vector_acc, vector_core, vector_sems, 0, core_peer)
    vector_second = remote(vector_sum.at[0], vector_x, vector_sems, 1, x_peer)
    vector_third = remote(vector_sum.at[1], vector_y, vector_sems, 2, y_peer)
    vector_last = []
    for step in range(1, 4):
        other = ((z + step) % 4) * 4 + y * 2 + core
        vector_last.append(
            remote(vector_sum.at[2], vector_z.at[step - 1], vector_sems, 2 + step, (other, x))
        )

    def tick(time):
        @pl.when((time >= 1) & (time - 1 < STEPS))
        def _():
            step = time - 1
            core_copy(step).wait()
            part[step % PART_RING, 1 - x] = low(wide(part[step % PART_RING, 1 - x]) + wide(core_in[step % CORE_RING, 1 - x]))
            x_copy(step).start()
            part[step % PART_RING, x] = low(wide(part[step % PART_RING, x]) + wide(core_in[step % CORE_RING, x]))

        @pl.when(time < STEPS)
        def _():
            step = time
            unit = step // SUB
            half = step % SUB
            fresh = half == 0

            @pl.when(fresh & (unit == 0))
            def _():
                a_vmem[...] = jnp.zeros(a_vmem.shape, jnp.bfloat16)
                a_vmem[:, :POOL_ROWS] = pooled_rows[...].T
                b_vmem[...] = jnp.zeros(b_vmem.shape, jnp.bfloat16)
                b_vmem[:POOL_ROWS] = embed_rows[...]

            @pl.when(fresh & (unit >= 1) & (unit <= 4))
            def _():
                block = unit - 1
                for side in range(2):
                    cols = pl.ds(pl.multiple_of(side * 2 * width + block * HALF, HALF), HALF)
                    a_vmem[pl.ds(side * HALF, HALF)] = hidden[:, cols].T

            @pl.when(fresh & (unit == 1))
            def _():
                b_vmem[...] = down_rows[...]

            @pl.when(fresh & (unit == 5))
            def _():
                a_vmem[...] = normed_two[...].T

            @pl.when(fresh & (unit >= 5) & (unit <= 8))
            def _():
                b_vmem[...] = pre_rows[:, span(unit - 5, width)]

            @pl.when(fresh & (unit == 9))
            def _():
                a_vmem[...] = attended[...].T
                b_vmem[...] = mix_rows[...]

            @pl.when(fresh & (unit == 10))
            def _():
                a_vmem[...] = normed[...].T

            @pl.when(fresh & (unit >= 10))
            def _():
                b_vmem[...] = triple[:, span(unit - 10, width)]

            term = b_vmem[...]
            for which in range(2):
                rows = pl.ds(
                    pl.multiple_of(which * HALF + (1 - core) * QUARTER + half * ROWS, ROWS), ROWS
                )
                core_out[step % 2, which] = low(product(a_vmem[rows], term))
            core_copy(step).start()
            for which in range(2):
                rows = pl.ds(
                    pl.multiple_of(which * HALF + core * QUARTER + half * ROWS, ROWS), ROWS
                )
                part[step % PART_RING, which] = low(product(a_vmem[rows], term))

        @pl.when((time >= 3) & (time - 3 < STEPS))
        def _():
            step = time - 3
            x_copy(step).wait()
            rows = pl.ds(pl.multiple_of((1 - y) * PART, PART), PART)
            part[step % PART_RING, x, rows] = low(wide(part[step % PART_RING, x, rows]) + wide(x_in[step % RING, rows]))
            y_copy(step).start()
            part[step % PART_RING, x, own_rows()] = low(
                wide(part[step % PART_RING, x, own_rows()]) + wide(x_in[step % RING, own_rows()])
            )

        @pl.when((time >= 4) & (time - 4 < STEPS))
        def _():
            step = time - 4
            y_copy(step).wait()
            part[step % PART_RING, x, own_rows()] = low(
                wide(part[step % PART_RING, x, own_rows()]) + wide(y_in[step % RING])
            )

            @pl.when(at_end)
            def _():
                end_copy(step).start()

        @pl.when((time >= 5) & (time - 5 < STEPS))
        def _():
            step = time - 5

            @pl.when(at_end)
            def _():
                end_copy(step).wait_send()

            @pl.when(at_mid)
            def _():
                end_copy(step).wait_recv()
                part[step % PART_RING, x, own_rows()] = low(
                    wide(part[step % PART_RING, x, own_rows()]) + wide(end_in[step % RING])
                )
                mid_copy(step).start()

        @pl.when((time >= 6) & (time - 6 < STEPS) & at_mid)
        def _():
            step = time - 6
            mid_copy(step).wait()
            total[step % TOTAL_RING] = low(
                wide(part[step % PART_RING, x, own_rows()]) + wide(mid_in[step % RING])
            )
            back_copy(step).start()
            wide_copy(step, total.at[step % TOTAL_RING]).start()
            own_copy(step).start()

        @pl.when((time >= 7) & (time - 7 < STEPS))
        def _():
            step = time - 7

            @pl.when(at_end)
            def _():
                back_copy(step).wait_recv()
                wide_copy(step, own_piece(step)).start()

            @pl.when(at_mid)
            def _():
                back_copy(step).wait_send()

        @pl.when((time >= 8) & (time - 8 < STEPS))
        def _():
            step = time - 8
            wide_copy(step, total.at[step % TOTAL_RING]).wait()

            @pl.when(at_mid)
            def _():
                own_copy(step).wait()

            twin_copy(step).start()

        @pl.when((time >= 9) & (time - 9 < STEPS))
        def _():
            step = time - 9
            twin_copy(step).wait()

        @pl.when(time == VECTOR_START + 0)
        def _():
            vector_first.start()

        @pl.when(time == VECTOR_START + 1)
        def _():
            vector_first.wait()
            vector_sum[0] = vector_acc[...] + vector_core[...]
            vector_second.start()

        @pl.when(time == VECTOR_START + 3)
        def _():
            vector_second.wait()
            vector_sum[1] = vector_sum[0] + vector_x[...]
            vector_third.start()

        @pl.when(time == VECTOR_START + 5)
        def _():
            vector_third.wait()
            vector_sum[2] = vector_sum[1] + vector_y[...]
            for copy in vector_last:
                copy.start()

        @pl.when(time == VECTOR_START + 7)
        def _():
            for copy in vector_last:
                copy.wait()
            order = lax.broadcasted_iota(jnp.int32, (VECTOR_ROWS, WIDTH), 0) * 0 + z
            own = vector_sum[2]
            before_one = vector_z[0]
            before_two = vector_z[1]
            before_three = vector_z[2]

            def pick(where):
                shift = (order - where + 4) % 4
                return jnp.where(
                    shift == 0,
                    own,
                    jnp.where(
                        shift == 1,
                        before_one,
                        jnp.where(shift == 2, before_two, before_three),
                    ),
                )

            vector_out[...] = (pick(0) + pick(1)) + (pick(2) + pick(3))

    pooled_rows[...] = jnp.zeros(pooled_rows.shape, jnp.bfloat16)
    pooled_rows[:SLOT_ROWS] = jnp.pad(pooled, ((0, SLOT_ROWS - seqs), (0, 0)))
    embed_rows[...] = jnp.zeros(embed_rows.shape, jnp.bfloat16)
    embed_rows[:SLOT_ROWS] = jnp.pad(embed_grad, ((0, SLOT_ROWS - seqs), (0, 0)))
    pooled_grad = contract_last(embed_grad, project[...]) * (1.0 / TEXT_LEN)
    pl.loop(0, 2)(tick)
    for index in range(rows // CHUNK):
        work[index * 8 : index * 8 + CHUNK // TEXT_LEN] = pooled_grad[
            index * (CHUNK // TEXT_LEN) : (index + 1) * (CHUNK // TEXT_LEN)
        ]

    vector_acc[...] = jnp.zeros(vector_acc.shape, jnp.float32)
    column = lax.broadcasted_iota(jnp.int32, (1, width), 1)
    vector_acc[12:13] = jnp.where(
        column == 0, loss_part, jnp.where(column == 1, temper * temper_grad, 0.0)
    )
    vector_acc[11:12] = column_sum(pooled_grad) * float(TEXT_LEN)

    def gather(index, value):
        vector_acc[index : index + 1] = vector_acc[index : index + 1] + value

    @pl.loop(0, rows // CHUNK)
    def _(index):
        chunk = span(index, CHUNK)
        grad = work[span(index, 8)][: CHUNK // TEXT_LEN]
        grad = jnp.broadcast_to(
            grad[:, None, :], (CHUNK // TEXT_LEN, TEXT_LEN, width)
        ).reshape(CHUNK, width)
        value, gain_part = norm_back(output[chunk], grad, end_gain)
        output[chunk] = value
        down_rows[chunk] = low(value)
        gather(10, column_sum(gain_part))
        gather(9, column_sum(value))

    @pl.loop(0, 6)
    def _(index):
        tick(2 + index)
        for side in range(2):
            cols = pl.ds(pl.multiple_of(index * (2 * TILE) + side * TILE, TILE), TILE)
            values = contract_last(down_rows[...], down[cols]) * gelu_slope(active_in[:, cols])
            pre_rows[:, cols] = low(values)
            bias_rows[:, cols] = jnp.sum(values.reshape(rows // 8, 8, TILE), axis=0)

    @pl.loop(0, 3)
    def _(index):
        tick(8 + index)
        cols = span(index, TILE)
        active_in[:, cols] = contract_last(pre_rows[...], up[cols])

    @pl.loop(0, 2)
    def _(half):
        tick(11 + half)

        @pl.loop(0, 3)
        def _(inner):
            chunk = span(half * 3 + inner, CHUNK)
            grad = active_in[chunk, :width]
            value, gain_part = norm_back(residual[chunk], grad, feed_gain)
            value = value + output[chunk]
            output[chunk] = value
            mix_rows[chunk] = low(value)
            gather(3, column_sum(gain_part))
            gather(4, column_sum(grad))
            gather(2, column_sum(value))

    tick(13)
    for index in range(width // TILE):
        active_in[:, pl.ds(width + index * TILE, TILE)] = contract_last(
            mix_rows[...], mixer[pl.ds(index * TILE, TILE)]
        )

    def attend_back(group, key_group, same, pair, count):
        cols = pl.ds(pair * PAIR, PAIR)
        key_cols = pl.ds(width + pair * PAIR, PAIR)
        value_cols = pl.ds(2 * width + pair * PAIR, PAIR)
        query = triple[group, cols]
        values = triple[key_group, value_cols]
        both, softs = scores_of(query, triple[key_group, key_cols], same)
        outer = low(active_in[group, pl.ds(width + pair * PAIR, PAIR)])
        grads = head_parts(
            contract_last(outer, jnp.concatenate([values * side for side in sides], axis=0))
        )
        lows, score_grads = [], []
        for soft, grad in zip(softs, grads):
            soft = soft / jnp.sum(soft, axis=-1, keepdims=True)
            lows.append(low(soft))
            score_grads.append(
                low(soft * (grad - jnp.sum(soft * grad, axis=-1, keepdims=True)))
            )
        score_grad = jnp.concatenate(score_grads, axis=1)
        left_lane = lax.broadcasted_iota(jnp.int32, (count, PAIR), 1) < HEAD_DIM

        def joined(stacked):
            top = stacked[TEXT_GROUP - count : TEXT_GROUP]
            bottom = stacked[2 * TEXT_GROUP - count :]
            return low(jnp.where(left_lane, top, bottom))

        triple[group, key_cols] = joined(contract_first(score_grad, query))
        triple[group, cols] = low(product(score_grad, both) * ROOT_SCALE)
        triple[group, value_cols] = joined(
            contract_first(jnp.concatenate(lows, axis=1), outer)
        )

    @pl.loop(0, rows // TEXT_GROUP)
    def _(index):
        tick(14 + index)
        group = span(index, TEXT_GROUP)
        for pair in range(pairs):
            attend_back(group, group, same_full, pair, TEXT_GROUP)

    tick(18)
    if tail_rows:
        for pair in range(pairs):
            attend_back(tail_group, tail_keys, same_tail, pair, tail_rows)

    @pl.loop(0, 3)
    def _(index):
        tick(19 + index)
        cols = span(index, TILE)
        active_in[:, cols] = contract_last(triple[...], joint[cols])

    @pl.loop(0, 2)
    def _(half):
        tick(22 + half)

        @pl.loop(0, 3)
        def _(inner):
            chunk = span(half * 3 + inner, CHUNK)
            grad = active_in[chunk, :width]
            value, gain_part = norm_back(wide(token_ref[chunk]), grad, gain)
            token_out[chunk] = value + output[chunk]
            gather(0, column_sum(gain_part))
            gather(1, column_sum(grad))

    for index in range(feed // width):
        vector_acc[5 + index : 6 + index] = column_sum(
            bias_rows[:, index * width : (index + 1) * width]
        )
    pl.loop(24, STEPS + TAIL + 1)(tick)


def text_kernel(tokens, vectors, image_low, pair_counts, log_scale, shards, others):
    rows, width = tokens.shape
    feed = shards[2].shape[1]
    any_spec = pl.BlockSpec(memory_space=pl.ANY)
    vmem_spec = pl.BlockSpec(memory_space=pltpu.VMEM)
    dma = pltpu.SemaphoreType.DMA
    low_type = jnp.bfloat16
    smem_spec = pl.BlockSpec(memory_space=pltpu.SMEM)
    slots = 2 * 2 * 2 * 4 * SLOT_ROWS
    return pl.pallas_call(
        text_body,
        out_shape=(
            jax.ShapeDtypeStruct((STEPS, 2, ROWS, width), low_type),
            jax.ShapeDtypeStruct((VECTOR_ROWS, width), jnp.float32),
            jax.ShapeDtypeStruct((rows, width), jnp.float32),
        ),
        in_specs=[vmem_spec] * 3 + [smem_spec] * 2 + [any_spec] * 10,
        out_specs=(any_spec, vmem_spec, vmem_spec),
        scratch_shapes=[
            pltpu.VMEM((2 * shard.shape[0], shard.shape[1]), low_type) for shard in shards
        ]
        + [
            pltpu.VMEM((rows, width), low_type),
            pltpu.VMEM((rows, width), low_type),
            pltpu.VMEM((rows, width), low_type),
            pltpu.VMEM((rows, feed), low_type),
            pltpu.VMEM((POOL_ROWS, width), low_type),
            pltpu.VMEM((POOL_ROWS, width), low_type),
            pltpu.VMEM((rows, width), low_type),
            pltpu.VMEM((rows, width), low_type),
            pltpu.VMEM((rows, feed), low_type),
            pltpu.VMEM((rows, 3 * width), low_type),
            pltpu.VMEM((rows, width), jnp.float32),
            pltpu.VMEM((rows, feed), jnp.float32),
            pltpu.VMEM((rows, width), jnp.float32),
            pltpu.VMEM((rows // CHUNK * 8, width), jnp.float32),
            pltpu.VMEM((8, feed), jnp.float32),
            pltpu.VMEM((2, 2, 2, 4, SLOT_ROWS, width), low_type),
            pltpu.VMEM((NEAR, 1, slots), jnp.float32),
            pltpu.VMEM((4, 1, slots), jnp.float32),
            dma((5, 2)),
            dma((2, 8)),
            dma((2, NEAR - 1)),
            dma((2, 3)),
            pltpu.VMEM((width, rows), low_type),
            pltpu.VMEM((rows, width), low_type),
            pltpu.VMEM((VECTOR_ROWS, width), jnp.float32),
            pltpu.VMEM((2, 2, ROWS, width), low_type),
            pltpu.VMEM((PART_RING, 2, ROWS, width), low_type),
            pltpu.VMEM((CORE_RING, 2, ROWS, width), low_type),
            pltpu.VMEM((RING, ROWS, width), low_type),
            pltpu.VMEM((RING, PART, width), low_type),
            pltpu.VMEM((RING, PART, width), low_type),
            pltpu.VMEM((RING, PART, width), low_type),
            pltpu.VMEM((TOTAL_RING, PART, width), low_type),
            pltpu.VMEM((VECTOR_ROWS, width), jnp.float32),
            pltpu.VMEM((VECTOR_ROWS, width), jnp.float32),
            pltpu.VMEM((VECTOR_ROWS, width), jnp.float32),
            pltpu.VMEM((3, VECTOR_ROWS, width), jnp.float32),
            pltpu.VMEM((3, VECTOR_ROWS, width), jnp.float32),
        ]
        + [dma((2, STEPS)) for _ in range(8)]
        + [
            dma((STEPS,)),
            dma((2, 6)),
        ],
        compiler_params=pltpu.CompilerParams(
            collective_id=1, has_side_effects=True, vmem_limit_bytes=62 * 1024 * 1024
        ),
    )(tokens, vectors, image_low, pair_counts, log_scale, *shards, *others)


def pack_rows(vectors):
    index = lax.broadcasted_iota(jnp.int32, (VECTOR_ROWS, vectors[0].shape[0]), 0)
    packed = jnp.zeros(index.shape, vectors[0].dtype)
    for row, vector in enumerate(vectors):
        packed = jnp.where(index == row, vector[None, :], packed)
    return packed


IMAGE_GROUP = 4
IMAGE_BLOCK = 12
IMAGE_ROWS = 104
IMAGE_KEYS = 128


def image_body(
    token_ref,
    vector_ref,
    shard_vector,
    joint_hbm,
    mixer_hbm,
    up_hbm,
    down_hbm,
    project_hbm,
    joint_shard,
    mixer_shard,
    up_shard,
    down_shard,
    project_shard,
    image_out,
    vector_out,
    joint_other,
    mixer_other,
    up_other,
    down_other,
    project_other,
    joint,
    mixer,
    up,
    down,
    project,
    normed,
    normed_two,
    triple,
    attended,
    residual,
    final,
    hidden,
    pooled,
    load_sem,
    x_sem,
    y_sem,
    z_sem,
    core_sem,
):
    dp = lax.axis_index("dp")
    x = lax.axis_index("fsdp")
    zb, y, core = (dp // 4) % 2, (dp // 2) % 2, dp % 2
    x_peer, y_peer, core_peer = (dp, 1 - x), (dp + 2 - 4 * y, x), (dp + 1 - 2 * core, x)
    z_peer = (dp + 4 - 8 * zb, x)
    loads = [
        pltpu.make_async_copy(source, target, load_sem.at[index])
        for index, (source, target) in enumerate(
            (
                (joint_hbm, joint),
                (mixer_hbm, mixer),
                (up_hbm, up),
                (down_hbm, down),
                (project_hbm, project),
            )
        )
    ]
    for load in loads:
        load.start()
    barrier = pltpu.get_barrier_semaphore()
    for peer in (x_peer, y_peer, z_peer, core_peer):
        pl.semaphore_signal(barrier, inc=1, device_id=peer, device_id_type=MESH)
    vector_out[x] = shard_vector[...]
    pl.semaphore_wait(barrier, 4)

    def send(source, target, sems, index, peer):
        return pltpu.make_async_remote_copy(
            src_ref=source,
            dst_ref=target,
            send_sem=sems.at[0, index],
            recv_sem=sems.at[1, index],
            device_id=peer,
            device_id_type=MESH,
        )

    shards = (joint_shard, mixer_shard, up_shard, down_shard, project_shard)
    others = (joint_other, mixer_other, up_other, down_other, project_other)
    x_sends, x_cross, y_sends, z_sends, core_sends, core_cross = [], [], [], [], [], []
    for index, (shard, other) in enumerate(zip(shards, others)):
        size = shard.shape[0] // 8

        def rows_of(piece):
            return pl.ds(pl.multiple_of(piece * size, size), size)

        own = rows_of(core * 4 + y * 2 + zb)
        beside_y = rows_of(core * 4 + (1 - y) * 2 + zb)
        beside_z = rows_of(core * 4 + y * 2 + 1 - zb)
        cross = rows_of(core * 4 + (1 - y) * 2 + 1 - zb)
        x_sends.append(send(shard.at[own], other.at[own], x_sem, index, x_peer))
        x_cross.append(send(shard.at[cross], other.at[cross], x_sem, 6 + index, x_peer))
        y_sends.append(send(other.at[own], other.at[own], y_sem, index, y_peer))
        z_sends.append(send(other.at[own], other.at[own], z_sem, index, z_peer))
        core_sends.append(
            [
                send(other.at[piece], other.at[piece], core_sem, 4 * index + place, core_peer)
                for place, piece in enumerate((own, beside_y, beside_z))
            ]
        )
        core_cross.append(
            send(other.at[cross], other.at[cross], core_sem, 4 * index + 3, core_peer)
        )
    vector_send = send(vector_out.at[x], vector_out.at[x], x_sem, 5, x_peer)
    vector_send.start()
    for index in (2, 3, 0, 1, 4):
        x_sends[index].start()
    for index in (2, 3, 0, 1, 4):
        x_cross[index].start()

    def pass_near(index):
        x_sends[index].wait()
        y_sends[index].start()
        z_sends[index].start()

    def pass_core(index):
        y_sends[index].wait()
        z_sends[index].wait()
        for copy in core_sends[index]:
            copy.start()

    def pass_cross(index):
        x_cross[index].wait()
        core_cross[index].start()

    blocks, rows, width = token_ref.shape
    feed = up.shape[1]
    gain, offset, mix_bias, feed_gain, feed_offset, down_bias, end_gain, end_offset = (
        wide(vector_ref[index : index + 1]) for index in range(8)
    )

    def span(index, size):
        return pl.ds(pl.multiple_of(index * size, 8), size)

    seqs = rows // IMAGE_LEN
    pool_row = lax.broadcasted_iota(jnp.int32, (seqs, rows), 0)
    pool_col = lax.broadcasted_iota(jnp.int32, (seqs, rows), 1) // IMAGE_LEN
    pool = low(jnp.where(pool_row == pool_col, 1.0, 0.0))
    group_rows = IMAGE_GROUP * IMAGE_LEN
    lane = lax.broadcasted_iota(jnp.int32, (1, PAIR), 1)
    sides = (
        low(jnp.where(lane < HEAD_DIM, 1.0, 0.0)),
        low(jnp.where(lane < HEAD_DIM, 0.0, 1.0)),
    )
    seam = lax.broadcasted_iota(jnp.int32, (8, PAIR), 0) < 4
    windows = []
    for row_start, key_start in (
        (0, 0),
        (group_rows - IMAGE_ROWS, group_rows - IMAGE_KEYS),
    ):
        row = lax.broadcasted_iota(jnp.int32, (IMAGE_ROWS, IMAGE_KEYS), 0) + row_start
        col = lax.broadcasted_iota(jnp.int32, (IMAGE_ROWS, IMAGE_KEYS), 1) + key_start
        same = jnp.where(row // IMAGE_LEN == col // IMAGE_LEN, 0.0, CUT)
        windows.append((row_start, key_start, same))
    counters = [jnp.broadcast_to(side, (IMAGE_KEYS, PAIR)) for side in sides]

    def attend(start, pair):
        cols = pair * PAIR
        parts = []
        for row_start, key_start, same in windows:
            query = triple[pl.ds(start + row_start, IMAGE_ROWS), pl.ds(cols, PAIR)]
            keys = triple[pl.ds(start + key_start, IMAGE_KEYS), pl.ds(width + cols, PAIR)]
            values = triple[pl.ds(start + key_start, IMAGE_KEYS), pl.ds(2 * width + cols, PAIR)]
            scores = contract_last(
                query, jnp.concatenate([keys * side for side in sides], axis=0)
            )
            softs = []
            for head in range(2):
                score = scores[:, head * IMAGE_KEYS : (head + 1) * IMAGE_KEYS] + same
                softs.append(low(jnp.exp(score - jnp.max(score, axis=-1, keepdims=True))))
            spread = jnp.concatenate(
                [
                    jnp.concatenate([values * side, counter], axis=1)
                    for side, counter in zip(sides, counters)
                ],
                axis=0,
            )
            mixed = product(jnp.concatenate(softs, axis=1), spread)
            parts.append(mixed[:, :PAIR] / mixed[:, PAIR:])
        first, second = parts
        edge = IMAGE_ROWS - 8
        attended[pl.ds(start, edge), pl.ds(cols, PAIR)] = low(first[:edge])
        attended[pl.ds(start + edge, 8), pl.ds(cols, PAIR)] = low(
            jnp.where(seam, first[edge:], second[:8])
        )
        attended[pl.ds(start + IMAGE_ROWS, edge), pl.ds(cols, PAIR)] = low(second[8:])

    pairs = width // PAIR
    groups = rows // group_rows

    def cols_of(index):
        return pl.ds(index * TILE, TILE)

    def first_norm(block):
        normed[...] = low(centred_scale(wide(token_ref[block]))[0] * gain + offset)

    def make_triple(index):
        cols = cols_of(index)
        values = product(normed[...], joint[:, cols])
        triple[:, cols] = low(values * ROOT_SCALE if index < 3 else values)

    def mix(block, index):
        cols = cols_of(index)
        residual[:, cols] = (
            wide(token_ref[block, :, cols])
            + product(attended[...], mixer[:, cols])
            + mix_bias[:, index * TILE : (index + 1) * TILE]
        )

    def second_norm():
        normed_two[...] = low(centred_scale(residual[...])[0] * feed_gain + feed_offset)

    def feed_up(index):
        cols = cols_of(index)
        row, start = 8 + index // 3, (index % 3) * TILE
        bias = wide(vector_ref[row : row + 1, start : start + TILE])
        hidden[:, cols] = low(gelu_value(product(normed_two[...], up[:, cols]) + bias))

    def feed_down(index):
        cols = cols_of(index)
        final[:, cols] = (
            residual[:, cols]
            + product(hidden[...], down[:, cols])
            + down_bias[:, index * TILE : (index + 1) * TILE]
        )

    def pool_rows(block):
        mean = product(pool, low(centred_scale(final[...])[0])) * (1.0 / IMAGE_LEN)
        pooled[block] = mean * end_gain + end_offset

    def attend_unit(unit):
        attend((unit // pairs) * group_rows, unit % pairs)

    units = groups * pairs

    first_norm(0)
    loads[0].wait()
    for index in range(9):
        make_triple(index)
    for unit in range(units):
        attend_unit(unit)
    loads[1].wait()
    loads[2].wait()
    loads[3].wait()
    pass_near(2)
    for index in range(3):
        mix(0, index)
    second_norm()
    for block in range(1, blocks):
        first_norm(block)
        for index in range(9):
            make_triple(index)
        if block == 1:
            pass_near(3)
        for unit in range(units):
            attend_unit(unit)
            if unit < 12:
                feed_up(unit)
            elif unit % 2 == 1:
                feed_down((unit - 12) // 2)
        if block == 1:
            pass_near(0)
            pass_near(1)
            pass_near(4)
            pass_core(2)
            pass_core(3)
        if block == 2:
            pass_core(0)
            pass_core(1)
            pass_core(4)
        for index in range(3):
            mix(block, index)
        pool_rows(block - 1)
        second_norm()

    for index in range(12):
        feed_up(index)
    for index in range(3):
        feed_down(index)
    for index in range(5):
        pass_cross(index)
    pool_rows(blocks - 1)
    loads[4].wait()
    rest = jnp.zeros((SLOT_ROWS - blocks * IMAGE_BLOCK, width), jnp.float32)
    means = jnp.concatenate([pooled[block] for block in range(blocks)] + [rest], axis=0)
    embedding = product(low(means), project[...])
    image_out[...] = low(
        embedding * lax.rsqrt(jnp.sum(embedding * embedding, axis=-1, keepdims=True) + EPSILON)
    )
    for copies, copy in zip(core_sends, core_cross):
        for near in copies:
            near.wait()
        copy.wait()
    vector_send.wait()


def image_kernel(tokens, weights, shard_vector, shards):
    (
        norm_gain,
        norm_offset,
        joint,
        mixer,
        mixer_bias,
        feed_gain,
        feed_offset,
        up,
        up_bias,
        down,
        down_bias,
        end_gain,
        end_offset,
        project,
    ) = weights
    total, width = tokens.shape
    rows = IMAGE_BLOCK * IMAGE_LEN
    blocks = total // rows
    feed = up.shape[1]
    vectors = pack_rows(
        [
            norm_gain,
            norm_offset,
            mixer_bias,
            feed_gain,
            feed_offset,
            down_bias,
            end_gain,
            end_offset,
        ]
        + [up_bias[start : start + width] for start in range(0, feed, width)],
    )
    any_spec = pl.BlockSpec(memory_space=pl.ANY)
    vmem_spec = pl.BlockSpec(memory_space=pltpu.VMEM)
    dma = pltpu.SemaphoreType.DMA
    low_type = jnp.bfloat16
    matrices = (joint, mixer, up, down, project)
    image_out, vector_out, *others = pl.pallas_call(
        image_body,
        out_shape=(
            jax.ShapeDtypeStruct((SLOT_ROWS, width), low_type),
            jax.ShapeDtypeStruct((2, *shard_vector.shape), low_type),
            *(
                jax.ShapeDtypeStruct(shard.shape, low_type)
                for shard in shards
            ),
        ),
        in_specs=[vmem_spec] * 3 + [any_spec] * 10,
        out_specs=(vmem_spec, vmem_spec, *([any_spec] * 5)),
        scratch_shapes=[pltpu.VMEM(matrix.shape, low_type) for matrix in matrices]
        + [
            pltpu.VMEM((rows, width), low_type),
            pltpu.VMEM((rows, width), low_type),
            pltpu.VMEM((rows, 3 * width), low_type),
            pltpu.VMEM((rows, width), low_type),
            pltpu.VMEM((rows, width), jnp.float32),
            pltpu.VMEM((rows, width), jnp.float32),
            pltpu.VMEM((rows, feed), low_type),
            pltpu.VMEM((blocks, IMAGE_BLOCK, width), jnp.float32),
            dma((5,)),
            dma((2, 11)),
            dma((2, 5)),
            dma((2, 5)),
            dma((2, 20)),
        ],
        compiler_params=pltpu.CompilerParams(
            collective_id=2, has_side_effects=True, vmem_limit_bytes=60 * 1024 * 1024
        ),
    )(
        tokens.reshape(blocks, rows, width),
        vectors,
        shard_vector,
        *matrices,
        *shards,
    )
    return image_out, vector_out, others


def finish_body(grad_hbm, packed_ref, *refs):
    (
        gain,
        offset,
        joint,
        mixer,
        mix_bias,
        feed_gain,
        feed_offset,
        up,
        up_bias,
        down,
        down_bias,
        end_gain,
        end_offset,
        project,
        scale_out,
        loss_out,
        low_values,
        wide_values,
        load_sem,
        store_sem,
    ) = refs
    shard = lax.axis_index("fsdp")
    loads = [
        pltpu.make_async_copy(
            grad_hbm.at[pl.ds(unit * SUB, SUB)],
            low_values.at[pl.ds(unit * SUB, SUB)],
            load_sem.at[unit],
        )
        for unit in range(UNITS)
    ]
    for load in loads:
        load.start()
    for row, target in (
        (0, gain),
        (1, offset),
        (2, mix_bias),
        (3, feed_gain),
        (4, feed_offset),
        (9, down_bias),
        (10, end_gain),
        (11, end_offset),
    ):
        cols = pl.ds(pl.multiple_of(shard * HALF, HALF), HALF)
        target[...] = packed_ref[pl.ds(row, 1), cols].reshape(HALF)
    for part in range(2):
        up_bias[pl.ds(part * WIDTH, WIDTH)] = packed_ref[
            pl.ds(5 + 2 * shard + part, 1), :
        ].reshape(WIDTH)
    loss_out[...] = packed_ref[12:13, 0:1]
    scale_out[...] = packed_ref[12:13, 1:2]
    places = (
        [(project, pl.ds(0, HALF), pl.ds(0, WIDTH))]
        + [(down, pl.ds(unit * HALF, HALF), pl.ds(0, WIDTH)) for unit in range(4)]
        + [(up, pl.ds(0, HALF), pl.ds(unit * WIDTH, WIDTH)) for unit in range(4)]
        + [(mixer, pl.ds(0, HALF), pl.ds(0, WIDTH))]
        + [(joint, pl.ds(0, HALF), pl.ds(unit * WIDTH, WIDTH)) for unit in range(3)]
    )
    stores = []
    for unit, (target, rows, cols) in enumerate(places):
        loads[unit].wait()
        for core in range(2):
            for half in range(SUB):
                rows_here = pl.ds(core * QUARTER + half * ROWS, ROWS)
                wide_values[unit, rows_here] = wide(low_values[unit * SUB + half, core])
        copy = pltpu.make_async_copy(wide_values.at[unit], target.at[rows, cols], store_sem.at[unit])
        copy.start()
        stores.append(copy)
    for copy in stores:
        copy.wait()


def finish_kernel(grads, packed):
    single = jnp.float32
    any_spec = pl.BlockSpec(memory_space=pl.ANY)
    vmem_spec = pl.BlockSpec(memory_space=pltpu.VMEM)
    vector = (jax.ShapeDtypeStruct((HALF,), single), vmem_spec)
    scalar = (jax.ShapeDtypeStruct((1, 1), single), vmem_spec)

    def matrix(rows, cols):
        return (jax.ShapeDtypeStruct((rows, cols), single), any_spec)

    outs = (
        vector,
        vector,
        matrix(HALF, 3 * WIDTH),
        matrix(HALF, WIDTH),
        vector,
        vector,
        vector,
        matrix(HALF, 4 * WIDTH),
        (jax.ShapeDtypeStruct((4 * HALF,), single), vmem_spec),
        matrix(4 * HALF, WIDTH),
        vector,
        vector,
        vector,
        matrix(HALF, WIDTH),
        scalar,
        scalar,
    )
    return pl.pallas_call(
        finish_body,
        out_shape=tuple(shape for shape, spec in outs),
        in_specs=[any_spec, vmem_spec],
        out_specs=tuple(spec for shape, spec in outs),
        scratch_shapes=[
            pltpu.VMEM((STEPS, 2, ROWS, WIDTH), jnp.bfloat16),
            pltpu.VMEM((UNITS, HALF, WIDTH), single),
            pltpu.SemaphoreType.DMA((UNITS,)),
            pltpu.SemaphoreType.DMA((UNITS,)),
        ],
        compiler_params=pltpu.CompilerParams(vmem_limit_bytes=48 * 1024 * 1024),
    )(grads, packed)


def reduce_plain(factors, vectors):
    terms = [contract_first(left, right) for left, right in factors]
    joint, mixer, upward, downward, project = terms
    gain, offset, mixbias, feedgain, feedoffset, upbias, downbias, endgain, endoffset = vectors
    ordered = (
        gain,
        offset,
        joint,
        mixer,
        mixbias,
        feedgain,
        feedoffset,
        upward,
        upbias,
        downward,
        downbias,
        endgain,
        endoffset,
        project,
    )
    shards = tuple(
        lax.psum_scatter(term, "fsdp", scatter_dimension=0, tiled=True) for term in ordered
    )
    return lax.psum(shards, "dp")


def on_device_plain(*arrays):
    (
        text_tokens,
        image_tokens,
        pair_counts,
        log_scale,
        text_gain,
        text_offset,
        text_joint,
        text_mixer,
        text_mixbias,
        text_feedgain,
        text_feedoffset,
        text_upward,
        text_upbias,
        text_downward,
        text_downbias,
        text_endgain,
        text_endoffset,
        text_project,
        image_gain,
        image_offset,
        image_joint,
        image_mixer,
        image_mixbias,
        image_feedgain,
        image_feedoffset,
        image_upward,
        image_upbias,
        image_downward,
        image_downbias,
        image_endgain,
        image_endoffset,
        image_project,
    ) = arrays
    image_weights = (
        image_gain,
        image_offset,
        image_joint,
        image_mixer,
        image_mixbias,
        image_feedgain,
        image_feedoffset,
        image_upward,
        image_upbias,
        image_downward,
        image_downbias,
        image_endgain,
        image_endoffset,
        image_project,
    )
    group_count = lax.axis_size("dp") * lax.axis_size("fsdp")
    device = lax.axis_index("dp") * lax.axis_size("fsdp") + lax.axis_index("fsdp")
    pair_total = group_count * SLOTS
    live_all = (
        (jnp.arange(SLOTS)[None, :] < pair_counts[:, None]).astype(jnp.float32).reshape(pair_total)
    )
    live_total = jnp.sum(live_all)
    text_live = lax.dynamic_slice_in_dim(live_all, device * SLOTS, SLOTS)
    temper = jnp.exp(log_scale[0])
    half_inverse = 1.0 / (2.0 * live_total)
    image_unit = forward_block(image_tokens, image_weights, IMAGE_LEN)[0]
    image_low = image_unit.astype(jnp.bfloat16)
    shard_piece = lax.all_gather(image_low, ("dp", "fsdp"), axis=0, tiled=True)
    text_weights = tuple(
        lax.all_gather(shard, "fsdp", axis=0, tiled=True)
        for shard in (
            text_gain,
            text_offset,
            text_joint,
            text_mixer,
            text_mixbias,
            text_feedgain,
            text_feedoffset,
            text_upward,
            text_upbias,
            text_downward,
            text_downbias,
            text_endgain,
            text_endoffset,
            text_project,
        )
    )
    text_unit, kept_values = forward_block(text_tokens, text_weights, TEXT_LEN)
    text_low = text_unit.astype(jnp.bfloat16)
    cosine = contract_last(text_low, shard_piece)
    scaled = jnp.exp(temper * cosine - temper)
    image_live = live_all
    forward_row_sum = jnp.sum(scaled * image_live[None, :], axis=1)
    forward_column_sum = jnp.sum(scaled * text_live[:, None], axis=0)
    column_sum = forward_column_sum
    column_sum = lax.psum(column_sum, ("dp", "fsdp"))
    diagonal_cos = jnp.sum(text_low.astype(jnp.float32) * image_low.astype(jnp.float32), axis=1)
    row_log = temper + jnp.log(forward_row_sum)
    column_log = temper + jnp.log(lax.dynamic_slice_in_dim(column_sum, device * SLOTS, SLOTS))
    diagonal = temper * diagonal_cos
    loss_part = jnp.sum(text_live * (row_log - diagonal) + text_live * (column_log - diagonal)) / (
        2.0 * live_total
    )
    coupling = (
        scaled * (text_live / forward_row_sum)[:, None] * image_live[None, :]
        + scaled * text_live[:, None] * (image_live / column_sum)[None, :]
    ) * half_inverse
    temper_grad = jnp.sum(coupling * cosine)
    unit_grad = product((temper * coupling).astype(jnp.bfloat16), shard_piece)
    unit_grad, temper_grad = (unit_grad, temper_grad)
    unit_grad = unit_grad - temper / live_total * text_live[:, None] * image_low.astype(jnp.float32)
    temper_grad = temper_grad - jnp.sum(text_live * diagonal_cos) / live_total
    loss_total, scale_total = lax.psum((loss_part, temper * temper_grad), ("dp", "fsdp"))
    factors, vectors, token_grad = backward_block(
        kept_values, text_weights, unit_grad, TEXT_LEN
    )
    final_grads = reduce_plain(factors, vectors)
    return (
        *final_grads,
        jnp.reshape(scale_total, (1,)),
        token_grad,
        jnp.reshape(loss_total, (1,)),
    )


def on_device(*arrays):
    if (lax.axis_size("dp"), lax.axis_size("fsdp")) != (16, 2):
        return on_device_plain(*arrays)
    text_tokens, image_tokens, pair_counts, log_scale = arrays[:4]
    text_weights, image_weights = arrays[4:18], arrays[18:32]
    matrix_places = (2, 3, 7, 9, 13)
    vector_places = (0, 1, 4, 5, 6, 10, 11, 12)
    shard_vector = pack_rows(
        [text_weights[place] for place in vector_places]
        + [text_weights[8][start : start + HALF] for start in range(0, 4 * HALF, HALF)]
    )
    shards = tuple(text_weights[place] for place in matrix_places)
    image_low, vectors, others = image_kernel(image_tokens, image_weights, shard_vector, shards)
    grads, packed, token_grad = text_kernel(
        text_tokens, vectors, image_low, pair_counts, log_scale, shards, others
    )
    *final_grads, scale_total, loss_total = finish_kernel(grads, packed)
    return (*final_grads, scale_total.reshape(1), token_grad, loss_total.reshape(1))


def solution(mesh):
    return jax.shard_map(
        on_device,
        mesh=mesh,
        in_specs=(
            P(("dp", "fsdp"), None),
            P(("dp", "fsdp"), None),
            P(),
            P(),
            P("fsdp"),
            P("fsdp"),
            P("fsdp", None),
            P("fsdp", None),
            P("fsdp"),
            P("fsdp"),
            P("fsdp"),
            P("fsdp", None),
            P("fsdp"),
            P("fsdp", None),
            P("fsdp"),
            P("fsdp"),
            P("fsdp"),
            P("fsdp", None),
            P(),
            P(),
            P(),
            P(),
            P(),
            P(),
            P(),
            P(),
            P(),
            P(),
            P(),
            P(),
            P(),
            P(),
        ),
        out_specs=(
            P("fsdp"),
            P("fsdp"),
            P("fsdp", None),
            P("fsdp", None),
            P("fsdp"),
            P("fsdp"),
            P("fsdp"),
            P("fsdp", None),
            P("fsdp"),
            P("fsdp", None),
            P("fsdp"),
            P("fsdp"),
            P("fsdp"),
            P("fsdp", None),
            P(),
            P(("dp", "fsdp"), None),
            P(),
        ),
        check_vma=False,
    )
```

```python
import jax
import jax.numpy as jnp
from jax import lax
from jax.experimental import pallas as pl
from jax.experimental.pallas import tpu as pltpu
from jax.sharding import PartitionSpec as P

HEADS = 12
HEAD_DIM = 64
TEXT_LEN = 16
IMAGE_LEN = 50
SLOTS = 36


EPSILON = 1e-06


def product(left_side, right_side):
    return jnp.dot(left_side, right_side, preferred_element_type=jnp.float32)


def contract_last(left_side, right_side):
    return lax.dot_general(
        left_side, right_side, (((1,), (1,)), ((), ())), preferred_element_type=jnp.float32
    )


def contract_first(left_side, right_side):
    return lax.dot_general(
        left_side, right_side, (((0,), (0,)), ((), ())), preferred_element_type=jnp.float32
    )


def layer_norm(values, gain_vector, offset):
    centred = values - jnp.mean(values, axis=-1, keepdims=True)
    variance = jnp.mean(centred * centred, axis=-1, keepdims=True)
    return centred * lax.rsqrt(variance + EPSILON) * gain_vector.astype(
        jnp.float32
    ) + offset.astype(jnp.float32)


def normalize(embedding):
    return embedding * lax.rsqrt(jnp.sum(embedding * embedding, axis=-1, keepdims=True) + EPSILON)


def forward_block(tokens, weights, length):
    (
        norm_gain,
        norm_offset,
        joint_weight,
        mixer_weight,
        mixer_bias,
        feed_gain,
        feed_offset,
        up_weight,
        up_bias,
        down_weight,
        down_bias,
        end_gain,
        end_offset,
        projection,
    ) = weights
    inputs = tokens.astype(jnp.float32)
    total_rows, model_width = inputs.shape
    seq_count = total_rows // length
    factor = HEAD_DIM ** (-0.5)
    normed = layer_norm(inputs, norm_gain, norm_offset).astype(jnp.bfloat16)
    triple = (
        product(normed, joint_weight)
        .astype(jnp.bfloat16)
        .reshape(seq_count, length, 3, HEADS, HEAD_DIM)
    )
    queries = triple[:, :, 0]
    keyset = triple[:, :, 1]
    valueset = triple[:, :, 2]
    scores = (
        jnp.einsum("sqhd,skhd->shqk", queries, keyset, preferred_element_type=jnp.float32) * factor
    )
    soft_weights = jax.nn.softmax(scores, axis=-1)
    soft_low = soft_weights.astype(jnp.bfloat16)
    attended = jnp.einsum("shqk,skhd->sqhd", soft_low, valueset, preferred_element_type=jnp.float32)
    attended = attended.reshape(total_rows, model_width).astype(jnp.bfloat16)
    residual = inputs + product(attended, mixer_weight) + mixer_bias.astype(jnp.float32)
    normed_two = layer_norm(residual, feed_gain, feed_offset).astype(jnp.bfloat16)
    pre_active = product(normed_two, up_weight) + up_bias.astype(jnp.float32)
    active = jax.nn.gelu(pre_active).astype(jnp.bfloat16)
    output = residual + product(active, down_weight) + down_bias.astype(jnp.float32)
    final_norm = layer_norm(output, end_gain, end_offset)
    pooled = jnp.mean(final_norm.reshape(seq_count, length, model_width), axis=1)
    embedding = product(pooled.astype(jnp.bfloat16), projection)
    unit_vector = normalize(embedding)
    kept_values = (
        inputs,
        normed,
        triple,
        soft_weights,
        soft_low,
        attended,
        residual,
        normed_two,
        pre_active,
        active,
        output,
        pooled,
        embedding,
    )
    return (unit_vector, kept_values)


def backward_block(kept_values, weights, unit_grad, length):
    (
        norm_gain,
        norm_offset,
        joint_weight,
        mixer_weight,
        mixer_bias,
        feed_gain,
        feed_offset,
        up_weight,
        up_bias,
        down_weight,
        down_bias,
        end_gain,
        end_offset,
        projection,
    ) = weights
    (
        inputs,
        normed,
        triple,
        soft_weights,
        soft_low,
        attended,
        residual,
        normed_two,
        pre_active,
        active,
        output,
        pooled,
        embedding,
    ) = kept_values
    total_rows, model_width = inputs.shape
    seq_count = total_rows // length
    factor = HEAD_DIM ** (-0.5)
    unused_unit, norm_back = jax.vjp(normalize, embedding)
    embed_grad = norm_back(unit_grad)[0].astype(jnp.bfloat16)
    pooled_grad = contract_last(embed_grad, projection)
    final_grad = jnp.broadcast_to(
        pooled_grad[:, None, :] / length, (seq_count, length, model_width)
    ).reshape(total_rows, model_width)
    unused_final, end_back = jax.vjp(
        layer_norm, output, end_gain.astype(jnp.float32), end_offset.astype(jnp.float32)
    )
    output_grad, endgain_grad, endoffset_grad = end_back(final_grad)
    down_low = output_grad.astype(jnp.bfloat16)
    downbias_grad = jnp.sum(output_grad, axis=0)
    active_grad = contract_last(down_low, down_weight)
    unused_active, gelu_back = jax.vjp(jax.nn.gelu, pre_active)
    pre_grad = gelu_back(active_grad)[0]
    upbias_grad = jnp.sum(pre_grad, axis=0)
    pre_low = pre_grad.astype(jnp.bfloat16)
    normed_grad = contract_last(pre_low, up_weight)
    unused_feed, feed_back = jax.vjp(
        layer_norm, residual, feed_gain.astype(jnp.float32), feed_offset.astype(jnp.float32)
    )
    residual_part, feedgain_grad, feedoffset_grad = feed_back(normed_grad)
    residual_grad = output_grad + residual_part
    mixbias_grad = jnp.sum(residual_grad, axis=0)
    mix_low = residual_grad.astype(jnp.bfloat16)
    attended_grad = contract_last(mix_low, mixer_weight).astype(jnp.bfloat16)
    attended_grad = attended_grad.reshape(seq_count, length, HEADS, HEAD_DIM)
    queries = triple[:, :, 0]
    keyset = triple[:, :, 1]
    valueset = triple[:, :, 2]
    soft_grad = jnp.einsum(
        "sqhd,skhd->shqk", attended_grad, valueset, preferred_element_type=jnp.float32
    )
    value_grad = jnp.einsum(
        "shqk,sqhd->skhd", soft_low, attended_grad, preferred_element_type=jnp.float32
    )
    score_grad = soft_weights * (
        soft_grad - jnp.sum(soft_weights * soft_grad, axis=-1, keepdims=True)
    )
    score_grad = score_grad.astype(jnp.bfloat16)
    query_grad = (
        jnp.einsum("shqk,skhd->sqhd", score_grad, keyset, preferred_element_type=jnp.float32)
        * factor
    )
    key_grad = (
        jnp.einsum("shqk,sqhd->skhd", score_grad, queries, preferred_element_type=jnp.float32)
        * factor
    )
    triple_grad = jnp.stack([query_grad, key_grad, value_grad], axis=2)
    triple_grad = triple_grad.reshape(total_rows, 3 * model_width).astype(jnp.bfloat16)
    first_grad = contract_last(triple_grad, joint_weight)
    unused_first, first_back = jax.vjp(
        layer_norm, inputs, norm_gain.astype(jnp.float32), norm_offset.astype(jnp.float32)
    )
    input_part, gain_grad, offset_grad = first_back(first_grad)
    input_grad = residual_grad + input_part
    factors = (
        (normed, triple_grad),
        (attended, mix_low),
        (normed_two, pre_low),
        (active, down_low),
        (pooled.astype(jnp.bfloat16), embed_grad),
    )
    vectors = (
        gain_grad,
        offset_grad,
        mixbias_grad,
        feedgain_grad,
        feedoffset_grad,
        upbias_grad,
        downbias_grad,
        endgain_grad,
        endoffset_grad,
    )
    return (factors, vectors, input_grad)


WIDTH = 768
HALF = 384
QUARTER = 192
SUB = 2
ROWS = QUARTER // SUB
PART = ROWS // 2
UNITS = 13
STEPS = UNITS * SUB
TILE = 256
POOL_ROWS = 128
VECTOR_ROWS = 16
PART_RING = 8
CORE_RING = 4
RING = 8
TOTAL_RING = 6
VECTOR_START = 24
TAIL = 8
MESH = pl.DeviceIdType.MESH


ROOT_SCALE = 0.125
PAIR = 128
CUT = -1e30
TEXT_GROUP = 128
CHUNK = 96
SLOT_ROWS = 40
NEAR = 8
GELU_ROOT = 0.7978845608028654
GELU_CUBE = 0.044715


def wide(values):
    return values.astype(jnp.float32)


def low(values):
    return values.astype(jnp.bfloat16)


def centred_scale(values):
    centred = values - jnp.mean(values, axis=-1, keepdims=True)
    variance = jnp.mean(centred * centred, axis=-1, keepdims=True)
    rate = lax.rsqrt(variance + EPSILON)
    return centred * rate, rate


def gelu_value(values):
    inner = GELU_ROOT * (values + GELU_CUBE * (values * values * values))
    half = 0.5 * values
    return half + half * jnp.tanh(inner)


def gelu_slope(values):
    square = values * values
    bend = jnp.tanh(GELU_ROOT * values * (1.0 + GELU_CUBE * square))
    inner_slope = GELU_ROOT * (1.0 + (3.0 * GELU_CUBE) * square)
    return 0.5 * (1.0 + bend) + 0.5 * values * (1.0 - bend * bend) * inner_slope


def norm_back(values, grad, gain):
    unit, rate = centred_scale(values)
    scaled = grad * gain
    mean = jnp.mean(scaled, axis=-1, keepdims=True)
    slope = jnp.mean(scaled * unit, axis=-1, keepdims=True)
    return rate * (scaled - mean - unit * slope), grad * unit


def column_sum(values):
    return jnp.sum(values, axis=0, keepdims=True)


def peers_of(dp, x):
    z, y, core = dp // 4, (dp // 2) % 2, dp % 2
    near = []
    for step in range(1, NEAR):
        flip_x, flip_y, flip_core = step % 2, (step // 2) % 2, step // 4
        other_y = y + flip_y - 2 * flip_y * y
        other_core = core + flip_core - 2 * flip_core * core
        other_x = x + flip_x - 2 * flip_x * x
        near.append((z * 4 + other_y * 2 + other_core, other_x))
    far = [(((z + step) % 4) * 4 + y * 2 + core, x) for step in range(1, 4)]
    return near, far


def text_body(
    token_ref,
    vector_ref,
    image_ref,
    count_ref,
    scale_ref,
    joint_own,
    mixer_own,
    up_own,
    down_own,
    project_own,
    joint_other,
    mixer_other,
    up_other,
    down_other,
    project_other,
    grad_hbm,
    vector_out,
    token_out,
    joint,
    mixer,
    up,
    down,
    project,
    normed,
    normed_two,
    attended,
    hidden,
    pooled_rows,
    embed_rows,
    down_rows,
    mix_rows,
    pre_rows,
    triple,
    residual,
    active_in,
    output,
    work,
    bias_rows,
    images,
    near_sums,
    far_sums,
    weight_sem,
    image_sem,
    near_sem,
    far_sem,
    a_vmem,
    b_vmem,
    vector_acc,
    core_out,
    part,
    core_in,
    x_in,
    y_in,
    end_in,
    mid_in,
    total,
    vector_core,
    vector_x,
    vector_y,
    vector_z,
    vector_sum,
    core_sems,
    x_sems,
    y_sems,
    end_sems,
    mid_sems,
    back_sems,
    wide_sems,
    twin_sems,
    own_sems,
    vector_sems,
):
    dp = lax.axis_index("dp")
    x = lax.axis_index("fsdp")
    z, y, core = dp // 4, (dp // 2) % 2, dp % 2
    near, far = peers_of(dp, x)
    x_peer, y_peer, core_peer = near[0], near[1], near[3]
    loads = []
    for index, (own_half, other_half, target) in enumerate(
        (
            (joint_own, joint_other, joint),
            (mixer_own, mixer_other, mixer),
            (up_own, up_other, up),
            (down_own, down_other, down),
            (project_own, project_other, project),
        )
    ):
        half = own_half.shape[0]
        pair = []
        for side, (source, place) in enumerate(((own_half, x), (other_half, 1 - x))):
            piece = target.at[pl.ds(pl.multiple_of(place * half, half), half)]
            pair.append(pltpu.make_async_copy(source, piece, weight_sem.at[index, side]))
        loads.append(pair)
    for pair in loads:
        for load in pair:
            load.start()

    def loaded(index):
        for load in loads[index]:
            load.wait()

    barrier = pltpu.get_barrier_semaphore()
    for peer in near + far:
        pl.semaphore_signal(barrier, inc=1, device_id=peer, device_id_type=MESH)

    def send(source, target, sems, index, peer):
        return pltpu.make_async_remote_copy(
            src_ref=source,
            dst_ref=target,
            send_sem=sems.at[0, index],
            recv_sem=sems.at[1, index],
            device_id=peer,
            device_id_type=MESH,
        )

    own_slot = images.at[core, y, x, z]
    z_sends = [send(own_slot, own_slot, image_sem, k, far[k]) for k in range(3)]
    line = images.at[core, y, x]
    y_send = send(line, line, image_sem, 3, y_peer)
    x_send = send(line, line, image_sem, 4, x_peer)
    other_line = images.at[core, 1 - y, x, pl.ds(0, 2)]
    x_again = send(other_line, other_line, image_sem, 5, x_peer)
    cross_line = images.at[core, y, 1 - x, pl.ds(2, 2)]
    y_again = send(cross_line, cross_line, image_sem, 7, y_peer)
    plane = images.at[core]
    core_send = send(plane, plane, image_sem, 6, core_peer)

    rows, width = token_ref.shape
    feed = up.shape[1]
    seqs = rows // TEXT_LEN

    def vector(index):
        return wide(
            jnp.concatenate(
                [vector_ref[0, index : index + 1], vector_ref[1, index : index + 1]], axis=1
            )
        )

    def span(index, size):
        return pl.ds(pl.multiple_of(index * size, size), size)

    gain, offset, mix_bias, feed_gain, feed_offset, down_bias, end_gain, end_offset = (
        vector(index) for index in range(8)
    )
    images[core, y, x, z] = image_ref[...]
    column = lax.broadcasted_iota(jnp.int32, (1, 32 * SLOT_ROWS), 1)
    limit = jnp.zeros(column.shape, jnp.int32)
    for slot in range(32):
        slot_core, slot_y, slot_x, slot_z = slot // 16, (slot // 8) % 2, (slot // 4) % 2, slot % 4
        owner = (slot_z * 4 + slot_y * 2 + slot_core) * 2 + slot_x
        limit = jnp.where(
            (column >= slot * SLOT_ROWS) & (column < (slot + 1) * SLOT_ROWS),
            slot * SLOT_ROWS + count_ref[owner],
            limit,
        )
    live = jnp.where(column < limit, 1.0, 0.0)
    own_limit = count_ref[dp * 2 + x]
    own_live = jnp.where(
        lax.broadcasted_iota(jnp.int32, (rows // TEXT_LEN, 1), 0) < own_limit, 1.0, 0.0
    )

    normed[...] = low(centred_scale(wide(token_ref[...]))[0] * gain + offset)
    loaded(0)
    pl.semaphore_wait(barrier, 10)
    for copy in z_sends:
        copy.start()

    def tiles(base):
        for index in range(width // TILE):
            yield pl.ds(base + index * TILE, TILE)

    for index in range(3):
        for cols in tiles(index * width):
            values = product(normed[...], joint[:, cols])
            triple[:, cols] = low(values * ROOT_SCALE if index == 0 else values)

    lane = lax.broadcasted_iota(jnp.int32, (1, PAIR), 1)
    sides = (
        low(jnp.where(lane < HEAD_DIM, 1.0, 0.0)),
        low(jnp.where(lane < HEAD_DIM, 0.0, 1.0)),
    )
    counters = [jnp.broadcast_to(side, (TEXT_GROUP, PAIR)) for side in sides]
    pairs = width // PAIR
    tail_rows = rows % TEXT_GROUP
    tail_start = rows - tail_rows

    def same_of(count):
        row = lax.broadcasted_iota(jnp.int32, (count, TEXT_GROUP), 0) + (TEXT_GROUP - count)
        col = lax.broadcasted_iota(jnp.int32, (count, TEXT_GROUP), 1)
        return jnp.where(row // TEXT_LEN == col // TEXT_LEN, 0.0, CUT)

    def head_parts(values):
        return [values[:, head * TEXT_GROUP : (head + 1) * TEXT_GROUP] for head in range(2)]

    def scores_of(query, keys, same):
        both = jnp.concatenate([keys * side for side in sides], axis=0)
        softs = []
        for score in head_parts(contract_last(query, both)):
            score = score + same
            softs.append(jnp.exp(score - jnp.max(score, axis=-1, keepdims=True)))
        return both, softs

    def attend(group, key_group, same, pair):
        cols = pl.ds(pair * PAIR, PAIR)
        keys = triple[key_group, pl.ds(width + pair * PAIR, PAIR)]
        values = triple[key_group, pl.ds(2 * width + pair * PAIR, PAIR)]
        both, softs = scores_of(triple[group, cols], keys, same)
        spread = jnp.concatenate(
            [
                jnp.concatenate([values * side, counter], axis=1)
                for side, counter in zip(sides, counters)
            ],
            axis=0,
        )
        mixed = product(low(jnp.concatenate(softs, axis=1)), spread)
        attended[group, cols] = low(mixed[:, :PAIR] / mixed[:, PAIR:])

    tail_group = pl.ds(tail_start, tail_rows)
    tail_keys = pl.ds(rows - TEXT_GROUP, TEXT_GROUP)
    same_full = same_of(TEXT_GROUP)
    same_tail = same_of(tail_rows) if tail_rows else None
    for index in range(rows // TEXT_GROUP):
        group = pl.ds(index * TEXT_GROUP, TEXT_GROUP)
        for pair in range(pairs):
            attend(group, group, same_full, pair)
    if tail_rows:
        for pair in range(pairs):
            attend(tail_group, tail_keys, same_tail, pair)

    loaded(1)
    for cols in tiles(0):
        residual[:, cols] = product(attended[...], mixer[:, cols])
    values = wide(token_ref[...]) + residual[...] + mix_bias
    residual[...] = values
    normed_two[...] = low(centred_scale(values)[0] * feed_gain + feed_offset)
    for copy in z_sends:
        copy.wait()
    x_send.start()
    y_send.start()
    loaded(2)
    for index in range(8):
        bias_rows[0:1, index * HALF : (index + 1) * HALF] = wide(
            vector_ref[index // 4, 8 + index % 4 : 9 + index % 4]
        )

    for index in range(feed // width):
        for cols in tiles(index * width):
            values = product(normed_two[...], up[:, cols])
            values = values + bias_rows[0:1, cols]
            active_in[:, cols] = values
            hidden[:, cols] = low(gelu_value(values))

    x_send.wait()
    y_send.wait()
    x_again.start()
    y_again.start()
    loaded(3)
    for cols in tiles(0):
        output[:, cols] = product(hidden[...], down[:, cols])

    x_again.wait()
    y_again.wait()
    core_send.start()
    values = residual[...] + output[...] + down_bias
    output[...] = values
    pooled = jnp.sum(centred_scale(values)[0].reshape(seqs, TEXT_LEN, width), axis=1)
    pooled = low(pooled * (1.0 / TEXT_LEN) * end_gain + end_offset)
    loaded(4)
    embedding = product(pooled, project[...])
    length_rate = lax.rsqrt(jnp.sum(embedding * embedding, axis=-1, keepdims=True) + EPSILON)
    text_unit = embedding * length_rate
    text_low = low(text_unit)
    core_send.wait()

    every = images[...].reshape(2 * 2 * 2 * 4 * SLOT_ROWS, width)
    temper = jnp.exp(jnp.full((1, 1), scale_ref[0], jnp.float32))
    live_total = jnp.sum(live, axis=1, keepdims=True)
    half_inverse = 0.5 / live_total
    cosine = contract_last(text_low, every)
    scaled = jnp.exp(temper * cosine - temper)
    row_sum = jnp.sum(scaled * live, axis=1, keepdims=True)
    near_place = x + 2 * y + 4 * core
    near_sums[near_place] = column_sum(scaled * own_live)
    near_sends = [
        send(near_sums.at[near_place], near_sums.at[near_place], near_sem, k, near[k])
        for k in range(NEAR - 1)
    ]
    for copy in near_sends:
        copy.start()
    image_own = wide(image_ref[:seqs])
    diagonal_cos = jnp.sum(wide(text_low) * image_own, axis=1, keepdims=True)
    row_part = scaled * (own_live / row_sum) * live
    for copy in near_sends:
        copy.wait()
    far_sums[z] = (
        ((near_sums[0] + near_sums[1]) + (near_sums[2] + near_sums[3]))
        + ((near_sums[4] + near_sums[5]) + (near_sums[6] + near_sums[7]))
    )
    far_sends = [
        send(far_sums.at[z], far_sums.at[z], far_sem, k, far[k]) for k in range(3)
    ]
    for copy in far_sends:
        copy.start()
    for copy in far_sends:
        copy.wait()
    columns = (far_sums[0] + far_sums[1]) + (far_sums[2] + far_sums[3])
    coupling = (row_part + scaled * own_live * (live / columns)) * half_inverse
    column_log = jnp.where(live > 0.0, temper + jnp.log(columns), 0.0)
    row_log = temper + jnp.log(row_sum)
    loss_own = column_sum(own_live * (row_log - 2.0 * temper * diagonal_cos))
    loss_shared = jnp.sum(live * column_log, axis=1, keepdims=True)
    devices = lax.axis_size("dp") * lax.axis_size("fsdp")
    loss_part = (loss_own + loss_shared * (1.0 / devices)) * half_inverse
    temper_grad = (
        jnp.sum(column_sum(coupling * cosine), axis=1, keepdims=True)
        - column_sum(own_live * diagonal_cos) / live_total
    )
    unit_grad = product(low(temper * coupling), every)
    unit_grad = unit_grad - (temper / live_total) * own_live * image_own
    embed_grad = low(
        (unit_grad - text_unit * jnp.sum(text_unit * unit_grad, axis=-1, keepdims=True))
        * length_rate
    )
    at_end = (z == 0) | (z == 3)
    at_mid = (z == 1) | (z == 2)
    pair_peer = ((z + 1 - 2 * (z % 2)) * 4 + y * 2 + core, x)
    mid_peer = ((3 - z) * 4 + y * 2 + core, x)

    def remote(source, target, sems, index, peer):
        return pltpu.make_async_remote_copy(
            src_ref=source,
            dst_ref=target,
            send_sem=sems.at[0, index],
            recv_sem=sems.at[1, index],
            device_id=peer,
            device_id_type=MESH,
        )

    def core_copy(step):
        return remote(core_out.at[step % 2], core_in.at[step % CORE_RING], core_sems, step, core_peer)

    def x_copy(step):
        return remote(part.at[step % PART_RING, 1 - x], x_in.at[step % RING], x_sems, step, x_peer)

    def y_copy(step):
        rows = pl.ds(pl.multiple_of((1 - y) * PART, PART), PART)
        return remote(part.at[step % PART_RING, x, rows], y_in.at[step % RING], y_sems, step, y_peer)

    def own_rows():
        return pl.ds(pl.multiple_of(y * PART, PART), PART)

    def end_copy(step):
        return remote(part.at[step % PART_RING, x, own_rows()], end_in.at[step % RING], end_sems, step, pair_peer)

    def mid_copy(step):
        return remote(part.at[step % PART_RING, x, own_rows()], mid_in.at[step % RING], mid_sems, step, mid_peer)

    def own_piece(step):
        return grad_hbm.at[step, core, own_rows()]

    def back_copy(step):
        return remote(total.at[step % TOTAL_RING], own_piece(step), back_sems, step, pair_peer)

    def wide_copy(step, source):
        return remote(source, own_piece(step), wide_sems, step, y_peer)

    def own_copy(step):
        return pltpu.make_async_copy(total.at[step % TOTAL_RING], own_piece(step), own_sems.at[step])

    def twin_copy(step):
        piece = grad_hbm.at[step, core]
        return remote(piece, piece, twin_sems, step, core_peer)

    vector_first = remote(vector_acc, vector_core, vector_sems, 0, core_peer)
    vector_second = remote(vector_sum.at[0], vector_x, vector_sems, 1, x_peer)
    vector_third = remote(vector_sum.at[1], vector_y, vector_sems, 2, y_peer)
    vector_last = []
    for step in range(1, 4):
        other = ((z + step) % 4) * 4 + y * 2 + core
        vector_last.append(
            remote(vector_sum.at[2], vector_z.at[step - 1], vector_sems, 2 + step, (other, x))
        )

    def tick(time):
        @pl.when((time >= 1) & (time - 1 < STEPS))
        def _():
            step = time - 1
            core_copy(step).wait()
            part[step % PART_RING, 1 - x] = low(wide(part[step % PART_RING, 1 - x]) + wide(core_in[step % CORE_RING, 1 - x]))
            x_copy(step).start()
            part[step % PART_RING, x] = low(wide(part[step % PART_RING, x]) + wide(core_in[step % CORE_RING, x]))

        @pl.when(time < STEPS)
        def _():
            step = time
            unit = step // SUB
            half = step % SUB
            fresh = half == 0

            @pl.when(fresh & (unit == 0))
            def _():
                a_vmem[...] = jnp.zeros(a_vmem.shape, jnp.bfloat16)
                a_vmem[:, :POOL_ROWS] = pooled_rows[...].T
                b_vmem[...] = jnp.zeros(b_vmem.shape, jnp.bfloat16)
                b_vmem[:POOL_ROWS] = embed_rows[...]

            @pl.when(fresh & (unit >= 1) & (unit <= 4))
            def _():
                block = unit - 1
                for side in range(2):
                    cols = pl.ds(pl.multiple_of(side * 2 * width + block * HALF, HALF), HALF)
                    a_vmem[pl.ds(side * HALF, HALF)] = hidden[:, cols].T

            @pl.when(fresh & (unit == 1))
            def _():
                b_vmem[...] = down_rows[...]

            @pl.when(fresh & (unit == 5))
            def _():
                a_vmem[...] = normed_two[...].T

            @pl.when(fresh & (unit >= 5) & (unit <= 8))
            def _():
                b_vmem[...] = pre_rows[:, span(unit - 5, width)]

            @pl.when(fresh & (unit == 9))
            def _():
                a_vmem[...] = attended[...].T
                b_vmem[...] = mix_rows[...]

            @pl.when(fresh & (unit == 10))
            def _():
                a_vmem[...] = normed[...].T

            @pl.when(fresh & (unit >= 10))
            def _():
                b_vmem[...] = triple[:, span(unit - 10, width)]

            term = b_vmem[...]
            for which in range(2):
                rows = pl.ds(
                    pl.multiple_of(which * HALF + (1 - core) * QUARTER + half * ROWS, ROWS), ROWS
                )
                core_out[step % 2, which] = low(product(a_vmem[rows], term))
            core_copy(step).start()
            for which in range(2):
                rows = pl.ds(
                    pl.multiple_of(which * HALF + core * QUARTER + half * ROWS, ROWS), ROWS
                )
                part[step % PART_RING, which] = low(product(a_vmem[rows], term))

        @pl.when((time >= 2) & (time - 2 < STEPS))
        def _():
            step = time - 2
            x_copy(step).wait()
            rows = pl.ds(pl.multiple_of((1 - y) * PART, PART), PART)
            part[step % PART_RING, x, rows] = low(wide(part[step % PART_RING, x, rows]) + wide(x_in[step % RING, rows]))
            y_copy(step).start()
            part[step % PART_RING, x, own_rows()] = low(
                wide(part[step % PART_RING, x, own_rows()]) + wide(x_in[step % RING, own_rows()])
            )

        @pl.when((time >= 3) & (time - 3 < STEPS))
        def _():
            step = time - 3
            y_copy(step).wait()
            part[step % PART_RING, x, own_rows()] = low(
                wide(part[step % PART_RING, x, own_rows()]) + wide(y_in[step % RING])
            )

            @pl.when(at_end)
            def _():
                end_copy(step).start()

        @pl.when((time >= 4) & (time - 4 < STEPS))
        def _():
            step = time - 4

            @pl.when(at_end)
            def _():
                end_copy(step).wait_send()

            @pl.when(at_mid)
            def _():
                end_copy(step).wait_recv()
                part[step % PART_RING, x, own_rows()] = low(
                    wide(part[step % PART_RING, x, own_rows()]) + wide(end_in[step % RING])
                )
                mid_copy(step).start()

        @pl.when((time >= 5) & (time - 5 < STEPS) & at_mid)
        def _():
            step = time - 5
            mid_copy(step).wait()
            total[step % TOTAL_RING] = low(
                wide(part[step % PART_RING, x, own_rows()]) + wide(mid_in[step % RING])
            )
            back_copy(step).start()
            wide_copy(step, total.at[step % TOTAL_RING]).start()
            own_copy(step).start()

        @pl.when((time >= 6) & (time - 6 < STEPS))
        def _():
            step = time - 6

            @pl.when(at_end)
            def _():
                back_copy(step).wait_recv()
                wide_copy(step, own_piece(step)).start()

            @pl.when(at_mid)
            def _():
                back_copy(step).wait_send()

        @pl.when((time >= 7) & (time - 7 < STEPS))
        def _():
            step = time - 7
            wide_copy(step, total.at[step % TOTAL_RING]).wait()

            @pl.when(at_mid)
            def _():
                own_copy(step).wait()

            twin_copy(step).start()

        @pl.when((time >= 8) & (time - 8 < STEPS))
        def _():
            step = time - 8
            twin_copy(step).wait()

        @pl.when(time == VECTOR_START + 0)
        def _():
            vector_first.start()

        @pl.when(time == VECTOR_START + 1)
        def _():
            vector_first.wait()
            vector_sum[0] = vector_acc[...] + vector_core[...]
            vector_second.start()

        @pl.when(time == VECTOR_START + 3)
        def _():
            vector_second.wait()
            vector_sum[1] = vector_sum[0] + vector_x[...]
            vector_third.start()

        @pl.when(time == VECTOR_START + 5)
        def _():
            vector_third.wait()
            vector_sum[2] = vector_sum[1] + vector_y[...]
            for copy in vector_last:
                copy.start()

        @pl.when(time == VECTOR_START + 7)
        def _():
            for copy in vector_last:
                copy.wait()
            order = lax.broadcasted_iota(jnp.int32, (VECTOR_ROWS, WIDTH), 0) * 0 + z
            own = vector_sum[2]
            before_one = vector_z[0]
            before_two = vector_z[1]
            before_three = vector_z[2]

            def pick(where):
                shift = (order - where + 4) % 4
                return jnp.where(
                    shift == 0,
                    own,
                    jnp.where(
                        shift == 1,
                        before_one,
                        jnp.where(shift == 2, before_two, before_three),
                    ),
                )

            vector_out[...] = (pick(0) + pick(1)) + (pick(2) + pick(3))

    pooled_rows[...] = jnp.zeros(pooled_rows.shape, jnp.bfloat16)
    pooled_rows[:SLOT_ROWS] = jnp.pad(pooled, ((0, SLOT_ROWS - seqs), (0, 0)))
    embed_rows[...] = jnp.zeros(embed_rows.shape, jnp.bfloat16)
    embed_rows[:SLOT_ROWS] = jnp.pad(embed_grad, ((0, SLOT_ROWS - seqs), (0, 0)))
    pooled_grad = contract_last(embed_grad, project[...]) * (1.0 / TEXT_LEN)
    pl.loop(0, 2)(tick)
    for index in range(rows // CHUNK):
        work[index * 8 : index * 8 + CHUNK // TEXT_LEN] = pooled_grad[
            index * (CHUNK // TEXT_LEN) : (index + 1) * (CHUNK // TEXT_LEN)
        ]

    vector_acc[...] = jnp.zeros(vector_acc.shape, jnp.float32)
    column = lax.broadcasted_iota(jnp.int32, (1, width), 1)
    vector_acc[12:13] = jnp.where(
        column == 0, loss_part, jnp.where(column == 1, temper * temper_grad, 0.0)
    )
    vector_acc[11:12] = column_sum(pooled_grad) * float(TEXT_LEN)

    def gather(index, value):
        vector_acc[index : index + 1] = vector_acc[index : index + 1] + value

    @pl.loop(0, rows // CHUNK)
    def _(index):
        chunk = span(index, CHUNK)
        grad = work[span(index, 8)][: CHUNK // TEXT_LEN]
        grad = jnp.broadcast_to(
            grad[:, None, :], (CHUNK // TEXT_LEN, TEXT_LEN, width)
        ).reshape(CHUNK, width)
        value, gain_part = norm_back(output[chunk], grad, end_gain)
        output[chunk] = value
        down_rows[chunk] = low(value)
        gather(10, column_sum(gain_part))
        gather(9, column_sum(value))

    @pl.loop(0, 6)
    def _(index):
        tick(2 + index)
        for side in range(2):
            cols = pl.ds(pl.multiple_of(index * (2 * TILE) + side * TILE, TILE), TILE)
            values = contract_last(down_rows[...], down[cols]) * gelu_slope(active_in[:, cols])
            pre_rows[:, cols] = low(values)
            bias_rows[:, cols] = jnp.sum(values.reshape(rows // 8, 8, TILE), axis=0)

    @pl.loop(0, 3)
    def _(index):
        tick(8 + index)
        cols = span(index, TILE)
        active_in[:, cols] = contract_last(pre_rows[...], up[cols])

    @pl.loop(0, 2)
    def _(half):
        tick(11 + half)

        @pl.loop(0, 3)
        def _(inner):
            chunk = span(half * 3 + inner, CHUNK)
            grad = active_in[chunk, :width]
            value, gain_part = norm_back(residual[chunk], grad, feed_gain)
            value = value + output[chunk]
            output[chunk] = value
            mix_rows[chunk] = low(value)
            gather(3, column_sum(gain_part))
            gather(4, column_sum(grad))
            gather(2, column_sum(value))

    tick(13)
    for index in range(width // TILE):
        active_in[:, pl.ds(width + index * TILE, TILE)] = contract_last(
            mix_rows[...], mixer[pl.ds(index * TILE, TILE)]
        )

    def attend_back(group, key_group, same, pair, count):
        cols = pl.ds(pair * PAIR, PAIR)
        key_cols = pl.ds(width + pair * PAIR, PAIR)
        value_cols = pl.ds(2 * width + pair * PAIR, PAIR)
        query = triple[group, cols]
        values = triple[key_group, value_cols]
        both, softs = scores_of(query, triple[key_group, key_cols], same)
        outer = low(active_in[group, pl.ds(width + pair * PAIR, PAIR)])
        grads = head_parts(
            contract_last(outer, jnp.concatenate([values * side for side in sides], axis=0))
        )
        lows, score_grads = [], []
        for soft, grad in zip(softs, grads):
            soft = soft / jnp.sum(soft, axis=-1, keepdims=True)
            lows.append(low(soft))
            score_grads.append(
                low(soft * (grad - jnp.sum(soft * grad, axis=-1, keepdims=True)))
            )
        score_grad = jnp.concatenate(score_grads, axis=1)
        left_lane = lax.broadcasted_iota(jnp.int32, (count, PAIR), 1) < HEAD_DIM

        def joined(stacked):
            top = stacked[TEXT_GROUP - count : TEXT_GROUP]
            bottom = stacked[2 * TEXT_GROUP - count :]
            return low(jnp.where(left_lane, top, bottom))

        triple[group, key_cols] = joined(contract_first(score_grad, query))
        triple[group, cols] = low(product(score_grad, both) * ROOT_SCALE)
        triple[group, value_cols] = joined(
            contract_first(jnp.concatenate(lows, axis=1), outer)
        )

    @pl.loop(0, rows // TEXT_GROUP)
    def _(index):
        tick(14 + index)
        group = span(index, TEXT_GROUP)
        for pair in range(pairs):
            attend_back(group, group, same_full, pair, TEXT_GROUP)

    tick(18)
    if tail_rows:
        for pair in range(pairs):
            attend_back(tail_group, tail_keys, same_tail, pair, tail_rows)

    @pl.loop(0, 3)
    def _(index):
        tick(19 + index)
        cols = span(index, TILE)
        active_in[:, cols] = contract_last(triple[...], joint[cols])

    @pl.loop(0, 2)
    def _(half):
        tick(22 + half)

        @pl.loop(0, 3)
        def _(inner):
            chunk = span(half * 3 + inner, CHUNK)
            grad = active_in[chunk, :width]
            value, gain_part = norm_back(wide(token_ref[chunk]), grad, gain)
            token_out[chunk] = value + output[chunk]
            gather(0, column_sum(gain_part))
            gather(1, column_sum(grad))

    for index in range(feed // width):
        vector_acc[5 + index : 6 + index] = column_sum(
            bias_rows[:, index * width : (index + 1) * width]
        )
    pl.loop(24, STEPS + TAIL + 1)(tick)


def text_kernel(tokens, vectors, image_low, pair_counts, log_scale, shards, others):
    rows, width = tokens.shape
    feed = shards[2].shape[1]
    any_spec = pl.BlockSpec(memory_space=pl.ANY)
    vmem_spec = pl.BlockSpec(memory_space=pltpu.VMEM)
    dma = pltpu.SemaphoreType.DMA
    low_type = jnp.bfloat16
    smem_spec = pl.BlockSpec(memory_space=pltpu.SMEM)
    slots = 2 * 2 * 2 * 4 * SLOT_ROWS
    return pl.pallas_call(
        text_body,
        out_shape=(
            jax.ShapeDtypeStruct((STEPS, 2, ROWS, width), low_type),
            jax.ShapeDtypeStruct((VECTOR_ROWS, width), jnp.float32),
            jax.ShapeDtypeStruct((rows, width), jnp.float32),
        ),
        in_specs=[vmem_spec] * 3 + [smem_spec] * 2 + [any_spec] * 10,
        out_specs=(any_spec, vmem_spec, vmem_spec),
        scratch_shapes=[
            pltpu.VMEM((2 * shard.shape[0], shard.shape[1]), low_type) for shard in shards
        ]
        + [
            pltpu.VMEM((rows, width), low_type),
            pltpu.VMEM((rows, width), low_type),
            pltpu.VMEM((rows, width), low_type),
            pltpu.VMEM((rows, feed), low_type),
            pltpu.VMEM((POOL_ROWS, width), low_type),
            pltpu.VMEM((POOL_ROWS, width), low_type),
            pltpu.VMEM((rows, width), low_type),
            pltpu.VMEM((rows, width), low_type),
            pltpu.VMEM((rows, feed), low_type),
            pltpu.VMEM((rows, 3 * width), low_type),
            pltpu.VMEM((rows, width), jnp.float32),
            pltpu.VMEM((rows, feed), jnp.float32),
            pltpu.VMEM((rows, width), jnp.float32),
            pltpu.VMEM((rows // CHUNK * 8, width), jnp.float32),
            pltpu.VMEM((8, feed), jnp.float32),
            pltpu.VMEM((2, 2, 2, 4, SLOT_ROWS, width), low_type),
            pltpu.VMEM((NEAR, 1, slots), jnp.float32),
            pltpu.VMEM((4, 1, slots), jnp.float32),
            dma((5, 2)),
            dma((2, 8)),
            dma((2, NEAR - 1)),
            dma((2, 3)),
            pltpu.VMEM((width, rows), low_type),
            pltpu.VMEM((rows, width), low_type),
            pltpu.VMEM((VECTOR_ROWS, width), jnp.float32),
            pltpu.VMEM((2, 2, ROWS, width), low_type),
            pltpu.VMEM((PART_RING, 2, ROWS, width), low_type),
            pltpu.VMEM((CORE_RING, 2, ROWS, width), low_type),
            pltpu.VMEM((RING, ROWS, width), low_type),
            pltpu.VMEM((RING, PART, width), low_type),
            pltpu.VMEM((RING, PART, width), low_type),
            pltpu.VMEM((RING, PART, width), low_type),
            pltpu.VMEM((TOTAL_RING, PART, width), low_type),
            pltpu.VMEM((VECTOR_ROWS, width), jnp.float32),
            pltpu.VMEM((VECTOR_ROWS, width), jnp.float32),
            pltpu.VMEM((VECTOR_ROWS, width), jnp.float32),
            pltpu.VMEM((3, VECTOR_ROWS, width), jnp.float32),
            pltpu.VMEM((3, VECTOR_ROWS, width), jnp.float32),
        ]
        + [dma((2, STEPS)) for _ in range(8)]
        + [
            dma((STEPS,)),
            dma((2, 6)),
        ],
        compiler_params=pltpu.CompilerParams(
            collective_id=1, has_side_effects=True, vmem_limit_bytes=62 * 1024 * 1024
        ),
    )(tokens, vectors, image_low, pair_counts, log_scale, *shards, *others)


def pack_rows(vectors):
    index = lax.broadcasted_iota(jnp.int32, (VECTOR_ROWS, vectors[0].shape[0]), 0)
    packed = jnp.zeros(index.shape, vectors[0].dtype)
    for row, vector in enumerate(vectors):
        packed = jnp.where(index == row, vector[None, :], packed)
    return packed


IMAGE_GROUP = 4
IMAGE_BLOCK = 12
IMAGE_ROWS = 104
IMAGE_KEYS = 128


def image_body(
    token_ref,
    vector_ref,
    shard_vector,
    joint_hbm,
    mixer_hbm,
    up_hbm,
    down_hbm,
    project_hbm,
    joint_shard,
    mixer_shard,
    up_shard,
    down_shard,
    project_shard,
    image_out,
    vector_out,
    joint_other,
    mixer_other,
    up_other,
    down_other,
    project_other,
    joint,
    mixer,
    up,
    down,
    project,
    normed,
    normed_two,
    triple,
    attended,
    residual,
    final,
    hidden,
    pooled,
    load_sem,
    x_sem,
    y_sem,
    z_sem,
    core_sem,
):
    dp = lax.axis_index("dp")
    x = lax.axis_index("fsdp")
    zb, y, core = (dp // 4) % 2, (dp // 2) % 2, dp % 2
    x_peer, y_peer, core_peer = (dp, 1 - x), (dp + 2 - 4 * y, x), (dp + 1 - 2 * core, x)
    z_peer = (dp + 4 - 8 * zb, x)
    loads = [
        pltpu.make_async_copy(source, target, load_sem.at[index])
        for index, (source, target) in enumerate(
            (
                (joint_hbm, joint),
                (mixer_hbm, mixer),
                (up_hbm, up),
                (down_hbm, down),
                (project_hbm, project),
            )
        )
    ]
    for load in loads:
        load.start()
    barrier = pltpu.get_barrier_semaphore()
    for peer in (x_peer, y_peer, z_peer, core_peer):
        pl.semaphore_signal(barrier, inc=1, device_id=peer, device_id_type=MESH)
    vector_out[x] = shard_vector[...]
    pl.semaphore_wait(barrier, 4)

    def send(source, target, sems, index, peer):
        return pltpu.make_async_remote_copy(
            src_ref=source,
            dst_ref=target,
            send_sem=sems.at[0, index],
            recv_sem=sems.at[1, index],
            device_id=peer,
            device_id_type=MESH,
        )

    shards = (joint_shard, mixer_shard, up_shard, down_shard, project_shard)
    others = (joint_other, mixer_other, up_other, down_other, project_other)
    x_sends, x_cross, y_sends, z_sends, core_sends, core_cross = [], [], [], [], [], []
    for index, (shard, other) in enumerate(zip(shards, others)):
        size = shard.shape[0] // 8

        def rows_of(piece):
            return pl.ds(pl.multiple_of(piece * size, size), size)

        own = rows_of(core * 4 + y * 2 + zb)
        beside_y = rows_of(core * 4 + (1 - y) * 2 + zb)
        beside_z = rows_of(core * 4 + y * 2 + 1 - zb)
        cross = rows_of(core * 4 + (1 - y) * 2 + 1 - zb)
        x_sends.append(send(shard.at[own], other.at[own], x_sem, index, x_peer))
        x_cross.append(send(shard.at[cross], other.at[cross], x_sem, 6 + index, x_peer))
        y_sends.append(send(other.at[own], other.at[own], y_sem, index, y_peer))
        z_sends.append(send(other.at[own], other.at[own], z_sem, index, z_peer))
        core_sends.append(
            [
                send(other.at[piece], other.at[piece], core_sem, 4 * index + place, core_peer)
                for place, piece in enumerate((own, beside_y, beside_z))
            ]
        )
        core_cross.append(
            send(other.at[cross], other.at[cross], core_sem, 4 * index + 3, core_peer)
        )
    vector_send = send(vector_out.at[x], vector_out.at[x], x_sem, 5, x_peer)
    vector_send.start()
    for index in (2, 3, 0, 1, 4):
        x_sends[index].start()
    for index in (2, 3, 0, 1, 4):
        x_cross[index].start()

    def pass_near(index):
        x_sends[index].wait()
        y_sends[index].start()
        z_sends[index].start()

    def pass_core(index):
        y_sends[index].wait()
        z_sends[index].wait()
        for copy in core_sends[index]:
            copy.start()

    def pass_cross(index):
        x_cross[index].wait()
        core_cross[index].start()

    blocks, rows, width = token_ref.shape
    feed = up.shape[1]
    gain, offset, mix_bias, feed_gain, feed_offset, down_bias, end_gain, end_offset = (
        wide(vector_ref[index : index + 1]) for index in range(8)
    )

    def span(index, size):
        return pl.ds(pl.multiple_of(index * size, 8), size)

    seqs = rows // IMAGE_LEN
    pool_row = lax.broadcasted_iota(jnp.int32, (seqs, rows), 0)
    pool_col = lax.broadcasted_iota(jnp.int32, (seqs, rows), 1) // IMAGE_LEN
    pool = low(jnp.where(pool_row == pool_col, 1.0, 0.0))
    group_rows = IMAGE_GROUP * IMAGE_LEN
    lane = lax.broadcasted_iota(jnp.int32, (1, PAIR), 1)
    sides = (
        low(jnp.where(lane < HEAD_DIM, 1.0, 0.0)),
        low(jnp.where(lane < HEAD_DIM, 0.0, 1.0)),
    )
    seam = lax.broadcasted_iota(jnp.int32, (8, PAIR), 0) < 4
    windows = []
    for row_start, key_start in (
        (0, 0),
        (group_rows - IMAGE_ROWS, group_rows - IMAGE_KEYS),
    ):
        row = lax.broadcasted_iota(jnp.int32, (IMAGE_ROWS, IMAGE_KEYS), 0) + row_start
        col = lax.broadcasted_iota(jnp.int32, (IMAGE_ROWS, IMAGE_KEYS), 1) + key_start
        same = jnp.where(row // IMAGE_LEN == col // IMAGE_LEN, 0.0, CUT)
        windows.append((row_start, key_start, same))
    counters = [jnp.broadcast_to(side, (IMAGE_KEYS, PAIR)) for side in sides]

    def attend(start, pair):
        cols = pair * PAIR
        parts = []
        for row_start, key_start, same in windows:
            query = triple[pl.ds(start + row_start, IMAGE_ROWS), pl.ds(cols, PAIR)]
            keys = triple[pl.ds(start + key_start, IMAGE_KEYS), pl.ds(width + cols, PAIR)]
            values = triple[pl.ds(start + key_start, IMAGE_KEYS), pl.ds(2 * width + cols, PAIR)]
            scores = contract_last(
                query, jnp.concatenate([keys * side for side in sides], axis=0)
            )
            softs = []
            for head in range(2):
                score = scores[:, head * IMAGE_KEYS : (head + 1) * IMAGE_KEYS] + same
                softs.append(low(jnp.exp(score - jnp.max(score, axis=-1, keepdims=True))))
            spread = jnp.concatenate(
                [
                    jnp.concatenate([values * side, counter], axis=1)
                    for side, counter in zip(sides, counters)
                ],
                axis=0,
            )
            mixed = product(jnp.concatenate(softs, axis=1), spread)
            parts.append(mixed[:, :PAIR] / mixed[:, PAIR:])
        first, second = parts
        edge = IMAGE_ROWS - 8
        attended[pl.ds(start, edge), pl.ds(cols, PAIR)] = low(first[:edge])
        attended[pl.ds(start + edge, 8), pl.ds(cols, PAIR)] = low(
            jnp.where(seam, first[edge:], second[:8])
        )
        attended[pl.ds(start + IMAGE_ROWS, edge), pl.ds(cols, PAIR)] = low(second[8:])

    pairs = width // PAIR
    groups = rows // group_rows

    def cols_of(index):
        return pl.ds(index * TILE, TILE)

    def first_norm(block):
        normed[...] = low(centred_scale(wide(token_ref[block]))[0] * gain + offset)

    def make_triple(index):
        cols = cols_of(index)
        values = product(normed[...], joint[:, cols])
        triple[:, cols] = low(values * ROOT_SCALE if index < 3 else values)

    def mix(block, index):
        cols = cols_of(index)
        residual[:, cols] = (
            wide(token_ref[block, :, cols])
            + product(attended[...], mixer[:, cols])
            + mix_bias[:, index * TILE : (index + 1) * TILE]
        )

    def second_norm():
        normed_two[...] = low(centred_scale(residual[...])[0] * feed_gain + feed_offset)

    def feed_up(index):
        cols = cols_of(index)
        row, start = 8 + index // 3, (index % 3) * TILE
        bias = wide(vector_ref[row : row + 1, start : start + TILE])
        hidden[:, cols] = low(gelu_value(product(normed_two[...], up[:, cols]) + bias))

    def feed_down(index):
        cols = cols_of(index)
        final[:, cols] = (
            residual[:, cols]
            + product(hidden[...], down[:, cols])
            + down_bias[:, index * TILE : (index + 1) * TILE]
        )

    def pool_rows(block):
        mean = product(pool, low(centred_scale(final[...])[0])) * (1.0 / IMAGE_LEN)
        pooled[block] = mean * end_gain + end_offset

    def attend_unit(unit):
        attend((unit // pairs) * group_rows, unit % pairs)

    units = groups * pairs

    first_norm(0)
    loads[0].wait()
    for index in range(9):
        make_triple(index)
    for unit in range(units):
        attend_unit(unit)
    loads[1].wait()
    loads[2].wait()
    loads[3].wait()
    pass_near(2)
    for index in range(3):
        mix(0, index)
    second_norm()
    for block in range(1, blocks):
        first_norm(block)
        for index in range(9):
            make_triple(index)
        if block == 1:
            pass_near(3)
        for unit in range(units):
            attend_unit(unit)
            if unit < 12:
                feed_up(unit)
            elif unit % 2 == 1:
                feed_down((unit - 12) // 2)
        if block == 1:
            pass_near(0)
            pass_near(1)
            pass_near(4)
            pass_core(2)
            pass_core(3)
        if block == 2:
            pass_core(0)
            pass_core(1)
            pass_core(4)
        for index in range(3):
            mix(block, index)
        pool_rows(block - 1)
        second_norm()

    for index in range(12):
        feed_up(index)
    for index in range(3):
        feed_down(index)
    for index in range(5):
        pass_cross(index)
    pool_rows(blocks - 1)
    loads[4].wait()
    rest = jnp.zeros((SLOT_ROWS - blocks * IMAGE_BLOCK, width), jnp.float32)
    means = jnp.concatenate([pooled[block] for block in range(blocks)] + [rest], axis=0)
    embedding = product(low(means), project[...])
    image_out[...] = low(
        embedding * lax.rsqrt(jnp.sum(embedding * embedding, axis=-1, keepdims=True) + EPSILON)
    )
    for copies, copy in zip(core_sends, core_cross):
        for near in copies:
            near.wait()
        copy.wait()
    vector_send.wait()


def image_kernel(tokens, weights, shard_vector, shards):
    (
        norm_gain,
        norm_offset,
        joint,
        mixer,
        mixer_bias,
        feed_gain,
        feed_offset,
        up,
        up_bias,
        down,
        down_bias,
        end_gain,
        end_offset,
        project,
    ) = weights
    total, width = tokens.shape
    rows = IMAGE_BLOCK * IMAGE_LEN
    blocks = total // rows
    feed = up.shape[1]
    vectors = pack_rows(
        [
            norm_gain,
            norm_offset,
            mixer_bias,
            feed_gain,
            feed_offset,
            down_bias,
            end_gain,
            end_offset,
        ]
        + [up_bias[start : start + width] for start in range(0, feed, width)],
    )
    any_spec = pl.BlockSpec(memory_space=pl.ANY)
    vmem_spec = pl.BlockSpec(memory_space=pltpu.VMEM)
    dma = pltpu.SemaphoreType.DMA
    low_type = jnp.bfloat16
    matrices = (joint, mixer, up, down, project)
    image_out, vector_out, *others = pl.pallas_call(
        image_body,
        out_shape=(
            jax.ShapeDtypeStruct((SLOT_ROWS, width), low_type),
            jax.ShapeDtypeStruct((2, *shard_vector.shape), low_type),
            *(
                jax.ShapeDtypeStruct(shard.shape, low_type)
                for shard in shards
            ),
        ),
        in_specs=[vmem_spec] * 3 + [any_spec] * 10,
        out_specs=(vmem_spec, vmem_spec, *([any_spec] * 5)),
        scratch_shapes=[pltpu.VMEM(matrix.shape, low_type) for matrix in matrices]
        + [
            pltpu.VMEM((rows, width), low_type),
            pltpu.VMEM((rows, width), low_type),
            pltpu.VMEM((rows, 3 * width), low_type),
            pltpu.VMEM((rows, width), low_type),
            pltpu.VMEM((rows, width), jnp.float32),
            pltpu.VMEM((rows, width), jnp.float32),
            pltpu.VMEM((rows, feed), low_type),
            pltpu.VMEM((blocks, IMAGE_BLOCK, width), jnp.float32),
            dma((5,)),
            dma((2, 11)),
            dma((2, 5)),
            dma((2, 5)),
            dma((2, 20)),
        ],
        compiler_params=pltpu.CompilerParams(
            collective_id=2, has_side_effects=True, vmem_limit_bytes=60 * 1024 * 1024
        ),
    )(
        tokens.reshape(blocks, rows, width),
        vectors,
        shard_vector,
        *matrices,
        *shards,
    )
    return image_out, vector_out, others


def finish_body(grad_hbm, packed_ref, *refs):
    (
        gain,
        offset,
        joint,
        mixer,
        mix_bias,
        feed_gain,
        feed_offset,
        up,
        up_bias,
        down,
        down_bias,
        end_gain,
        end_offset,
        project,
        scale_out,
        loss_out,
        low_values,
        wide_values,
        load_sem,
        store_sem,
    ) = refs
    shard = lax.axis_index("fsdp")
    loads = [
        pltpu.make_async_copy(
            grad_hbm.at[pl.ds(unit * SUB, SUB)],
            low_values.at[pl.ds(unit * SUB, SUB)],
            load_sem.at[unit],
        )
        for unit in range(UNITS)
    ]
    for load in loads:
        load.start()
    for row, target in (
        (0, gain),
        (1, offset),
        (2, mix_bias),
        (3, feed_gain),
        (4, feed_offset),
        (9, down_bias),
        (10, end_gain),
        (11, end_offset),
    ):
        cols = pl.ds(pl.multiple_of(shard * HALF, HALF), HALF)
        target[...] = packed_ref[pl.ds(row, 1), cols].reshape(HALF)
    for part in range(2):
        up_bias[pl.ds(part * WIDTH, WIDTH)] = packed_ref[
            pl.ds(5 + 2 * shard + part, 1), :
        ].reshape(WIDTH)
    loss_out[...] = packed_ref[12:13, 0:1]
    scale_out[...] = packed_ref[12:13, 1:2]
    places = (
        [(project, pl.ds(0, HALF), pl.ds(0, WIDTH))]
        + [(down, pl.ds(unit * HALF, HALF), pl.ds(0, WIDTH)) for unit in range(4)]
        + [(up, pl.ds(0, HALF), pl.ds(unit * WIDTH, WIDTH)) for unit in range(4)]
        + [(mixer, pl.ds(0, HALF), pl.ds(0, WIDTH))]
        + [(joint, pl.ds(0, HALF), pl.ds(unit * WIDTH, WIDTH)) for unit in range(3)]
    )
    stores = []
    for unit, (target, rows, cols) in enumerate(places):
        loads[unit].wait()
        for core in range(2):
            for half in range(SUB):
                rows_here = pl.ds(core * QUARTER + half * ROWS, ROWS)
                wide_values[unit, rows_here] = wide(low_values[unit * SUB + half, core])
        copy = pltpu.make_async_copy(wide_values.at[unit], target.at[rows, cols], store_sem.at[unit])
        copy.start()
        stores.append(copy)
    for copy in stores:
        copy.wait()


def finish_kernel(grads, packed):
    single = jnp.float32
    any_spec = pl.BlockSpec(memory_space=pl.ANY)
    vmem_spec = pl.BlockSpec(memory_space=pltpu.VMEM)
    vector = (jax.ShapeDtypeStruct((HALF,), single), vmem_spec)
    scalar = (jax.ShapeDtypeStruct((1, 1), single), vmem_spec)

    def matrix(rows, cols):
        return (jax.ShapeDtypeStruct((rows, cols), single), any_spec)

    outs = (
        vector,
        vector,
        matrix(HALF, 3 * WIDTH),
        matrix(HALF, WIDTH),
        vector,
        vector,
        vector,
        matrix(HALF, 4 * WIDTH),
        (jax.ShapeDtypeStruct((4 * HALF,), single), vmem_spec),
        matrix(4 * HALF, WIDTH),
        vector,
        vector,
        vector,
        matrix(HALF, WIDTH),
        scalar,
        scalar,
    )
    return pl.pallas_call(
        finish_body,
        out_shape=tuple(shape for shape, spec in outs),
        in_specs=[any_spec, vmem_spec],
        out_specs=tuple(spec for shape, spec in outs),
        scratch_shapes=[
            pltpu.VMEM((STEPS, 2, ROWS, WIDTH), jnp.bfloat16),
            pltpu.VMEM((UNITS, HALF, WIDTH), single),
            pltpu.SemaphoreType.DMA((UNITS,)),
            pltpu.SemaphoreType.DMA((UNITS,)),
        ],
        compiler_params=pltpu.CompilerParams(vmem_limit_bytes=48 * 1024 * 1024),
    )(grads, packed)


def reduce_plain(factors, vectors):
    terms = [contract_first(left, right) for left, right in factors]
    joint, mixer, upward, downward, project = terms
    gain, offset, mixbias, feedgain, feedoffset, upbias, downbias, endgain, endoffset = vectors
    ordered = (
        gain,
        offset,
        joint,
        mixer,
        mixbias,
        feedgain,
        feedoffset,
        upward,
        upbias,
        downward,
        downbias,
        endgain,
        endoffset,
        project,
    )
    shards = tuple(
        lax.psum_scatter(term, "fsdp", scatter_dimension=0, tiled=True) for term in ordered
    )
    return lax.psum(shards, "dp")


def on_device_plain(*arrays):
    (
        text_tokens,
        image_tokens,
        pair_counts,
        log_scale,
        text_gain,
        text_offset,
        text_joint,
        text_mixer,
        text_mixbias,
        text_feedgain,
        text_feedoffset,
        text_upward,
        text_upbias,
        text_downward,
        text_downbias,
        text_endgain,
        text_endoffset,
        text_project,
        image_gain,
        image_offset,
        image_joint,
        image_mixer,
        image_mixbias,
        image_feedgain,
        image_feedoffset,
        image_upward,
        image_upbias,
        image_downward,
        image_downbias,
        image_endgain,
        image_endoffset,
        image_project,
    ) = arrays
    image_weights = (
        image_gain,
        image_offset,
        image_joint,
        image_mixer,
        image_mixbias,
        image_feedgain,
        image_feedoffset,
        image_upward,
        image_upbias,
        image_downward,
        image_downbias,
        image_endgain,
        image_endoffset,
        image_project,
    )
    group_count = lax.axis_size("dp") * lax.axis_size("fsdp")
    device = lax.axis_index("dp") * lax.axis_size("fsdp") + lax.axis_index("fsdp")
    pair_total = group_count * SLOTS
    live_all = (
        (jnp.arange(SLOTS)[None, :] < pair_counts[:, None]).astype(jnp.float32).reshape(pair_total)
    )
    live_total = jnp.sum(live_all)
    text_live = lax.dynamic_slice_in_dim(live_all, device * SLOTS, SLOTS)
    temper = jnp.exp(log_scale[0])
    half_inverse = 1.0 / (2.0 * live_total)
    image_unit = forward_block(image_tokens, image_weights, IMAGE_LEN)[0]
    image_low = image_unit.astype(jnp.bfloat16)
    shard_piece = lax.all_gather(image_low, ("dp", "fsdp"), axis=0, tiled=True)
    text_weights = tuple(
        lax.all_gather(shard, "fsdp", axis=0, tiled=True)
        for shard in (
            text_gain,
            text_offset,
            text_joint,
            text_mixer,
            text_mixbias,
            text_feedgain,
            text_feedoffset,
            text_upward,
            text_upbias,
            text_downward,
            text_downbias,
            text_endgain,
            text_endoffset,
            text_project,
        )
    )
    text_unit, kept_values = forward_block(text_tokens, text_weights, TEXT_LEN)
    text_low = text_unit.astype(jnp.bfloat16)
    cosine = contract_last(text_low, shard_piece)
    scaled = jnp.exp(temper * cosine - temper)
    image_live = live_all
    forward_row_sum = jnp.sum(scaled * image_live[None, :], axis=1)
    forward_column_sum = jnp.sum(scaled * text_live[:, None], axis=0)
    column_sum = forward_column_sum
    column_sum = lax.psum(column_sum, ("dp", "fsdp"))
    diagonal_cos = jnp.sum(text_low.astype(jnp.float32) * image_low.astype(jnp.float32), axis=1)
    row_log = temper + jnp.log(forward_row_sum)
    column_log = temper + jnp.log(lax.dynamic_slice_in_dim(column_sum, device * SLOTS, SLOTS))
    diagonal = temper * diagonal_cos
    loss_part = jnp.sum(text_live * (row_log - diagonal) + text_live * (column_log - diagonal)) / (
        2.0 * live_total
    )
    coupling = (
        scaled * (text_live / forward_row_sum)[:, None] * image_live[None, :]
        + scaled * text_live[:, None] * (image_live / column_sum)[None, :]
    ) * half_inverse
    temper_grad = jnp.sum(coupling * cosine)
    unit_grad = product((temper * coupling).astype(jnp.bfloat16), shard_piece)
    unit_grad, temper_grad = (unit_grad, temper_grad)
    unit_grad = unit_grad - temper / live_total * text_live[:, None] * image_low.astype(jnp.float32)
    temper_grad = temper_grad - jnp.sum(text_live * diagonal_cos) / live_total
    loss_total, scale_total = lax.psum((loss_part, temper * temper_grad), ("dp", "fsdp"))
    factors, vectors, token_grad = backward_block(
        kept_values, text_weights, unit_grad, TEXT_LEN
    )
    final_grads = reduce_plain(factors, vectors)
    return (
        *final_grads,
        jnp.reshape(scale_total, (1,)),
        token_grad,
        jnp.reshape(loss_total, (1,)),
    )


def on_device(*arrays):
    if (lax.axis_size("dp"), lax.axis_size("fsdp")) != (16, 2):
        return on_device_plain(*arrays)
    text_tokens, image_tokens, pair_counts, log_scale = arrays[:4]
    text_weights, image_weights = arrays[4:18], arrays[18:32]
    matrix_places = (2, 3, 7, 9, 13)
    vector_places = (0, 1, 4, 5, 6, 10, 11, 12)
    shard_vector = pack_rows(
        [text_weights[place] for place in vector_places]
        + [text_weights[8][start : start + HALF] for start in range(0, 4 * HALF, HALF)]
    )
    shards = tuple(text_weights[place] for place in matrix_places)
    image_low, vectors, others = image_kernel(image_tokens, image_weights, shard_vector, shards)
    grads, packed, token_grad = text_kernel(
        text_tokens, vectors, image_low, pair_counts, log_scale, shards, others
    )
    *final_grads, scale_total, loss_total = finish_kernel(grads, packed)
    return (*final_grads, scale_total.reshape(1), token_grad, loss_total.reshape(1))


def solution(mesh):
    return jax.shard_map(
        on_device,
        mesh=mesh,
        in_specs=(
            P(("dp", "fsdp"), None),
            P(("dp", "fsdp"), None),
            P(),
            P(),
            P("fsdp"),
            P("fsdp"),
            P("fsdp", None),
            P("fsdp", None),
            P("fsdp"),
            P("fsdp"),
            P("fsdp"),
            P("fsdp", None),
            P("fsdp"),
            P("fsdp", None),
            P("fsdp"),
            P("fsdp"),
            P("fsdp"),
            P("fsdp", None),
            P(),
            P(),
            P(),
            P(),
            P(),
            P(),
            P(),
            P(),
            P(),
            P(),
            P(),
            P(),
            P(),
            P(),
        ),
        out_specs=(
            P("fsdp"),
            P("fsdp"),
            P("fsdp", None),
            P("fsdp", None),
            P("fsdp"),
            P("fsdp"),
            P("fsdp"),
            P("fsdp", None),
            P("fsdp"),
            P("fsdp", None),
            P("fsdp"),
            P("fsdp"),
            P("fsdp"),
            P("fsdp", None),
            P(),
            P(("dp", "fsdp"), None),
            P(),
        ),
        check_vma=False,
    )
```
